32 devices in a mesh: seq: 8 (over z, y), wt: 4 (over x, core).
Axes of the slice: x: 2, y: 2, z: 4, core: 2. Of those that a mesh axis runs over, the one named last changes fastest.
Arguments:
- inputs: bfloat16 [51200, 512], P(('seq', 'wt')), may hold values from -6 to 6
- key_mask: int32 [256, 200], P(('seq', 'wt')), may hold values from 0 to 1, as said below
- routes: int32 [51200, 2], P(('seq', 'wt')), may hold values from 0 to 7, as said below
- priority: int32 [32, 1600], P(('seq', 'wt')), may hold values from 0 to 1599, each once within a row
- capacity: int32 [8], replicated, may hold values from 200 to 400, as said below
- attention_gain: bfloat16 [512], P('wt'), may hold values from 0.5 to 1.5
- attention_shift: bfloat16 [512], P('wt'), may hold values from -2.5 to 2.5
- query_key_value: bfloat16 [512, 1536], P('wt'), may hold values from -0.25 to 0.25
- attention_out: bfloat16 [512, 512], P('wt'), may hold values from -1.5 to 1.5
- mixture_gain: bfloat16 [512], P('wt'), may hold values from 0.5 to 1.5
- mixture_shift: bfloat16 [512], P('wt'), may hold values from -2.5 to 2.5
- router_weight: bfloat16 [512, 8], P('wt'), may hold values from -0.5 to 0.5
- expert_in: bfloat16 [8, 2048, 512], P('seq', 'wt'), may hold values from -0.25 to 0.25
- expert_in_bias: bfloat16 [8, 2048], P('seq', 'wt'), may hold values from -3 to 3
- expert_out: bfloat16 [8, 2048, 512], P('seq', 'wt'), may hold values from -0.1875 to 0.1875
- expert_out_bias: bfloat16 [8, 512], P('seq', 'wt'), may hold values from -3 to 3
- cotangent: bfloat16 [51200, 512], P(('seq', 'wt')), may hold values from -6 to 6
Outputs:
- block_output: bfloat16 [51200, 512], P(('seq', 'wt'))
- input_grad: float32 [51200, 512], P(('seq', 'wt'))
- attention_gain_grad: float32 [512], P('wt')
- attention_shift_grad: float32 [512], P('wt')
- query_key_value_grad: float32 [512, 1536], P('wt')
- attention_out_grad: float32 [512, 512], P('wt')
- mixture_gain_grad: float32 [512], P('wt')
- mixture_shift_grad: float32 [512], P('wt')
- router_weight_grad: float32 [512, 8], P('wt')
- expert_in_grad: float32 [8, 2048, 512], P('seq', 'wt')
- expert_in_bias_grad: float32 [8, 2048], P('seq', 'wt')
- expert_out_grad: float32 [8, 2048, 512], P('seq', 'wt')
- expert_out_bias_grad: float32 [8, 512], P('seq', 'wt')
The draws below stay inside these ranges and needn't reach their ends.
Inputs may be any that keep to these rules, and one draw needn't show every extreme that they name: `routes`: the two experts of a token differ. In every aligned block of 1600 rows (the tokens of one device) some expert is the first route of 400 or more tokens. `capacity`: some expert has 400 slots. `priority`: each row names each of the 1600 local rows of its block once. `key_mask`: position 0 of every image is 1; positions 197 and beyond are 0.
All inputs are finite; a program needn't handle non-finite values.
Results may differ from the reference program's by a relative error of at most 0.019.
Values may be sent and summed in bfloat16 or wider, within the bound.
No kernel may reach another device: no remote copies, remote signals or barrier semaphores. Data moves between devices by JAX's collectives and lax.ppermute only.
A program may use at most 128 MiB of HBM per device.

```python
import jax
import jax.numpy as jnp
from jax import lax

D = 512
HEADS = 8
HEAD_DIM = 64
FF = 2048
L = 200
VALID = 197
IMG_DEV = 8
EXPERTS = 8
TOK_DEV = 1600
IMAGES = 256
TOKENS = 51200
CAP = 400
N_SEQ = 8
N_WT = 4


def expert_ranking(key):
    return jax.random.permutation(jax.random.fold_in(key, 101), EXPERTS).astype(jnp.int32)


def draw_capacity(key, part):
    ranking = expert_ranking(key)
    lowered = jax.random.randint(jax.random.fold_in(key, 202), (EXPERTS,), CAP // 2, CAP + 1, dtype=jnp.int32)
    return jnp.where(jnp.arange(EXPERTS, dtype=jnp.int32) == ranking[0], CAP, lowered).astype(jnp.int32)


def draw_routes(key, part):
    ranking = expert_ranking(key)
    block_total = TOKENS // TOK_DEV
    first_left = jax.random.randint(jax.random.fold_in(key, 303), (TOKENS,), 0, EXPERTS, dtype=jnp.int32)
    first_right = jax.random.randint(jax.random.fold_in(key, 304), (TOKENS,), 0, EXPERTS, dtype=jnp.int32)
    first_rank = first_left * first_right // EXPERTS
    raw_keys = jax.random.randint(jax.random.fold_in(key, 305), (block_total, TOK_DEV), 0, 2 ** 19, dtype=jnp.int32)
    distinct = raw_keys * TOK_DEV + jnp.arange(TOK_DEV, dtype=jnp.int32)[None, :]
    order_rank = jnp.argsort(jnp.argsort(distinct, axis=1), axis=1)
    forced = (order_rank < min(TOK_DEV, CAP + CAP // 2)).reshape(TOKENS)
    first_rank = jnp.where(forced, 0, first_rank)
    step_left = jax.random.randint(jax.random.fold_in(key, 306), (TOKENS,), 0, EXPERTS - 1, dtype=jnp.int32)
    step_right = jax.random.randint(jax.random.fold_in(key, 307), (TOKENS,), 0, EXPERTS - 1, dtype=jnp.int32)
    second_rank = (first_rank + 1 + step_left * step_right // EXPERTS) % EXPERTS
    return jnp.stack([jnp.take(ranking, first_rank), jnp.take(ranking, second_rank)], axis=1).astype(jnp.int32)


def draw_key_mask(key, part):
    dropped = jax.random.randint(jax.random.fold_in(key, 404), (IMAGES, L), 0, 16, dtype=jnp.int32)
    position = jnp.arange(L, dtype=jnp.int32)[None, :]
    return jnp.where(position == 0, 1, jnp.where((position < VALID) & (dropped > 0), 1, 0)).astype(jnp.int32)


def steps_of(rng, extent, split, smallest, high):
    def one(dim, shards_of):
        heights = jax.random.uniform(jax.random.fold_in(jax.random.fold_in(rng, 6), dim), (shards_of,), jnp.float32, smallest / len(split), high / len(split))
        return jnp.repeat(jnp.exp(heights), extent[dim] // shards_of).reshape((-1,) + (1,) * (len(extent) - dim - 1))

    loudness = one(*split[0])
    for cut in split[1:]:
        loudness = loudness * one(*cut)
    return loudness


def normal_values(key, shape, deviation, bound, cuts=(), kind=jnp.bfloat16):
    entries = deviation * jax.random.normal(key, shape, jnp.float32)
    if cuts:
        entries = entries * steps_of(key, shape, cuts, -0.22, 0.18)
    return jnp.clip(entries, -bound, bound).astype(kind)


def setup_inputs(seed: int = 0) -> dict:
    seeds = jax.random.split(jax.random.key(seed), 18)
    return {
        "inputs": normal_values(seeds[0], (TOKENS, D), 1.0, 6.0, ((0, 32),)),
        "key_mask": draw_key_mask(jax.random.fold_in(seeds[17], 71), 0),
        "routes": draw_routes(jax.random.fold_in(seeds[17], 71), 0),
        "priority": jax.vmap(lambda own: jax.random.permutation(own, TOK_DEV))(jax.random.split(seeds[3], (N_SEQ * N_WT))).reshape((N_SEQ * N_WT, TOK_DEV)).astype(jnp.int32),
        "capacity": draw_capacity(jax.random.fold_in(seeds[17], 71), 0),
        "attention_gain": jnp.clip(1.0 + 0.1 * jax.random.normal(seeds[5], (D,), jnp.float32), 0.5, 1.5).astype(jnp.bfloat16),
        "attention_shift": normal_values(seeds[6], (D,), 0.3, 2.5, ((0, 4),)),
        "query_key_value": normal_values(seeds[7], (D, 3 * D), D ** -0.5, 0.25, ((0, 4),)),
        "attention_out": normal_values(seeds[8], (D, D), (D // 32) ** -0.5, 1.5, ((0, 4),)),
        "mixture_gain": jnp.clip(1.0 + 0.1 * jax.random.normal(seeds[9], (D,), jnp.float32), 0.5, 1.5).astype(jnp.bfloat16),
        "mixture_shift": normal_values(seeds[10], (D,), 0.3, 2.5, ((0, 4),)),
        "router_weight": normal_values(seeds[11], (D, EXPERTS), (D // 4) ** -0.5, 0.5, ((0, 4),)),
        "expert_in": normal_values(seeds[12], (EXPERTS, FF, D), D ** -0.5, 0.25, ((0, 8), (1, 4))),
        "expert_in_bias": normal_values(seeds[13], (EXPERTS, FF), 0.5, 3.0, ((0, 8), (1, 4))),
        "expert_out": normal_values(seeds[14], (EXPERTS, FF, D), (FF // 2) ** -0.5, 0.1875, ((0, 8), (1, 4))),
        "expert_out_bias": normal_values(seeds[15], (EXPERTS, D), 0.5, 3.0, ((0, 8), (1, 4))),
        "cotangent": normal_values(seeds[16], (TOKENS, D), 1.0, 6.0, ((0, 32),)),
    }


@jax.custom_vjp
def low(v):
    return lax.optimization_barrier(v.astype(jnp.bfloat16)).astype(jnp.float32)

@jax.custom_vjp
def low_back(v):
    return v

def low_keep(v):
    return (low(v), None)

def low_pass(kept, grad):
    return (grad,)

def back_keep(v):
    return (v, None)

def back_low(kept, grad):
    return (low(grad),)
low.defvjp(low_keep, low_pass)
low_back.defvjp(back_keep, back_low)
HIGHEST = lax.Precision.HIGHEST
NEGATIVE = -1e+30
EPSILON = 1e-06

def layer_norm(values, norm_gain, norm_shift):
    row_mean = lax.optimization_barrier(jnp.mean(values, axis=-1, keepdims=True))
    offsets = values - row_mean
    spread = lax.optimization_barrier(jnp.mean(offsets * offsets, axis=-1, keepdims=True))
    return offsets * lax.rsqrt(spread + EPSILON) * norm_gain + norm_shift

def slot_tables(route_rows, order_rows, capacity, expert_count, slot_count):
    pair_tokens = route_rows.shape[0]
    ordered = jnp.take(route_rows, order_rows, axis=0).astype(jnp.int32)
    labels = jnp.arange(expert_count, dtype=jnp.int32)[None, :]
    first_hot = (ordered[:, 0:1] == labels).astype(jnp.int32)
    second_hot = (ordered[:, 1:2] == labels).astype(jnp.int32)
    first_seen = jnp.cumsum(first_hot, axis=0, dtype=jnp.int32) - first_hot
    second_seen = jnp.cumsum(second_hot, axis=0, dtype=jnp.int32) - second_hot + lax.optimization_barrier(jnp.sum(first_hot, axis=0, keepdims=True, dtype=jnp.int32))
    places = jnp.stack([lax.optimization_barrier(jnp.sum(first_seen * first_hot, axis=1, dtype=jnp.int32)), lax.optimization_barrier(jnp.sum(second_seen * second_hot, axis=1, dtype=jnp.int32))], axis=1)
    limits = jnp.stack([lax.optimization_barrier(jnp.sum(first_hot * capacity[None, :], axis=1, dtype=jnp.int32)), lax.optimization_barrier(jnp.sum(second_hot * capacity[None, :], axis=1, dtype=jnp.int32))], axis=1)
    sorted_kept = (places < limits).astype(jnp.int32)
    sorted_slot = (places * expert_count + ordered).astype(jnp.int32)
    kept_flags = jnp.zeros((pair_tokens, 2), jnp.int32).at[order_rows].set(sorted_kept)
    slot_index = jnp.zeros((pair_tokens, 2), jnp.int32).at[order_rows].set(sorted_slot * sorted_kept)
    pair_ids = (jnp.arange(2, dtype=jnp.int32)[None, :] * pair_tokens + order_rows[:, None]).astype(jnp.int32)
    target = jnp.where(sorted_kept > 0, sorted_slot, slot_count * expert_count).astype(jnp.int32)
    slot_table = jnp.full((slot_count * expert_count,), 2 * pair_tokens, jnp.int32).at[target.reshape(-1)].set(pair_ids.reshape(-1), mode='drop')
    return (kept_flags, slot_index, slot_table)

def block_forward(block_rows, mask_rows, route_rows, order_rows, capacity, parameters):
    first_gain, first_shift, triple_weight, output_weight, second_gain, second_shift, router_full, weight_in, bias_in, weight_out, bias_out = parameters
    normed_first = low(layer_norm(block_rows, first_gain, first_shift))
    triple = low(low_back(jnp.dot(normed_first, triple_weight, precision=HIGHEST)))
    shaped = triple.reshape(IMG_DEV, L, 3, HEADS, HEAD_DIM)
    queries = shaped[:, :, 0]
    keys_part = shaped[:, :, 1]
    values_part = shaped[:, :, 2]
    raw_scores = jnp.einsum('iqhd,ikhd->ihqk', queries, keys_part, precision=HIGHEST) * HEAD_DIM ** (-0.5)
    scores = jnp.where(mask_rows[:, None, None, :] > 0, low_back(raw_scores), NEGATIVE)
    softmax_low = low(jax.nn.softmax(scores, axis=-1))
    mixed = jnp.einsum('ihqk,ikhd->iqhd', softmax_low, values_part, precision=HIGHEST)
    context = low(low_back(mixed.reshape(TOK_DEV, D)))
    residual = block_rows + low_back(jnp.dot(context, output_weight, precision=HIGHEST))
    normed_second = low(layer_norm(residual, second_gain, second_shift))
    logits = low_back(jnp.dot(normed_second, router_full, precision=HIGHEST))
    gate_values = jax.nn.softmax(jnp.take_along_axis(logits, route_rows, axis=1), axis=1)
    kept_flags, slot_index, slot_table = slot_tables(route_rows, order_rows, capacity, EXPERTS, CAP)
    kept_float = kept_flags.astype(jnp.float32)
    padded_rows = jnp.concatenate([normed_second, jnp.zeros((1, D), jnp.float32)], axis=0)
    row_of_slot = jnp.where(slot_table < 2 * TOK_DEV, slot_table % TOK_DEV, TOK_DEV).astype(jnp.int32)
    dispatched = low_back(jnp.take(padded_rows, row_of_slot, axis=0)).reshape(CAP, EXPERTS, D)
    before = low_back(jnp.einsum('ced,efd->cef', dispatched, weight_in, precision=HIGHEST) + bias_in[None])
    hidden = low(jax.nn.gelu(before, approximate=True))
    produced = low(low_back(jnp.einsum('cef,efd->ced', hidden, weight_out, precision=HIGHEST) + bias_out[None]))
    produced_flat = produced.reshape(CAP * EXPERTS, D)
    weight_first = kept_float[:, 0] * gate_values[:, 0]
    weight_second = kept_float[:, 1] * gate_values[:, 1]
    mixture = weight_first[:, None] * jnp.take(produced_flat, slot_index[:, 0], axis=0) + weight_second[:, None] * jnp.take(produced_flat, slot_index[:, 1], axis=0)
    return residual + mixture

def reference(inputs, key_mask, routes, priority, capacity, attention_gain, attention_shift, query_key_value, attention_out, mixture_gain, mixture_shift, router_weight, expert_in, expert_in_bias, expert_out, expert_out_bias, cotangent):
    parameters = tuple((weight.astype(jnp.float32) for weight in (attention_gain, attention_shift, query_key_value, attention_out, mixture_gain, mixture_shift, router_weight, expert_in, expert_in_bias, expert_out, expert_out_bias)))
    block_total = TOKENS // TOK_DEV
    pieces = (key_mask.reshape(block_total, IMG_DEV, L), routes.reshape(block_total, TOK_DEV, 2), priority)

    def forward(inputs_wide, weights_wide):

        def block_step(carried, items):
            block_rows, mask_rows, route_rows, order_rows = items
            return (carried, block_forward(block_rows, mask_rows, route_rows, order_rows, capacity, weights_wide))
        _, outputs = lax.scan(jax.checkpoint(block_step), jnp.zeros((), jnp.float32), (inputs_wide.reshape(block_total, TOK_DEV, D),) + pieces)
        return outputs.reshape(TOKENS, D)
    result, pullback = jax.vjp(forward, inputs.astype(jnp.float32), parameters)
    input_grad, grads = pullback(cotangent.astype(jnp.float32))
    return (result.astype(jnp.bfloat16), input_grad, grads[0], grads[1], grads[2], grads[3], grads[4], grads[5], grads[6], grads[7], grads[8], grads[9], grads[10])
```

```python
from functools import partial

import jax
import jax.numpy as jnp
from jax import lax
from jax.experimental import pallas as pl
from jax.experimental.pallas import tpu as pltpu
from jax.sharding import PartitionSpec as P

HEADS = 8
NEGATIVE = -1e30
EPSILON = 1e-06
LANES = 128
CHUNK = 256
VMEM_BYTES = 60 * 1024 * 1024
F32 = jnp.float32
BF16 = jnp.bfloat16
ROOT = 0.7978845608028654
CUBIC = 0.044715

NT = (((1,), (1,)), ((), ()))
TN = (((0,), (0,)), ((), ()))


def mm(a, b):
    return jnp.dot(a, b, preferred_element_type=F32)


def mm_nt(a, b):
    return lax.dot_general(a, b, NT, preferred_element_type=F32)


def mm_tn(a, b):
    return lax.dot_general(a, b, TN, preferred_element_type=F32)


def params(steps=0):
    return pltpu.CompilerParams(
        dimension_semantics=("arbitrary",) * steps if steps else None,
        vmem_limit_bytes=VMEM_BYTES,
    )


def whole(shape):
    zeros = (0,) * len(shape)
    return pl.BlockSpec(shape, lambda *_: zeros, pipeline_mode=pl.Buffered(1))


def lane_iota(rows, width):
    return lax.broadcasted_iota(jnp.int32, (rows, width), 1)


def norm_stats(values):
    row_mean = jnp.mean(values, axis=-1, keepdims=True)
    offsets = values - row_mean
    spread = jnp.mean(offsets * offsets, axis=-1, keepdims=True)
    scale = lax.rsqrt(spread + EPSILON)
    return offsets * scale, scale


def norm_back(grad, unit, scale, gain):
    weighted = grad * gain
    first = jnp.mean(weighted, axis=-1, keepdims=True)
    second = jnp.mean(weighted * unit, axis=-1, keepdims=True)
    return scale * (weighted - first - unit * second)


def slots_kernel(cap, block, prow, pcol, routes, limits, out, posrow):
    total = routes.shape[0]
    steps = total // block
    lane_t = lane_iota(1, total)

    def row_step(i, acc):
        rows = pl.ds(pl.multiple_of(i * block, block), block)
        rank = (lax.broadcasted_iota(jnp.int32, (block, 1), 0) + i * block).astype(F32)
        hit = pcol[rows, :] == lane_t
        return acc + jnp.sum(jnp.where(hit, rank, 0.0), axis=0, keepdims=True)

    posrow[...] = lax.fori_loop(0, steps, row_step, jnp.zeros((1, total), F32))
    lane = lane_iota(1, LANES)
    half = LANES // 2
    first_all = routes[:, 0:1]
    second_all = routes[:, 1:2]
    hot_all = jnp.where((first_all == lane) | (second_all + half == lane), 1.0, 0.0).astype(BF16)
    seen_first = jnp.sum(
        jnp.where(first_all + half == lane, 1.0, 0.0), axis=0, keepdims=True
    )
    rank_row = lane_t.astype(F32)

    def step(i, carry):
        rows = pl.ds(pl.multiple_of(i * block, block), block)
        token = lax.broadcasted_iota(jnp.int32, (block, 1), 0) + i * block
        poscol = jnp.sum(jnp.where(prow[...] == token, rank_row, 0.0), axis=1, keepdims=True)
        earlier = jnp.where(posrow[...] < poscol, 1.0, 0.0).astype(BF16)
        counts = mm(earlier, hot_all)
        first = routes[rows, 0:1]
        second = routes[rows, 1:2]
        first_hot = jnp.where(first == lane, 1.0, 0.0)
        second_hot = jnp.where(second + half == lane, 1.0, 0.0)
        place_a = jnp.sum(counts * first_hot, axis=1, keepdims=True)
        place_b = jnp.sum((counts + seen_first) * second_hot, axis=1, keepdims=True)
        limit_a = jnp.sum(limits[...] * first_hot, axis=1, keepdims=True)
        limit_b = jnp.sum(limits[...] * second_hot, axis=1, keepdims=True)
        slot_a = jnp.where(place_a < limit_a, first * cap + place_a.astype(jnp.int32), -1)
        slot_b = jnp.where(place_b < limit_b, second * cap + place_b.astype(jnp.int32), -1)
        out[rows, :] = jnp.where(lane_iota(block, 2) == 0, slot_a, slot_b)
        return carry

    lax.fori_loop(0, steps, step, 0)


def make_slots(routes, priority, capacity, cap):
    total = routes.shape[0]
    experts = capacity.shape[0]
    half = LANES // 2
    padded = jnp.pad(capacity.astype(F32), (0, half - experts))
    limits = jnp.concatenate([padded, padded])[None, :]
    return pl.pallas_call(
        partial(slots_kernel, cap, 200),
        out_shape=jax.ShapeDtypeStruct((total, 2), jnp.int32),
        scratch_shapes=[pltpu.VMEM((1, total), F32)],
        compiler_params=params(),
        name="slots",
    )(priority, priority.reshape(total, 1), routes, limits)


def dispatch_kernel(cap, with_other, slot_rows, route_rows, rows, out, *other):
    base = pl.program_id(0) * cap
    place = lax.broadcasted_iota(jnp.int32, (cap, 1), 0) + base
    hit_a = slot_rows[0:1, :] == place
    hit_b = slot_rows[1:2, :] == place
    pick = jnp.where(hit_a | hit_b, 1.0, 0.0).astype(BF16)
    out[...] = mm(pick, rows[...]).astype(BF16)
    if with_other:
        named = route_rows[...] + 1.0
        found = jnp.where(hit_a, named[1:2, :], jnp.where(hit_b, named[0:1, :], 0.0))
        other[0][...] = jnp.sum(found, axis=1, keepdims=True) - 1.0


def dispatch(slot_rows, route_rows, rows, experts, cap, with_other):
    total, width = rows.shape
    out_shape = [jax.ShapeDtypeStruct((experts * cap, width), BF16)]
    out_specs = [pl.BlockSpec((cap, width), lambda e: (e, 0))]
    if with_other:
        out_shape.append(jax.ShapeDtypeStruct((experts * cap, 1), F32))
        out_specs.append(pl.BlockSpec((cap, 1), lambda e: (e, 0)))
    return pl.pallas_call(
        partial(dispatch_kernel, cap, with_other),
        grid=(experts,),
        in_specs=[whole((2, total)), whole((2, total)), whole((total, width))],
        out_specs=out_specs,
        out_shape=out_shape,
        compiler_params=params(1),
        name="dispatch",
        cost_estimate=pl.CostEstimate(
            flops=2 * experts * cap * total * width, bytes_accessed=6000000, transcendentals=0
        ),
    )(slot_rows, route_rows, rows)


def attention_kernel(x, mask, gains, wqkv, wout, triple, context, logs, residual, normed):
    width = x.shape[1]
    length = x.shape[0]
    x_wide = x[...].astype(F32)
    unit, _ = norm_stats(x_wide)
    low = (unit * gains[0:1, :] + gains[1:2, :]).astype(BF16)
    mixed = mm(low, wqkv[...]).astype(BF16)
    triple[...] = mixed
    bias = jnp.where(mask[0] > 0, 0.0, NEGATIVE)
    lane = lane_iota(1, LANES)
    head_width = width // HEADS
    scale = head_width ** (-0.5)
    per = LANES // head_width
    gathered = jnp.zeros((length, LANES), F32)
    lanes_all = lane_iota(length, LANES)
    for group in range(HEADS // per):
        begin = group * LANES
        queries = mixed[:, begin : begin + LANES]
        keys = mixed[:, width + begin : width + begin + LANES]
        values = mixed[:, 2 * width + begin : 2 * width + begin + LANES]
        merged = jnp.zeros((length, LANES), F32)
        for inner in range(per):
            inside = (lane >= inner * head_width) & (lane < (inner + 1) * head_width)
            chosen = queries * jnp.where(inside, scale, 0.0).astype(BF16)
            scores = mm_nt(chosen, keys) + bias
            peak = jnp.max(scores, axis=-1, keepdims=True)
            raised = jnp.exp(scores - peak)
            sums = jnp.sum(raised, axis=-1, keepdims=True)
            found = mm(raised.astype(BF16), values) * (1.0 / sums)
            merged = jnp.where(inside, found, merged)
            gathered = jnp.where(
                lanes_all == group * per + inner, peak + jnp.log(sums), gathered
            )
        context[:, begin : begin + LANES] = merged.astype(BF16)
    logs[0] = jnp.transpose(gathered)[:HEADS, :]
    after = x_wide + mm(context[...], wout[...])
    residual[...] = after
    unit_b, _ = norm_stats(after)
    normed[...] = (unit_b * gains[2:3, :] + gains[3:4, :]).astype(BF16)


def attention_forward(x, mask, gains, dense):
    total, width = x.shape
    images, length = mask.shape
    rows = lambda i: (i, 0)
    return pl.pallas_call(
        attention_kernel,
        grid=(images,),
        in_specs=[
            pl.BlockSpec((length, width), rows),
            pl.BlockSpec((1, 1, length), lambda i: (i, 0, 0)),
            whole(gains.shape),
            pl.BlockSpec((width, 3 * width), lambda i: (0, 0), pipeline_mode=pl.Buffered(1)),
            pl.BlockSpec((width, width), lambda i: (0, 3), pipeline_mode=pl.Buffered(1)),
        ],
        out_specs=[
            pl.BlockSpec((length, 3 * width), rows),
            pl.BlockSpec((length, width), rows),
            pl.BlockSpec((1, HEADS, length), lambda i: (i, 0, 0)),
            pl.BlockSpec((length, width), rows),
            pl.BlockSpec((length, width), rows),
        ],
        out_shape=[
            jax.ShapeDtypeStruct((total, 3 * width), BF16),
            jax.ShapeDtypeStruct((total, width), BF16),
            jax.ShapeDtypeStruct((images, HEADS, length), F32),
            jax.ShapeDtypeStruct((total, width), F32),
            jax.ShapeDtypeStruct((total, width), BF16),
        ],
        compiler_params=params(1),
        name="attention_forward",
    )(x, mask.reshape(images, 1, length), gains, dense, dense)


def experts_kernel(
    block, rows, ups, other, own, router, w_in, w_out, b_in, b_out,
    sent, back, dw_in, dw_out, db_in, db_out, drouter,
    gate, weighted, rows_t, weighted_t, made, pushed, hid, pre_g,
):
    f = pl.program_id(0)
    last = pl.num_programs(0) - 1
    total, width = rows.shape
    steps = total // block
    lane = lane_iota(1, LANES)
    tile = 512

    def spans():
        return [(s, min(tile, total - s)) for s in range(0, total, tile)]

    @pl.when(f == 0)
    def _():
        own_hot = own[...] > 0.0

        def step(i, acc):
            at = pl.ds(pl.multiple_of(i * block, block), block)
            logits = mm(rows[at, :], router[...])
            mine = jnp.sum(jnp.where(own_hot, logits, 0.0), axis=1, keepdims=True)
            rival = other[at, :].astype(jnp.int32)
            theirs = jnp.sum(jnp.where(lane == rival, logits, 0.0), axis=1, keepdims=True)
            share = 1.0 / (1.0 + jnp.exp(theirs - mine))
            gate[at, 0:1] = share
            gate[at, 1:2] = 1.0 / (1.0 + jnp.exp(mine - theirs))
            scaled = (share * ups[at, :].astype(F32)).astype(BF16)
            weighted[at, :] = scaled
            return acc + jnp.sum(scaled.astype(F32), axis=0, keepdims=True)

        db_out[...] = lax.fori_loop(0, steps, step, jnp.zeros((1, width), F32))
        for s, n in spans():
            rows_t[:, s : s + n] = jnp.transpose(rows[s : s + n, :])
            weighted_t[:, s : s + n] = jnp.transpose(weighted[s : s + n, :])

    bias = b_in[0]

    def body(i, acc):
        at = pl.ds(pl.multiple_of(i * block, block), block)
        here = rows[at, :]
        u = mm_nt(here, w_in[0]) + bias
        square = u * u
        t = jnp.tanh(ROOT * (u * (1.0 + CUBIC * square)))
        up_half = 0.5 + 0.5 * t
        hidden = (u * up_half).astype(BF16)
        slope = up_half + (0.5 * ROOT) * (u * (1.0 - t * t)) * (1.0 + (3.0 * CUBIC) * square)
        hid[at, :] = hidden
        grad = mm_nt(weighted[at, :], w_out[0]) * slope
        low = grad.astype(BF16)
        pre_g[at, :] = low
        part = mm(hidden, w_out[0])
        part_b = mm(low, w_in[0])

        @pl.when(f == 0)
        def _():
            made[at, :] = part
            pushed[at, :] = part_b

        @pl.when(f > 0)
        def _():
            made[at, :] += part
            pushed[at, :] += part_b

        return acc + jnp.sum(grad, axis=0, keepdims=True)

    db_in[0] = lax.fori_loop(0, steps, body, jnp.zeros((1, w_in.shape[1]), F32))
    dw_out[0] = jnp.transpose(mm(weighted_t[...], hid[...])).astype(BF16)
    dw_in[0] = jnp.transpose(mm(rows_t[...], pre_g[...])).astype(BF16)

    @pl.when(f == last)
    def _():
        own_row = own[...]

        def step(i, carry):
            at = pl.ds(pl.multiple_of(i * block, block), block)
            produced = (made[at, :] + b_out[...]).astype(BF16).astype(F32)
            share = gate[at, 0:1]
            sent[at, :] = (share * produced).astype(BF16)
            inner = jnp.sum(produced * ups[at, :].astype(F32), axis=1, keepdims=True)
            pull = share * gate[at, 1:2] * inner
            rival = other[at, :].astype(jnp.int32)
            spread = (pull * (own_row - jnp.where(lane == rival, 1.0, 0.0))).astype(BF16)
            back[at, :] = (pushed[at, :] + mm_nt(spread, router[...])).astype(BF16)
            hid[at, 0:LANES] = spread
            return carry

        lax.fori_loop(0, steps, step, 0)
        drouter[...] = mm(rows_t[...], hid[:, 0:LANES])


def run_experts(rows, ups, other, own, dense, weights, b_in, b_out, block):
    total, width = rows.shape
    quarters, double, _ = weights.shape
    per = double // 2 // CHUNK
    hidden = quarters * per * CHUNK
    views = weights.reshape(quarters * 2 * per, CHUNK, width)
    in_at = lambda f: ((f // per) * 2 * per + f % per, 0, 0)
    out_at = lambda f: ((f // per) * 2 * per + per + f % per, 0, 0)
    small = dense.shape[1] // LANES - 1
    steps = hidden // CHUNK
    dw_shape = jax.ShapeDtypeStruct((steps, CHUNK, width), BF16)
    outs = pl.pallas_call(
        partial(experts_kernel, block),
        grid=(steps,),
        in_specs=[
            whole((total, width)),
            whole((total, width)),
            whole((total, 1)),
            whole((1, LANES)),
            pl.BlockSpec((width, LANES), lambda f: (0, small), pipeline_mode=pl.Buffered(1)),
            pl.BlockSpec((1, CHUNK, width), in_at),
            pl.BlockSpec((1, CHUNK, width), out_at),
            pl.BlockSpec((1, 1, CHUNK), lambda f: (f, 0, 0)),
            whole((1, width)),
        ],
        out_specs=[
            whole((total, width)),
            whole((total, width)),
            pl.BlockSpec((1, CHUNK, width), lambda f: (f, 0, 0)),
            pl.BlockSpec((1, CHUNK, width), lambda f: (f, 0, 0)),
            pl.BlockSpec((1, 1, CHUNK), lambda f: (f, 0, 0)),
            whole((1, width)),
            whole((width, LANES)),
        ],
        out_shape=[
            jax.ShapeDtypeStruct((total, width), BF16),
            jax.ShapeDtypeStruct((total, width), BF16),
            dw_shape,
            dw_shape,
            jax.ShapeDtypeStruct((steps, 1, CHUNK), F32),
            jax.ShapeDtypeStruct((1, width), F32),
            jax.ShapeDtypeStruct((width, LANES), F32),
        ],
        scratch_shapes=[
            pltpu.VMEM((total, 2), F32),
            pltpu.VMEM((total, width), BF16),
            pltpu.VMEM((width, total), BF16),
            pltpu.VMEM((width, total), BF16),
            pltpu.VMEM((total, width), F32),
            pltpu.VMEM((total, width), F32),
            pltpu.VMEM((total, CHUNK), BF16),
            pltpu.VMEM((total, CHUNK), BF16),
        ],
        compiler_params=params(1),
        name="experts",
        cost_estimate=pl.CostEstimate(
            flops=12 * total * width * hidden, bytes_accessed=20000000, transcendentals=0
        ),
    )(rows, ups, other, own, dense, views, views, b_in.reshape(steps, 1, CHUNK), b_out)
    return outs


def backward_kernel(
    x, kbias, gains, wqkv, wout, triple, context, logs, residual, up, slot, ret,
    input_grad, dqkv, dwout, dgains,
    tg,
):
    step = pl.program_id(0)
    length, width = x.shape
    total = ret.shape[0]
    lanes_total = lane_iota(1, total)

    @pl.when(step == 0)
    def _():
        dqkv[...] = jnp.zeros_like(dqkv)
        dwout[...] = jnp.zeros_like(dwout)
        dgains[...] = jnp.zeros_like(dgains)

    pick = jnp.where(
        (lanes_total == slot[:, 0:1]) | (lanes_total == slot[:, 1:2]), 1.0, 0.0
    ).astype(BF16)
    second_grad = mm(pick, ret[...])
    unit_b, scale_b = norm_stats(residual[...])
    dgains[2:3, :] += jnp.sum(second_grad * unit_b, axis=0, keepdims=True)
    dgains[3:4, :] += jnp.sum(second_grad, axis=0, keepdims=True)
    residual_grad = up[...].astype(F32) + norm_back(second_grad, unit_b, scale_b, gains[2:3, :])
    residual_low = residual_grad.astype(BF16)
    dwout[...] += mm_tn(context[...], residual_low)
    context_grad = mm_nt(residual_low, wout[...]).astype(BF16)

    lane = lane_iota(1, LANES)
    head_width = width // HEADS
    scale = head_width ** (-0.5)
    per = LANES // head_width
    hide = kbias[...]
    for group in range(HEADS // per):
        begin = group * LANES
        queries = triple[:, begin : begin + LANES]
        keys = triple[:, width + begin : width + begin + LANES]
        values = triple[:, 2 * width + begin : 2 * width + begin + LANES]
        pulled = context_grad[:, begin : begin + LANES]
        dq = jnp.zeros((length, LANES), F32)
        dk = jnp.zeros((length, LANES), F32)
        dv = jnp.zeros((length, LANES), F32)
        for inner in range(per):
            head = group * per + inner
            inside = (lane >= inner * head_width) & (lane < (inner + 1) * head_width)
            chosen = queries * jnp.where(inside, scale, 0.0).astype(BF16)
            log_row = logs[0, head : head + 1, :]
            probs = jnp.exp(mm_nt(keys, chosen) + hide - log_row)
            picked = pulled * jnp.where(inside, 1.0, 0.0).astype(BF16)
            prob_grad = mm_nt(values, picked)
            inner_sum = jnp.sum(probs * prob_grad, axis=0, keepdims=True)
            score_grad = (probs * (prob_grad - inner_sum)).astype(BF16)
            dq = jnp.where(inside, mm_tn(score_grad, keys), dq)
            dk = jnp.where(inside, mm(score_grad, queries), dk)
            dv = jnp.where(inside, mm(probs.astype(BF16), pulled), dv)
        tg[:, begin : begin + LANES] = (dq * scale).astype(BF16)
        tg[:, width + begin : width + begin + LANES] = (dk * scale).astype(BF16)
        tg[:, 2 * width + begin : 2 * width + begin + LANES] = dv.astype(BF16)
    unit, scale_a = norm_stats(x[...].astype(F32))
    low = (unit * gains[0:1, :] + gains[1:2, :]).astype(BF16)
    dqkv[...] += mm_tn(low, tg[...])
    first_grad = mm_nt(tg[...], wqkv[...])
    dgains[0:1, :] += jnp.sum(first_grad * unit, axis=0, keepdims=True)
    dgains[1:2, :] += jnp.sum(first_grad, axis=0, keepdims=True)
    input_grad[...] = residual_grad + norm_back(first_grad, unit, scale_a, gains[0:1, :])


def attention_backward(x, mask, gains, dense, triple, context, logs, residual, up, slot, ret):
    total, width = x.shape
    images, length = mask.shape
    rows = lambda i: (i, 0)
    kbias = jnp.where(mask > 0, 0.0, NEGATIVE).reshape(total, 1)
    return pl.pallas_call(
        backward_kernel,
        grid=(images,),
        in_specs=[
            pl.BlockSpec((length, width), rows),
            pl.BlockSpec((length, 1), rows),
            whole(gains.shape),
            pl.BlockSpec((width, 3 * width), lambda i: (0, 0), pipeline_mode=pl.Buffered(1)),
            pl.BlockSpec((width, width), lambda i: (0, 3), pipeline_mode=pl.Buffered(1)),
            pl.BlockSpec((length, 3 * width), rows),
            pl.BlockSpec((length, width), rows),
            pl.BlockSpec((1, HEADS, length), lambda i: (i, 0, 0)),
            pl.BlockSpec((length, width), rows),
            pl.BlockSpec((length, width), rows),
            pl.BlockSpec((length, 2), rows),
            whole(ret.shape),
        ],
        out_specs=[
            pl.BlockSpec((length, width), rows),
            whole((width, 3 * width)),
            whole((width, width)),
            whole((8, width)),
        ],
        out_shape=[
            jax.ShapeDtypeStruct((total, width), F32),
            jax.ShapeDtypeStruct((width, 3 * width), F32),
            jax.ShapeDtypeStruct((width, width), F32),
            jax.ShapeDtypeStruct((8, width), F32),
        ],
        scratch_shapes=[pltpu.VMEM((length, 3 * width), BF16)],
        compiler_params=params(1),
        name="attention_backward",
        cost_estimate=pl.CostEstimate(
            flops=40000000000, bytes_accessed=20000000, transcendentals=0
        ),
    )(x, kbias, gains, dense, dense, triple, context, logs, residual, up, slot, ret)


def combine_kernel(slot, residual, ret, out):
    lanes_total = lane_iota(1, ret.shape[0])
    pick = jnp.where(
        (lanes_total == slot[:, 0:1]) | (lanes_total == slot[:, 1:2]), 1.0, 0.0
    ).astype(BF16)
    out[...] = (residual[...] + mm(pick, ret[...])).astype(BF16)


def combine(slot, residual, ret, block):
    total, width = residual.shape
    rows = lambda i: (i, 0)
    return pl.pallas_call(
        combine_kernel,
        grid=(total // block,),
        in_specs=[
            pl.BlockSpec((block, 2), rows),
            pl.BlockSpec((block, width), rows),
            whole(ret.shape),
        ],
        out_specs=pl.BlockSpec((block, width), rows),
        out_shape=jax.ShapeDtypeStruct((total, width), BF16),
        compiler_params=params(1),
        name="combine",
        cost_estimate=pl.CostEstimate(
            flops=2 * total * ret.shape[0] * width, bytes_accessed=9000000, transcendentals=0
        ),
    )(slot, residual, ret)


def local(
    inputs,
    key_mask,
    routes,
    priority,
    capacity,
    attention_gain,
    attention_shift,
    query_key_value,
    attention_out,
    mixture_gain,
    mixture_shift,
    router_weight,
    expert_in,
    expert_in_bias,
    expert_out,
    expert_out_bias,
    cotangent,
):
    total, width = inputs.shape
    experts = capacity.shape[0]
    cap = 8 * max(1, total // (4 * experts))
    share = query_key_value.shape[0]

    def exchange(a):
        return lax.all_to_all(
            a.reshape(experts, cap, a.shape[-1]), "seq", split_axis=0, concat_axis=0, tiled=True
        ).reshape(a.shape)

    small = jnp.concatenate(
        [
            router_weight,
            jnp.stack([attention_gain, attention_shift, mixture_gain, mixture_shift], axis=1),
            jnp.zeros((share, LANES - experts - 4), BF16),
        ],
        axis=1,
    )
    packed = jnp.concatenate([query_key_value, attention_out, small], axis=1)
    dense = lax.all_gather(packed, "wt", axis=0, tiled=True)
    weights = lax.all_gather(
        jnp.concatenate([expert_in[0], expert_out[0]], axis=0), "wt", axis=0
    )
    biases = lax.all_gather(
        jnp.concatenate([expert_in_bias[0], expert_out_bias[0]]), "wt", axis=0
    ).astype(F32)
    b_in = biases[:, : expert_in_bias.shape[1]].reshape(-1)
    b_out = biases[:, expert_in_bias.shape[1] :].reshape(1, width)
    own_id = lax.axis_index("seq")
    own = (jnp.arange(LANES) == own_id).astype(F32)[None, :]

    slot = make_slots(routes, priority, capacity, cap)
    slot_rows = slot.T
    route_rows = routes.T.astype(F32)
    ups_out, other_out = dispatch(slot_rows, route_rows, cotangent, experts, cap, True)
    ups = exchange(ups_out)
    other = lax.all_to_all(
        other_out.reshape(experts, cap), "seq", split_axis=0, concat_axis=0, tiled=True
    ).reshape(experts * cap, 1)

    gains = dense[:, 4 * width + experts : 4 * width + experts + 4].T.astype(F32)
    gains = jnp.pad(gains, ((0, 4), (0, 0)))
    triple, context, logs, residual, normed = attention_forward(inputs, key_mask, gains, dense)
    (rows_out,) = dispatch(slot_rows, route_rows, normed, experts, cap, False)
    rows = exchange(rows_out)
    sent, back, dw_in, dw_out, db_in, db_out, drouter = run_experts(
        rows, ups, other, own, dense, weights, b_in, b_out, cap
    )
    ret_back = exchange(back)
    ret_sent = exchange(sent)
    input_grad, dqkv, dwout, dgains = attention_backward(
        inputs, key_mask, gains, dense, triple, context, logs, residual, cotangent, slot, ret_back
    )
    block_output = combine(slot, residual, ret_sent, 400)

    tail = jnp.concatenate(
        [drouter[:, :experts], dgains[:4].T, jnp.zeros((width, LANES - experts - 4), F32)], axis=1
    )
    grads = jnp.concatenate([dqkv, dwout, tail], axis=1).astype(BF16)
    part = lax.psum_scatter(grads, "wt", scatter_dimension=0, tiled=True)
    done = lax.psum(part, "seq").astype(F32)
    hidden_share = expert_in.shape[1]
    in_grad = lax.psum_scatter(
        dw_in.reshape(-1, width), "wt", scatter_dimension=0, tiled=True
    ).astype(F32)[None]
    out_grad = lax.psum_scatter(
        dw_out.reshape(-1, width), "wt", scatter_dimension=0, tiled=True
    ).astype(F32)[None]
    in_bias = lax.psum_scatter(
        db_in.reshape(-1).astype(BF16), "wt", scatter_dimension=0, tiled=True
    ).astype(F32)[None]
    out_bias = lax.psum_scatter(
        db_out.reshape(-1).astype(BF16), "wt", scatter_dimension=0, tiled=True
    ).astype(F32)[None]
    base = 4 * width
    return (
        block_output,
        input_grad,
        done[:, base + experts],
        done[:, base + experts + 1],
        done[:, : 3 * width],
        done[:, 3 * width : base],
        done[:, base + experts + 2],
        done[:, base + experts + 3],
        done[:, base : base + experts],
        in_grad,
        in_bias,
        out_grad,
        out_bias,
    )


def solution(mesh):
    both = P(("seq", "wt"), None)
    placed = (
        both,
        both,
        both,
        both,
        P(),
        P("wt"),
        P("wt"),
        P("wt", None),
        P("wt", None),
        P("wt"),
        P("wt"),
        P("wt", None),
        P("seq", "wt", None),
        P("seq", "wt"),
        P("seq", "wt", None),
        P("seq", "wt"),
        both,
    )
    return jax.shard_map(
        local,
        mesh=mesh,
        in_specs=placed,
        out_specs=(
            both,
            both,
            P("wt"),
            P("wt"),
            P("wt", None),
            P("wt", None),
            P("wt"),
            P("wt"),
            P("wt", None),
            P("seq", "wt", None),
            P("seq", "wt"),
            P("seq", "wt", None),
            P("seq", "wt"),
        ),
        check_vma=False,
    )
```

```python
from functools import partial

import jax
import jax.numpy as jnp
from jax import lax
from jax.experimental import pallas as pl
from jax.experimental.pallas import tpu as pltpu
from jax.sharding import PartitionSpec as P

HEADS = 8
NEGATIVE = -1e30
EPSILON = 1e-06
LANES = 128
BIG_STEPS = 2
VMEM_BYTES = 60 * 1024 * 1024
F32 = jnp.float32
BF16 = jnp.bfloat16
ROOT = 0.7978845608028654
CUBIC = 0.044715

NT = (((1,), (1,)), ((), ()))
TN = (((0,), (0,)), ((), ()))


def mm(a, b):
    return jnp.dot(a, b, preferred_element_type=F32)


def mm_nt(a, b):
    return lax.dot_general(a, b, NT, preferred_element_type=F32)


def mm_tn(a, b):
    return lax.dot_general(a, b, TN, preferred_element_type=F32)


def params(steps=0):
    return pltpu.CompilerParams(
        dimension_semantics=("arbitrary",) * steps if steps else None,
        vmem_limit_bytes=VMEM_BYTES,
    )


def cost(micros):
    return pl.CostEstimate(
        flops=int(micros * 1.0e7), bytes_accessed=int(micros * 1.0e4), transcendentals=0
    )


def gain_rows(small, experts):
    turned = jnp.transpose(small[...].astype(F32))
    return turned[experts : experts + 4, :]


def whole(shape):
    zeros = (0,) * len(shape)
    return pl.BlockSpec(shape, lambda *_: zeros, pipeline_mode=pl.Buffered(1))


def gather_slots(slot, parts):
    found = None
    start = 0
    for piece in parts:
        rows = piece[...].reshape(-1, piece.shape[-1])
        lanes = lane_iota(1, rows.shape[0]) + start
        start += rows.shape[0]
        pick = jnp.where((lanes == slot[:, 0:1]) | (lanes == slot[:, 1:2]), 1.0, 0.0)
        piece = jnp.dot(pick.astype(BF16), rows, preferred_element_type=F32)
        found = piece if found is None else found + piece
    return found


def returned_specs(ret, which):
    both, alone = ret
    experts, _, size, width = both.shape
    spot = lambda *_: (0, which, 0, 0)
    return [
        pl.BlockSpec((experts, None, size, width), spot, pipeline_mode=pl.Buffered(1)),
        whole(alone.shape),
    ]


def lane_iota(rows, width):
    return lax.broadcasted_iota(jnp.int32, (rows, width), 1)


def norm_stats(values):
    row_mean = jnp.mean(values, axis=-1, keepdims=True)
    offsets = values - row_mean
    spread = jnp.mean(offsets * offsets, axis=-1, keepdims=True)
    scale = lax.rsqrt(spread + EPSILON)
    return offsets * scale, scale


def norm_back(grad, unit, scale, gain):
    weighted = grad * gain
    first = jnp.mean(weighted, axis=-1, keepdims=True)
    second = jnp.mean(weighted * unit, axis=-1, keepdims=True)
    return scale * (weighted - first - unit * second)


EXTRA = 16


def pack_kernel(wqkv, wout, router, ga, sa, gm, sm, w_in, w_out, b_in, b_out, dense, first, second, tail):
    width = wout.shape[1]
    experts = router.shape[1]
    share = wout.shape[0]
    hidden = w_in.shape[0]
    dense[:, : 3 * width] = wqkv[...]
    dense[:, 3 * width : 4 * width] = wout[...]
    tail[...] = jnp.zeros_like(tail)
    for k, row in enumerate((ga, sa, gm, sm)):
        tail[experts + k : experts + k + 1, 0:share] = row[...].astype(F32)
    columns = jnp.transpose(tail[0:LANES, 0:LANES])[:share, :]
    dense[:, 4 * width :] = columns.astype(BF16)
    dense[:, 4 * width : 4 * width + experts] = router[...]
    first[...] = w_in[...]
    second[0:hidden, :] = w_out[...]
    tail[0:EXTRA, :] = jnp.zeros((EXTRA, width), F32)
    tail[0:1, 0:hidden] = b_in[...].astype(F32)
    tail[1:2, 0:share] = b_out[...].astype(F32)
    second[hidden:, :] = tail[0:EXTRA, :].astype(BF16)


def pack(wqkv, wout, router, gains, w_in, w_out, b_in, b_out):
    share, width = wout.shape
    hidden = w_in.shape[0]
    return pl.pallas_call(
        pack_kernel,
        out_shape=[
            jax.ShapeDtypeStruct((share, 4 * width + LANES), BF16),
            jax.ShapeDtypeStruct((hidden, width), BF16),
            jax.ShapeDtypeStruct((hidden + EXTRA, width), BF16),
        ],
        scratch_shapes=[pltpu.VMEM((LANES, width), F32)],
        compiler_params=params(),
        name="pack",
        cost_estimate=cost(3),
    )(wqkv, wout, router, *[g[None, :] for g in gains], w_in, w_out, b_in, b_out)


def slots_kernel(parts, block, prow, routes, capacity, out, out_rows, poscol, hot, limits, wide):
    total = routes.shape[1]
    experts = capacity.shape[1]
    steps = total // block
    half = LANES // 2
    sub = lax.broadcasted_iota(jnp.int32, (LANES, 1), 0)
    hot_t = jnp.where((routes[0:1, :] == sub) | (routes[1:2, :] + half == sub), 1.0, 0.0)
    hot[...] = jnp.transpose(hot_t).astype(BF16)
    limits[...] = jnp.zeros_like(limits)
    limits[:, 0:experts] = capacity[...].astype(F32)
    limits[:, half : half + experts] = capacity[...].astype(F32)
    lane = lane_iota(1, LANES)
    index = lax.broadcasted_iota(jnp.int32, (total, LANES), 0)
    digits = jnp.where(
        lane_iota(total, LANES) == 0, index // 8, jnp.where(lane_iota(total, LANES) == 1, index % 8, 0)
    ).astype(F32).astype(BF16)

    def find(i, carry):
        at = pl.ds(pl.multiple_of(i * block, block), block)
        token = lax.broadcasted_iota(jnp.int32, (block, 1), 0) + i * block
        hit = jnp.where(prow[...] == token, 1.0, 0.0).astype(BF16)
        poscol[at, :] = mm(hit, digits)
        return carry

    lax.fori_loop(0, steps, find, 0)
    turned = jnp.transpose(poscol[...])
    posrow = turned[0:1, :] * 8.0 + turned[1:2, :]
    low_lanes = lane < half
    seen = jnp.sum(hot[...].astype(F32), axis=0, keepdims=True)
    seen_b = jnp.where(low_lanes, 0.0, pltpu.roll(jnp.broadcast_to(seen, (8, LANES)), half, 1)[0:1, :])
    expert = jnp.where(low_lanes, lane, lane - half)
    front, rest = parts
    base = (expert * front + 1).astype(F32)
    base_b = (experts * front + expert * rest - front + 1).astype(F32)

    def step(i, carry):
        at = pl.ds(pl.multiple_of(i * block, block), block)
        mine = poscol[at, 0:1] * 8.0 + poscol[at, 1:2]
        earlier = jnp.where(posrow < mine, 1.0, 0.0).astype(BF16)
        own = hot[at, :].astype(F32)
        place = mm(earlier, hot[...]) + seen_b
        number = place + jnp.where(place < front, base, base_b)
        value = jnp.where(place < limits[...], number, 0.0) * own
        slot_a = jnp.sum(jnp.where(low_lanes, value, 0.0), axis=1, keepdims=True) - 1.0
        slot_b = jnp.sum(jnp.where(low_lanes, 0.0, value), axis=1, keepdims=True) - 1.0
        wide[at, :] = jnp.where(lane == 0, slot_a, slot_b)
        out[at, :] = jnp.where(lane_iota(1, 2) == 0, slot_a, slot_b).astype(jnp.int32)
        return carry

    lax.fori_loop(0, steps, step, 0)
    out_rows[...] = jnp.transpose(wide[...])[0:2, :].astype(jnp.int32)


def make_slots(route_rows, priority, capacity, parts):
    total = route_rows.shape[1]
    return pl.pallas_call(
        partial(slots_kernel, parts, 400),
        out_shape=[
            jax.ShapeDtypeStruct((total, 2), jnp.int32),
            jax.ShapeDtypeStruct((2, total), jnp.int32),
        ],
        scratch_shapes=[
            pltpu.VMEM((total, LANES), F32),
            pltpu.VMEM((total, LANES), BF16),
            pltpu.VMEM((1, LANES), F32),
            pltpu.VMEM((total, LANES), F32),
        ],
        compiler_params=params(),
        name="slots",
        cost_estimate=cost(8),
    )(priority, route_rows, capacity[None, :])


def dispatch_kernel(parts, with_other, slot_rows, route_rows, rows, *outs):
    e = pl.program_id(0)
    if not with_other:
        carry, *outs = outs
        outs[-1][0, parts[-1] :, :] = carry[0]
    start = 0
    for size, out in zip(parts, outs):
        place = lax.broadcasted_iota(jnp.int32, (size, 1), 0) + (start + e * size)
        start += pl.num_programs(0) * size
        hit_a = slot_rows[0:1, :] == place
        hit_b = slot_rows[1:2, :] == place
        pick = jnp.where(hit_a | hit_b, 1.0, 0.0).astype(BF16)
        out[0, 0:size, :] = mm(pick, rows[...]).astype(BF16)
        if with_other:
            named = route_rows[...].astype(F32) + 1.0
            found = jnp.where(hit_a, named[1:2, :], jnp.where(hit_b, named[0:1, :], 0.0))
            column = jnp.sum(found, axis=1, keepdims=True) - 1.0
            turned = jnp.transpose(jnp.broadcast_to(column, (size, LANES)))
            out[0, size : size + EXTRA, 0:size] = turned[0:EXTRA, :].astype(BF16)


def dispatch(slot_rows, route_rows, rows, experts, parts, carry=None):
    total, width = rows.shape
    with_other = carry is None
    if with_other:
        tall = [size + EXTRA for size in parts]
        extra, extra_spec = (), ()
    else:
        tall = [parts[0], parts[1] + carry.shape[1]]
        extra = (carry,)
        extra_spec = (pl.BlockSpec((1,) + carry.shape[1:], lambda e: (e, 0, 0)),)
    return pl.pallas_call(
        partial(dispatch_kernel, parts, with_other),
        grid=(experts,),
        in_specs=[whole((2, total)), whole((2, total)), whole((total, width)), *extra_spec],
        out_specs=[pl.BlockSpec((1, t, width), lambda e: (e, 0, 0)) for t in tall],
        out_shape=[jax.ShapeDtypeStruct((experts, t, width), BF16) for t in tall],
        compiler_params=params(1),
        name="dispatch",
        cost_estimate=cost(10),
    )(slot_rows, route_rows, rows, *extra)


def attention_kernel(
    experts, x, mask, small, wqkv, wout, triple, context, logs, residual, normed, gains
):
    @pl.when(pl.program_id(0) == 0)
    def _():
        gains[0:4, :] = gain_rows(small, experts)

    width = x.shape[1]
    length = x.shape[0]
    x_wide = x[...].astype(F32)
    unit, _ = norm_stats(x_wide)
    low = (unit * gains[0:1, :] + gains[1:2, :]).astype(BF16)
    mixed = mm(low, wqkv[...]).astype(BF16)
    triple[...] = mixed
    bias = jnp.where(mask[0] > 0, 0.0, NEGATIVE)
    lane = lane_iota(1, LANES)
    head_width = width // HEADS
    scale = head_width ** (-0.5)
    per = LANES // head_width
    gathered = jnp.zeros((length, LANES), F32)
    lanes_all = lane_iota(length, LANES)
    for group in range(HEADS // per):
        begin = group * LANES
        queries = mixed[:, begin : begin + LANES]
        keys = mixed[:, width + begin : width + begin + LANES]
        values = mixed[:, 2 * width + begin : 2 * width + begin + LANES]
        merged = jnp.zeros((length, LANES), F32)
        for inner in range(per):
            inside = (lane >= inner * head_width) & (lane < (inner + 1) * head_width)
            chosen = queries * jnp.where(inside, scale, 0.0).astype(BF16)
            scores = mm_nt(chosen, keys) + bias
            peak = jnp.max(scores, axis=-1, keepdims=True)
            raised = jnp.exp(scores - peak)
            sums = jnp.sum(raised, axis=-1, keepdims=True)
            found = mm(raised.astype(BF16), values) * (1.0 / sums)
            merged = jnp.where(inside, found, merged)
            gathered = jnp.where(
                lanes_all == group * per + inner, peak + jnp.log(sums), gathered
            )
        context[:, begin : begin + LANES] = merged.astype(BF16)
    logs[0] = jnp.transpose(gathered)[:HEADS, :]
    after = x_wide + mm(context[...], wout[...])
    residual[...] = after
    unit_b, _ = norm_stats(after)
    normed[...] = (unit_b * gains[2:3, :] + gains[3:4, :]).astype(BF16)


def small_spec(width):
    last = 4 * width // LANES
    return pl.BlockSpec((width, LANES), lambda i: (0, last), pipeline_mode=pl.Buffered(1))


def attention_forward(x, mask, dense, experts):
    total, width = x.shape
    images, length = mask.shape
    rows = lambda i: (i, 0)
    return pl.pallas_call(
        partial(attention_kernel, experts),
        grid=(images,),
        in_specs=[
            pl.BlockSpec((length, width), rows),
            pl.BlockSpec((1, 1, length), lambda i: (i, 0, 0)),
            small_spec(width),
            pl.BlockSpec((width, 3 * width), lambda i: (0, 0), pipeline_mode=pl.Buffered(1)),
            pl.BlockSpec((width, width), lambda i: (0, 3), pipeline_mode=pl.Buffered(1)),
        ],
        out_specs=[
            pl.BlockSpec((length, 3 * width), rows),
            pl.BlockSpec((length, width), rows),
            pl.BlockSpec((1, HEADS, length), lambda i: (i, 0, 0)),
            pl.BlockSpec((length, width), rows),
            pl.BlockSpec((length, width), rows),
        ],
        out_shape=[
            jax.ShapeDtypeStruct((total, 3 * width), BF16),
            jax.ShapeDtypeStruct((total, width), BF16),
            jax.ShapeDtypeStruct((images, HEADS, length), F32),
            jax.ShapeDtypeStruct((total, width), F32),
            jax.ShapeDtypeStruct((total, width), BF16),
        ],
        scratch_shapes=[pltpu.VMEM((8, width), F32)],
        compiler_params=params(1),
        name="attention_forward",
        cost_estimate=cost(17),
    )(x, mask.reshape(images, 1, length), dense, dense, dense)


def experts_kernel(block, more, *refs):
    if more:
        mixed, own, router, w_in, w_out, b_in, b_out, *rest = refs
        old_mine, old_mate, old_router, back, sent, dw_mine, dw_mate, drouter, *rest = rest
        *rest, rows = rest
        ups, shift = mixed, block

        @pl.when(pl.program_id(0) == 0)
        def _():
            for i in range(mixed.shape[0]):
                rows[i * block : (i + 1) * block, :] = mixed[i, 0:block, :]

        outs = (back, sent, 0)
        old = (old_mine, old_mate, old_router)
    else:
        rows, ups, own, router, w_in, w_out, b_in, b_out, *rest = refs
        ret, dw_mine, dw_mate, drouter, *rest = rest
        outs = (ret, ret, block)
        shift, old = 0, None
    experts_body(
        block, rows, ups, shift, own, router, w_in, w_out, b_in, b_out, old,
        outs, dw_mine, dw_mate, drouter, *rest,
    )


def experts_body(
    block, rows, ups, shift, own, router, w_in, w_out, b_in, b_out, old,
    outs, dw_mine, dw_mate, drouter,
    gate, weighted, made, pushed, hid, pre_g, other, db,
):
    f = pl.program_id(0)
    last = pl.num_programs(0) - 1
    total, width = rows.shape
    steps = total // block
    lane = lane_iota(1, LANES)

    @pl.when(f == 0)
    def _():
        own_hot = own[...] > 0.0

        def step(i, acc):
            at = pl.ds(pl.multiple_of(i * block, block), block)
            logits = mm(rows[at, :], router[...])
            mine = jnp.sum(jnp.where(own_hot, logits, 0.0), axis=1, keepdims=True)
            named = ups[i, shift + block : shift + block + EXTRA, 0:block].astype(F32)
            rival = jnp.transpose(named)[:, 0:1].astype(jnp.int32)
            other[at, :] = rival
            theirs = jnp.sum(jnp.where(lane == rival, logits, 0.0), axis=1, keepdims=True)
            share = 1.0 / (1.0 + jnp.exp(theirs - mine))
            gate[at, 0:1] = share
            gate[at, 1:2] = 1.0 / (1.0 + jnp.exp(mine - theirs))
            scaled = (share * ups[i, shift : shift + block, :].astype(F32)).astype(BF16)
            weighted[at, :] = scaled
            return acc + jnp.sum(scaled.astype(F32), axis=0, keepdims=True)

        db[...] = jnp.zeros_like(db)
        db[1:2, :] = lax.fori_loop(0, steps, step, jnp.zeros((1, width), F32))

    chunk = w_in.shape[1]
    hidden_share = (dw_mine.shape[1] - EXTRA) // 2
    per = hidden_share // chunk
    place = f % per
    biases = b_in[0, 0:1, :].astype(F32)
    bias = biases[:, 0:chunk]
    for k in range(1, per):
        bias = jnp.where(place == k, biases[:, k * chunk : (k + 1) * chunk], bias)

    big = total // BIG_STEPS

    def body(i, acc):
        at = pl.ds(pl.multiple_of(i * big, big), big)
        here = rows[at, :]
        u = mm_nt(here, w_in[0]) + bias
        inner = ROOT + (ROOT * CUBIC) * (u * u)
        share = 0.5 + 0.5 * jnp.tanh(u * inner)
        raised = u * share
        hidden = raised.astype(BF16)
        slope = share + raised * (1.0 - share) * (6.0 * inner - 4.0 * ROOT)
        hid[at, :] = hidden
        grad = mm_nt(weighted[at, :], w_out[0]) * slope
        low = grad.astype(BF16)
        pre_g[at, :] = low
        part = mm(hidden, w_out[0])
        part_b = mm(low, w_in[0])

        @pl.when(f == 0)
        def _():
            made[at, :] = part
            pushed[at, :] = part_b

        @pl.when(f > 0)
        def _():
            made[at, :] += part
            pushed[at, :] += part_b

        return acc + jnp.sum(grad, axis=0, keepdims=True)

    db_here = lax.fori_loop(0, BIG_STEPS, body, jnp.zeros((1, chunk), F32))
    for k in range(per):

        @pl.when(place == k)
        def _():
            db[0:1, k * chunk : (k + 1) * chunk] = db_here

    dw_out_here = mm_tn(hid[...], weighted[...])
    dw_in_here = mm_tn(pre_g[...], rows[...])

    def put(target, prior):
        spots = (
            (pl.ds(pl.multiple_of(place * chunk, chunk), chunk), dw_in_here),
            (pl.ds(pl.multiple_of(hidden_share + place * chunk, chunk), chunk), dw_out_here),
            (pl.ds(2 * hidden_share, EXTRA), db[...]),
        )
        for spot, value in spots:
            if prior is not None:
                value = value + prior[0, spot, :].astype(F32)
            target[0, spot, :] = value.astype(BF16)

    quarters = (last + 1) // per

    @pl.when(f // per < quarters // 2)
    def _():
        put(dw_mine, old and old[0])

    @pl.when(f // per >= quarters // 2)
    def _():
        put(dw_mate, old and old[1])

    @pl.when(f == last)
    def _():
        own_row = own[...]
        back, sent, after = outs

        def step(i, carry):
            at = pl.ds(pl.multiple_of(i * block, block), block)
            produced = (made[at, :] + b_out[...]).astype(BF16).astype(F32)
            share = gate[at, 0:1]
            sent[i, after : after + block, :] = (share * produced).astype(BF16)
            inner = jnp.sum(produced * ups[i, shift : shift + block, :].astype(F32), axis=1, keepdims=True)
            pull = share * gate[at, 1:2] * inner
            rival = other[at, :]
            spread = (pull * (own_row - jnp.where(lane == rival, 1.0, 0.0))).astype(BF16)
            back[i, 0:block, :] = (pushed[at, :] + mm_nt(spread, router[...])).astype(BF16)
            hid[at, 0:LANES] = spread
            return carry

        lax.fori_loop(0, steps, step, 0)
        drouter[...] = mm_tn(rows[...], hid[:, 0:LANES]) + (0.0 if old is None else old[2][...])


def run_experts(given, block, own, dense, weights, b_out, old):
    experts, _, width = given[0].shape
    total = experts * block
    first, second = weights
    quarters, share, _ = first.shape
    chunk = min(share, 512)
    per = share // chunk
    half = quarters // 2
    at = lambda f: (f // per, f % per, 0)
    bias_at = lambda f: (f // per, share // EXTRA, 0)
    mine_at = lambda f: (jnp.minimum(f // per, half - 1), 0, 0)
    mate_at = lambda f: (jnp.maximum(f // per - half, 0), 0, 0)
    double = 2 * share + EXTRA
    steps = quarters * per
    dw_shape = jax.ShapeDtypeStruct((half, double, width), BF16)
    sums = [
        pl.BlockSpec((1, double, width), mine_at),
        pl.BlockSpec((1, double, width), mate_at),
        whole((width, LANES)),
    ]
    if old:
        given_specs = [whole(given[0].shape)]
        ret_shapes = [(experts, block, width)] * 2
        more_scratch = [pltpu.VMEM((total, width), BF16)]
    else:
        given = (given[0].reshape(total, width), given[1])
        given_specs = [whole(given[0].shape), whole(given[1].shape)]
        ret_shapes = [(experts, 2 * block, width)]
        more_scratch = []
    return pl.pallas_call(
        partial(experts_kernel, block, bool(old)),
        grid=(steps,),
        in_specs=given_specs
        + [
            whole((1, LANES)),
            small_spec(width),
            pl.BlockSpec((1, chunk, width), at),
            pl.BlockSpec((1, chunk, width), at),
            pl.BlockSpec((1, EXTRA, width), bias_at),
            whole((1, width)),
        ]
        + (sums if old else []),
        out_specs=[whole(r) for r in ret_shapes] + sums,
        out_shape=[jax.ShapeDtypeStruct(r, BF16) for r in ret_shapes]
        + [dw_shape, dw_shape, jax.ShapeDtypeStruct((width, LANES), F32)],
        scratch_shapes=[
            pltpu.VMEM((total, 2), F32),
            pltpu.VMEM((total, width), BF16),
            pltpu.VMEM((total, width), F32),
            pltpu.VMEM((total, width), F32),
            pltpu.VMEM((total, chunk), BF16),
            pltpu.VMEM((total, chunk), BF16),
            pltpu.VMEM((total, 1), jnp.int32),
            pltpu.VMEM((EXTRA, width), F32),
        ]
        + more_scratch,
        compiler_params=params(1),
        name="experts",
        cost_estimate=cost(50),
    )(*given, own, dense, first, second, second, b_out, *old)


def backward_kernel(
    experts, x, mask, small, wqkv, wout, triple, context, logs, residual, up, slot, ret_a, ret_b, drouter,
    input_grad, packed,
    tg, gains, dqkv, dwout, dgains,
):
    step = pl.program_id(0)
    length, width = x.shape

    @pl.when(step == 0)
    def _():
        dqkv[...] = jnp.zeros_like(dqkv)
        dwout[...] = jnp.zeros_like(dwout)
        dgains[...] = jnp.zeros_like(dgains)
        gains[0:4, :] = gain_rows(small, experts)

    second_grad = gather_slots(slot, (ret_a, ret_b))
    unit_b, scale_b = norm_stats(residual[...])
    dgains[experts + 2 : experts + 3, :] += jnp.sum(second_grad * unit_b, axis=0, keepdims=True)
    dgains[experts + 3 : experts + 4, :] += jnp.sum(second_grad, axis=0, keepdims=True)
    residual_grad = up[...].astype(F32) + norm_back(second_grad, unit_b, scale_b, gains[2:3, :])
    residual_low = residual_grad.astype(BF16)
    dwout[...] += mm_tn(context[...], residual_low)
    context_grad = mm_nt(residual_low, wout[...]).astype(BF16)

    lane = lane_iota(1, LANES)
    head_width = width // HEADS
    scale = head_width ** (-0.5)
    per = LANES // head_width
    hide_row = jnp.where(mask[0] > 0, 0.0, NEGATIVE)
    hide = jnp.transpose(jnp.broadcast_to(hide_row, (LANES, length)))[:, 0:1]
    for group in range(HEADS // per):
        begin = group * LANES
        queries = triple[:, begin : begin + LANES]
        keys = triple[:, width + begin : width + begin + LANES]
        values = triple[:, 2 * width + begin : 2 * width + begin + LANES]
        pulled = context_grad[:, begin : begin + LANES]
        dq = jnp.zeros((length, LANES), F32)
        dk = jnp.zeros((length, LANES), F32)
        dv = jnp.zeros((length, LANES), F32)
        for inner in range(per):
            head = group * per + inner
            inside = (lane >= inner * head_width) & (lane < (inner + 1) * head_width)
            chosen = queries * jnp.where(inside, scale, 0.0).astype(BF16)
            log_row = logs[0, head : head + 1, :]
            probs = jnp.exp(mm_nt(keys, chosen) + hide - log_row)
            picked = pulled * jnp.where(inside, 1.0, 0.0).astype(BF16)
            prob_grad = mm_nt(values, picked)
            inner_sum = jnp.sum(probs * prob_grad, axis=0, keepdims=True)
            score_grad = (probs * (prob_grad - inner_sum)).astype(BF16)
            dq = jnp.where(inside, mm_tn(score_grad, keys), dq)
            dk = jnp.where(inside, mm(score_grad, queries), dk)
            dv = jnp.where(inside, mm(probs.astype(BF16), pulled), dv)
        tg[:, begin : begin + LANES] = (dq * scale).astype(BF16)
        tg[:, width + begin : width + begin + LANES] = (dk * scale).astype(BF16)
        tg[:, 2 * width + begin : 2 * width + begin + LANES] = dv.astype(BF16)
    unit, scale_a = norm_stats(x[...].astype(F32))
    low = (unit * gains[0:1, :] + gains[1:2, :]).astype(BF16)
    dqkv[...] += mm_tn(low, tg[...])
    first_grad = mm_nt(tg[...], wqkv[...])
    dgains[experts + 0 : experts + 1, :] += jnp.sum(first_grad * unit, axis=0, keepdims=True)
    dgains[experts + 1 : experts + 2, :] += jnp.sum(first_grad, axis=0, keepdims=True)
    input_grad[...] = residual_grad + norm_back(first_grad, unit, scale_a, gains[0:1, :])

    @pl.when(step == pl.num_programs(0) - 1)
    def _():
        packed[:, : 3 * width] = dqkv[...].astype(BF16)
        packed[:, 3 * width : 4 * width] = dwout[...].astype(BF16)
        packed[:, 4 * width :] = (drouter[...] + jnp.transpose(dgains[...])).astype(BF16)


def attention_backward(
    x, mask, dense, triple, context, logs, residual, up, slot, ret, drouter, experts
):
    total, width = x.shape
    images, length = mask.shape
    rows = lambda i: (i, 0)
    return pl.pallas_call(
        partial(backward_kernel, experts),
        grid=(images,),
        in_specs=[
            pl.BlockSpec((length, width), rows),
            pl.BlockSpec((1, 1, length), lambda i: (i, 0, 0)),
            small_spec(width),
            pl.BlockSpec((width, 3 * width), lambda i: (0, 0), pipeline_mode=pl.Buffered(1)),
            pl.BlockSpec((width, width), lambda i: (0, 3), pipeline_mode=pl.Buffered(1)),
            pl.BlockSpec((length, 3 * width), rows),
            pl.BlockSpec((length, width), rows),
            pl.BlockSpec((1, HEADS, length), lambda i: (i, 0, 0)),
            pl.BlockSpec((length, width), rows),
            pl.BlockSpec((length, width), rows),
            pl.BlockSpec((length, 2), rows),
            *returned_specs(ret, 0),
            whole((width, LANES)),
        ],
        out_specs=[
            pl.BlockSpec((length, width), rows),
            whole((width, 4 * width + LANES)),
        ],
        out_shape=[
            jax.ShapeDtypeStruct((total, width), F32),
            jax.ShapeDtypeStruct((width, 4 * width + LANES), BF16),
        ],
        scratch_shapes=[
            pltpu.VMEM((length, 3 * width), BF16),
            pltpu.VMEM((8, width), F32),
            pltpu.VMEM((width, 3 * width), F32),
            pltpu.VMEM((width, width), F32),
            pltpu.VMEM((LANES, width), F32),
        ],
        compiler_params=params(1),
        name="attention_backward",
        cost_estimate=cost(50),
    )(
        x, mask.reshape(images, 1, length), dense, dense, dense, triple, context, logs, residual,
        up, slot, *ret, drouter,
    )


def combine_kernel(slot, residual, ret_a, ret_b, out):
    out[...] = (residual[...] + gather_slots(slot, (ret_a, ret_b))).astype(BF16)


def combine(slot, residual, ret, block):
    total, width = residual.shape
    rows = lambda i: (i, 0)
    return pl.pallas_call(
        combine_kernel,
        grid=(total // block,),
        in_specs=[
            pl.BlockSpec((block, 2), rows),
            pl.BlockSpec((block, width), rows),
            *returned_specs(ret, 1),
        ],
        out_specs=pl.BlockSpec((block, width), rows),
        out_shape=jax.ShapeDtypeStruct((total, width), BF16),
        compiler_params=params(1),
        name="combine",
        cost_estimate=cost(10),
    )(slot, residual, *ret)


class PlainPlan:
    def __init__(self, seq, wt):
        self.seq, self.wt = seq, wt

    def own_id(self):
        return lax.axis_index("seq")

    def exchange(self, a):
        return lax.all_to_all(a, "seq", split_axis=0, concat_axis=0, tiled=True)

    def begin_dense(self, packed):
        return packed

    def gather_dense(self, packed, begun):
        return lax.all_gather(begun, "wt", axis=0, tiled=True)

    def begin_fetch(self, packed):
        return (packed,)

    def fetch(self, packed, begun):
        return lax.all_gather(begun[0], "wt", axis=0)

    def spread_out_bias(self, quarters):
        return quarters

    def begin_reduce(self, mine, mate):
        return (jnp.concatenate([mine, mate]).reshape(-1, mine.shape[-1]),)

    def reduce_expert(self, parts):
        (parts,) = parts
        return lax.psum_scatter(parts, "wt", scatter_dimension=0, tiled=True)

    def finish_expert(self, parts, received):
        return received.astype(F32)

    def begin_dense_sum(self, grads):
        return lax.psum_scatter(grads, "wt", scatter_dimension=0, tiled=True)

    def reduce_dense(self, part):
        return lax.psum(part, "seq").astype(F32)


class CubePlan:
    AXES = ("seq", "wt")

    def __init__(self, seq, wt):
        self.seq, self.wt = seq, wt
        self.levels = seq // 2
        places = [
            (z, y, x, c)
            for z in range(self.levels)
            for y in range(2)
            for x in range(2)
            for c in range(2)
        ]
        flat = self.flat
        self.cross = [(flat(*p), flat(p[0], p[1], 1 - p[2], p[3])) for p in places]
        self.core = [(flat(*p), flat(p[0], p[1], p[2], 1 - p[3])) for p in places]
        swap = lambda p: (p[0] ^ 2, p[1], 1, p[3]) if p[2] == 0 else (p[0], p[1], 0, p[3])
        self.first = [(flat(*p), flat(*swap(p))) for p in places]
        self.second = [
            (flat(*p), flat(p[0] ^ 2, p[1], 1, p[3])) for p in places if p[2] == 1
        ]
        self.groups = [
            [self.host(half, e, c) for e in range(seq)] for half in range(2) for c in range(2)
        ]

    def flat(self, z, y, x, c):
        return (z * 2 + y) * self.wt + x * 2 + c

    def host(self, half, expert, c):
        z, y = expert // 2, expert % 2
        if z // 2 == half:
            return self.flat(z, y, 0, c)
        return self.flat(z ^ 2, y, 1, c)

    def send(self, a, pairs):
        return lax.ppermute(a, self.AXES, pairs)

    def x_zero(self):
        return lax.axis_index("wt") < 2

    def core_zero(self):
        return lax.axis_index("wt") % 2 == 0

    def own_id(self):
        rank = lax.axis_index("seq")
        return jnp.where(self.x_zero(), rank, rank ^ 4)

    def exchange(self, a):
        return lax.all_to_all(
            a, self.AXES, split_axis=0, concat_axis=0, axis_index_groups=self.groups, tiled=True
        )

    def begin_dense(self, packed):
        return self.send(packed, self.cross)

    def gather_dense(self, packed, far):
        mate = self.send(packed, self.core)
        far_mate = self.send(far, self.core)
        flip = self.x_zero()
        low, high = jnp.where(flip, packed, far), jnp.where(flip, far, packed)
        low_mate, high_mate = jnp.where(flip, mate, far_mate), jnp.where(flip, far_mate, mate)
        first = self.core_zero()
        return jnp.concatenate(
            [
                jnp.where(first, low, low_mate),
                jnp.where(first, low_mate, low),
                jnp.where(first, high, high_mate),
                jnp.where(first, high_mate, high),
            ],
            axis=0,
        )

    def begin_fetch(self, packed):
        return self.send(packed, self.first), self.send(packed, self.second)

    def fetch(self, packed, begun):
        got, got_b = begun
        flip = self.x_zero()
        low = jnp.where(flip, packed, got)
        high = jnp.where(flip, got, got_b)
        return jnp.stack([low, high, self.send(low, self.core), self.send(high, self.core)])

    def spread_out_bias(self, quarters):
        a, b, c, d = (quarters[i] for i in range(4))
        return jnp.where(
            self.core_zero(), jnp.stack([a, c, b, d]), jnp.stack([c, a, d, b])
        )

    def begin_reduce(self, mine, mate):
        got = self.send(mate, self.core)
        low = (mine[0].astype(F32) + got[0].astype(F32)).astype(BF16)
        high = (mine[1].astype(F32) + got[1].astype(F32)).astype(BF16)
        return low, high, jnp.where(self.x_zero(), high, low)

    def reduce_expert(self, parts):
        low, high, give = parts
        return self.send(give, self.first_back()), self.send(high, self.second)

    def finish_expert(self, parts, received):
        far, far_b = received
        return jnp.where(self.x_zero(), parts[0], far_b).astype(F32) + far.astype(F32)

    def first_back(self):
        return [(b, a) for a, b in self.first]

    def begin_dense_sum(self, grads):
        share = grads.shape[0] // 4
        width = grads.shape[1]
        parts = [grads[i * share : (i + 1) * share] for i in range(4)]
        first = self.core_zero()
        keep = [jnp.where(first, parts[0], parts[1]), jnp.where(first, parts[2], parts[3])]
        give = [jnp.where(first, parts[1], parts[0]), jnp.where(first, parts[3], parts[2])]
        got = [self.send(v.astype(BF16), self.core).astype(F32) for v in give]
        low, high = keep[0].astype(F32) + got[0], keep[1].astype(F32) + got[1]
        flip = self.x_zero()
        out = self.send(jnp.where(flip, high, low).astype(BF16), self.cross)
        mine = jnp.where(flip, low, high) + out.astype(F32)
        return mine.astype(BF16)

    def reduce_dense(self, mine):
        share, width = mine.shape
        pieces = mine.reshape(self.seq, share // self.seq, width)
        swap = lambda v: lax.all_to_all(v, "seq", split_axis=0, concat_axis=0, tiled=True)
        total = jnp.sum(swap(pieces).astype(F32), axis=0, keepdims=True).astype(BF16)
        spread = swap(jnp.broadcast_to(total, pieces.shape))
        return spread.reshape(share, width).astype(F32)


def plan_of(seq, wt):
    return CubePlan(seq, wt) if (seq, wt) == (8, 4) else PlainPlan(seq, wt)


def local(
    inputs,
    key_mask,
    routes,
    priority,
    capacity,
    attention_gain,
    attention_shift,
    query_key_value,
    attention_out,
    mixture_gain,
    mixture_shift,
    router_weight,
    expert_in,
    expert_in_bias,
    expert_out,
    expert_out_bias,
    cotangent,
):
    total, width = inputs.shape
    experts = capacity.shape[0]
    cap = 8 * max(1, total // (4 * experts))
    share = query_key_value.shape[0]
    hidden_share = expert_in.shape[1]
    plan = plan_of(lax.axis_size("seq"), lax.axis_size("wt"))

    tie = lax.optimization_barrier
    front = (cap // 2 + EXTRA - 1) // EXTRA * EXTRA
    parts = (front, cap - front)
    packed, *shards = pack(
        query_key_value, attention_out, router_weight,
        (attention_gain, attention_shift, mixture_gain, mixture_shift),
        expert_in[0], expert_out[0], expert_in_bias, expert_out_bias,
    )
    fetched = [plan.begin_fetch(shard) for shard in shards]
    far = plan.begin_dense(packed)
    own = (jnp.arange(LANES) == plan.own_id()).astype(F32)[None, :]
    route_rows = routes.T
    slot, slot_rows = make_slots(route_rows, priority, capacity, parts)
    slot_rows, far = tie((slot_rows, far))
    ups_a, ups_b = dispatch(slot_rows, route_rows, cotangent, experts, parts)
    dense = plan.gather_dense(packed, far)
    dense, ups_a, fetched[0] = tie((dense, ups_a, fetched[0]))
    ups_a = plan.exchange(ups_a)

    triple, context, logs, residual, normed = attention_forward(inputs, key_mask, dense, experts)
    rows_a, mixed_b = dispatch(slot_rows, route_rows, normed, experts, parts, ups_b)
    rows_a, ups_a, fetched[1] = tie((rows_a, ups_a, fetched[1]))
    weights = [plan.fetch(*pair) for pair in zip(shards, fetched)]
    b_out = plan.spread_out_bias(
        weights[1][:, hidden_share + 1, :share].astype(F32)
    ).reshape(1, width)
    rows_a = plan.exchange(rows_a)
    rows_a, mixed_b = tie((rows_a, mixed_b))
    mixed_b = plan.exchange(mixed_b)
    ret_a, *sums = run_experts((rows_a, ups_a), parts[0], own, dense, weights, b_out, ())
    ret_a, mixed_b = tie((ret_a, mixed_b))
    ret_a = plan.exchange(ret_a)
    back_b, sent_b, *sums = run_experts(
        (mixed_b,), parts[1], own, dense, weights, b_out, tuple(sums)
    )
    back_b, ret_a = tie((back_b, ret_a))
    back_b = plan.exchange(back_b)
    halves = plan.begin_reduce(*sums[:2])
    back_b, sent_b, halves = tie((back_b, sent_b, halves))
    sent_b = plan.exchange(sent_b)
    received = plan.reduce_expert(halves)
    ret_a = ret_a.reshape(experts, 2, front, width)
    input_grad, grads = attention_backward(
        inputs, key_mask, dense, triple, context, logs, residual, cotangent, slot,
        (ret_a, back_b), sums[2], experts,
    )
    grads, sent_b, received = tie((grads, sent_b, received))
    mine = plan.begin_dense_sum(grads)
    shard = plan.finish_expert(halves, received)
    done = plan.reduce_dense(mine)
    block_output = combine(slot, residual, (ret_a, sent_b), 400)
    base = 4 * width
    rank = lax.axis_index("wt")
    return (
        block_output,
        input_grad,
        done[:, base + experts],
        done[:, base + experts + 1],
        done[:, : 3 * width],
        done[:, 3 * width : base],
        done[:, base + experts + 2],
        done[:, base + experts + 3],
        done[:, base : base + experts],
        shard[None, :hidden_share],
        shard[2 * hidden_share, :hidden_share][None],
        shard[None, hidden_share : 2 * hidden_share],
        lax.dynamic_slice(shard[2 * hidden_share + 1], (rank * share,), (share,))[None],
    )


def solution(mesh):
    both = P(("seq", "wt"), None)
    placed = (
        both,
        both,
        both,
        both,
        P(),
        P("wt"),
        P("wt"),
        P("wt", None),
        P("wt", None),
        P("wt"),
        P("wt"),
        P("wt", None),
        P("seq", "wt", None),
        P("seq", "wt"),
        P("seq", "wt", None),
        P("seq", "wt"),
        both,
    )
    return jax.shard_map(
        local,
        mesh=mesh,
        in_specs=placed,
        out_specs=(
            both,
            both,
            P("wt"),
            P("wt"),
            P("wt", None),
            P("wt", None),
            P("wt"),
            P("wt"),
            P("wt", None),
            P("seq", "wt", None),
            P("seq", "wt"),
            P("seq", "wt", None),
            P("seq", "wt"),
        ),
        check_vma=False,
    )
```

```python
from functools import partial

import jax
import jax.numpy as jnp
from jax import lax
from jax.experimental import pallas as pl
from jax.experimental.pallas import tpu as pltpu
from jax.sharding import PartitionSpec as P

HEADS = 8
NEGATIVE = -1e30
EPSILON = 1e-06
LANES = 128
BIG_STEPS = 2
VMEM_BYTES = 60 * 1024 * 1024
F32 = jnp.float32
BF16 = jnp.bfloat16
ROOT = 0.7978845608028654
CUBIC = 0.044715

NT = (((1,), (1,)), ((), ()))
TN = (((0,), (0,)), ((), ()))


def mm(a, b):
    return jnp.dot(a, b, preferred_element_type=F32)


def mm_nt(a, b):
    return lax.dot_general(a, b, NT, preferred_element_type=F32)


def mm_tn(a, b):
    return lax.dot_general(a, b, TN, preferred_element_type=F32)


def params(steps=0):
    return pltpu.CompilerParams(
        dimension_semantics=("arbitrary",) * steps if steps else None,
        vmem_limit_bytes=VMEM_BYTES,
    )


def cost(micros):
    return pl.CostEstimate(
        flops=int(micros * 1.0e7), bytes_accessed=int(micros * 1.0e4), transcendentals=0
    )


def gain_rows(small, experts):
    turned = jnp.transpose(small[...].astype(F32))
    return turned[experts : experts + 4, :]


def whole(shape):
    zeros = (0,) * len(shape)
    return pl.BlockSpec(shape, lambda *_: zeros, pipeline_mode=pl.Buffered(1))


def gather_slots(slot, parts):
    found = None
    start = 0
    for piece in parts:
        rows = piece[...].reshape(-1, piece.shape[-1])
        lanes = lane_iota(1, rows.shape[0]) + start
        start += rows.shape[0]
        pick = jnp.where((lanes == slot[:, 0:1]) | (lanes == slot[:, 1:2]), 1.0, 0.0)
        piece = jnp.dot(pick.astype(BF16), rows, preferred_element_type=F32)
        found = piece if found is None else found + piece
    return found


def returned_specs(ret, which):
    both, alone = ret
    experts, _, size, width = both.shape
    spot = lambda *_: (0, which, 0, 0)
    return [
        pl.BlockSpec((experts, None, size, width), spot, pipeline_mode=pl.Buffered(1)),
        whole(alone.shape),
    ]


def lane_iota(rows, width):
    return lax.broadcasted_iota(jnp.int32, (rows, width), 1)


def norm_stats(values):
    row_mean = jnp.mean(values, axis=-1, keepdims=True)
    offsets = values - row_mean
    spread = jnp.mean(offsets * offsets, axis=-1, keepdims=True)
    scale = lax.rsqrt(spread + EPSILON)
    return offsets * scale, scale


def norm_back(grad, unit, scale, gain):
    weighted = grad * gain
    first = jnp.mean(weighted, axis=-1, keepdims=True)
    second = jnp.mean(weighted * unit, axis=-1, keepdims=True)
    return scale * (weighted - first - unit * second)


EXTRA = 16


def pack_kernel(wqkv, wout, router, ga, sa, gm, sm, w_in, w_out, b_in, b_out, dense, *refs):
    *pieces, tail = refs
    width = wout.shape[1]
    experts = router.shape[0]
    share = wout.shape[0]
    hidden = w_in.shape[0]
    dense[:, : 3 * width] = wqkv[...]
    dense[:, 3 * width : 4 * width] = wout[...]
    tail[...] = jnp.zeros_like(tail)
    tail[0:experts, 0:share] = router[...].astype(F32)
    for k, row in enumerate((ga, sa, gm, sm)):
        tail[experts + k : experts + k + 1, 0:share] = row[...].astype(F32)
    columns = jnp.transpose(tail[0:LANES, 0:LANES])[:share, :]
    dense[:, 4 * width :] = columns.astype(BF16)
    sources = ((w_in, 0), (w_out, hidden))
    start = 0
    for piece in pieces:
        stop = start + piece.shape[0]
        for source, base in sources:
            low, high = max(start, base), min(stop, base + hidden)
            if low < high:
                piece[low - start : high - start, :] = source[low - base : high - base, :]
        start = stop
    tail[0:EXTRA, :] = jnp.zeros((EXTRA, width), F32)
    tail[0:1, 0:hidden] = b_in[...].astype(F32)
    tail[1:2, 0:share] = b_out[...].astype(F32)
    pieces[-1][pieces[-1].shape[0] - EXTRA :, :] = tail[0:EXTRA, :].astype(BF16)


def pack(wqkv, wout, router, gains, w_in, w_out, b_in, b_out):
    share, width = wout.shape
    hidden = w_in.shape[0]
    double = 2 * hidden + EXTRA
    cuts = [0] + [double * part // 100 // EXTRA * EXTRA for part in (50,)] + [double]
    sizes = [high - low for low, high in zip(cuts, cuts[1:])]
    return pl.pallas_call(
        pack_kernel,
        out_shape=[
            jax.ShapeDtypeStruct((share, 4 * width + LANES), BF16),
            *[jax.ShapeDtypeStruct((n, width), BF16) for n in sizes],
        ],
        scratch_shapes=[pltpu.VMEM((LANES, width), F32)],
        compiler_params=params(),
        name="pack",
        cost_estimate=cost(3),
    )(wqkv, wout, router, *[g[None, :] for g in gains], w_in, w_out, b_in, b_out)


def slots_kernel(parts, block, prow, routes, capacity, out, out_rows, poscol, hot, limits, wide):
    total = routes.shape[1]
    experts = capacity.shape[1]
    steps = total // block
    half = LANES // 2
    sub = lax.broadcasted_iota(jnp.int32, (LANES, 1), 0)
    hot_t = jnp.where((routes[0:1, :] == sub) | (routes[1:2, :] + half == sub), 1.0, 0.0)
    hot[...] = jnp.transpose(hot_t).astype(BF16)
    limits[...] = jnp.zeros_like(limits)
    limits[:, 0:experts] = capacity[...].astype(F32)
    limits[:, half : half + experts] = capacity[...].astype(F32)
    lane = lane_iota(1, LANES)
    index = lax.broadcasted_iota(jnp.int32, (total, LANES), 0)
    digits = jnp.where(
        lane_iota(total, LANES) == 0, index // 8, jnp.where(lane_iota(total, LANES) == 1, index % 8, 0)
    ).astype(F32).astype(BF16)

    def find(i, carry):
        at = pl.ds(pl.multiple_of(i * block, block), block)
        token = lax.broadcasted_iota(jnp.int32, (block, 1), 0) + i * block
        hit = jnp.where(prow[...] == token, 1.0, 0.0).astype(BF16)
        poscol[at, :] = mm(hit, digits)
        return carry

    lax.fori_loop(0, steps, find, 0)
    turned = jnp.transpose(poscol[...])
    posrow = turned[0:1, :] * 8.0 + turned[1:2, :]
    low_lanes = lane < half
    seen = jnp.sum(hot[...].astype(F32), axis=0, keepdims=True)
    seen_b = jnp.where(low_lanes, 0.0, pltpu.roll(jnp.broadcast_to(seen, (8, LANES)), half, 1)[0:1, :])
    expert = jnp.where(low_lanes, lane, lane - half)
    front, rest = parts
    base = (expert * front + 1).astype(F32)
    base_b = (experts * front + expert * rest - front + 1).astype(F32)

    def step(i, carry):
        at = pl.ds(pl.multiple_of(i * block, block), block)
        mine = poscol[at, 0:1] * 8.0 + poscol[at, 1:2]
        earlier = jnp.where(posrow < mine, 1.0, 0.0).astype(BF16)
        own = hot[at, :].astype(F32)
        place = mm(earlier, hot[...]) + seen_b
        number = place + jnp.where(place < front, base, base_b)
        value = jnp.where(place < limits[...], number, 0.0) * own
        slot_a = jnp.sum(jnp.where(low_lanes, value, 0.0), axis=1, keepdims=True) - 1.0
        slot_b = jnp.sum(jnp.where(low_lanes, 0.0, value), axis=1, keepdims=True) - 1.0
        wide[at, :] = jnp.where(lane == 0, slot_a, slot_b)
        out[at, :] = jnp.where(lane_iota(1, 2) == 0, slot_a, slot_b).astype(jnp.int32)
        return carry

    lax.fori_loop(0, steps, step, 0)
    out_rows[...] = jnp.transpose(wide[...])[0:2, :].astype(jnp.int32)


def make_slots(route_rows, priority, capacity, parts):
    total = route_rows.shape[1]
    return pl.pallas_call(
        partial(slots_kernel, parts, 400),
        out_shape=[
            jax.ShapeDtypeStruct((total, 2), jnp.int32),
            jax.ShapeDtypeStruct((2, total), jnp.int32),
        ],
        scratch_shapes=[
            pltpu.VMEM((total, LANES), F32),
            pltpu.VMEM((total, LANES), BF16),
            pltpu.VMEM((1, LANES), F32),
            pltpu.VMEM((total, LANES), F32),
        ],
        compiler_params=params(),
        name="slots",
        cost_estimate=cost(8),
    )(priority, route_rows, capacity[None, :])


def dispatch_kernel(pieces, with_other, has_carry, slot_rows, route_rows, rows, *outs):
    e = pl.program_id(0)
    if has_carry:
        carry, *outs = outs
        outs[-1][0, pieces[-1][1] :, :] = carry[0]
    for (start, size), out in zip(pieces, outs):
        place = lax.broadcasted_iota(jnp.int32, (size, 1), 0) + (start + e * size)
        hit_a = slot_rows[0:1, :] == place
        hit_b = slot_rows[1:2, :] == place
        pick = jnp.where(hit_a | hit_b, 1.0, 0.0).astype(BF16)
        out[0, 0:size, :] = mm(pick, rows[...]).astype(BF16)
        if with_other:
            named = route_rows[...].astype(F32) + 1.0
            found = jnp.where(hit_a, named[1:2, :], jnp.where(hit_b, named[0:1, :], 0.0))
            column = jnp.sum(found, axis=1, keepdims=True) - 1.0
            turned = jnp.transpose(jnp.broadcast_to(column, (size, LANES)))
            out[0, size : size + EXTRA, 0:size] = turned[0:EXTRA, :].astype(BF16)


def dispatch(slot_rows, route_rows, rows, experts, pieces, with_other, carry=None):
    total, width = rows.shape
    tall = [size + (EXTRA if with_other else 0) for _, size in pieces]
    extra, extra_spec = (), ()
    if carry is not None:
        tall[-1] += carry.shape[1]
        extra = (carry,)
        extra_spec = (pl.BlockSpec((1,) + carry.shape[1:], lambda e: (e, 0, 0)),)
    return pl.pallas_call(
        partial(dispatch_kernel, pieces, with_other, carry is not None),
        grid=(experts,),
        in_specs=[whole((2, total)), whole((2, total)), whole((total, width)), *extra_spec],
        out_specs=[pl.BlockSpec((1, t, width), lambda e: (e, 0, 0)) for t in tall],
        out_shape=[jax.ShapeDtypeStruct((experts, t, width), BF16) for t in tall],
        compiler_params=params(1),
        name="dispatch",
        cost_estimate=cost(10),
    )(slot_rows, route_rows, rows, *extra)


def stack_rows(length, width):
    return LANES * HEADS // width * ((length + 15) // 16 * 16)


def attention_kernel(
    experts, x, mask, small, wqkv, wout, triple, context, logs, residual, normed, gains
):
    @pl.when(pl.program_id(0) == 0)
    def _():
        gains[0:4, :] = gain_rows(small, experts)

    width = x.shape[1]
    length = x.shape[0]
    x_wide = x[...].astype(F32)
    unit, _ = norm_stats(x_wide)
    low = (unit * gains[0:1, :] + gains[1:2, :]).astype(BF16)
    mixed = mm(low, wqkv[...]).astype(BF16)
    triple[...] = mixed
    bias = jnp.where(mask[0] > 0, 0.0, NEGATIVE)
    lane = lane_iota(1, LANES)
    head_width = width // HEADS
    scale = head_width ** (-0.5)
    per = LANES // head_width
    gathered = jnp.zeros((length, LANES), F32)
    lanes_all = lane_iota(length, LANES)
    for group in range(HEADS // per):
        begin = group * LANES
        queries = mixed[:, begin : begin + LANES]
        keys = mixed[:, width + begin : width + begin + LANES]
        values = mixed[:, 2 * width + begin : 2 * width + begin + LANES]
        merged = jnp.zeros((length, LANES), F32)
        for inner in range(per):
            inside = (lane >= inner * head_width) & (lane < (inner + 1) * head_width)
            chosen = queries * jnp.where(inside, scale, 0.0).astype(BF16)
            scores = mm_nt(chosen, keys) + bias
            peak = jnp.max(scores, axis=-1, keepdims=True)
            raised = jnp.exp(scores - peak)
            sums = jnp.sum(raised, axis=-1, keepdims=True)
            found = mm(raised.astype(BF16), values) * (1.0 / sums)
            merged = jnp.where(inside, found, merged)
            gathered = jnp.where(
                lanes_all == group * per + inner, peak + jnp.log(sums), gathered
            )
        context[:, begin : begin + LANES] = merged.astype(BF16)
    logs[0] = jnp.transpose(gathered)[:HEADS, :]
    after = x_wide + mm(context[...], wout[...])
    residual[...] = after
    unit_b, _ = norm_stats(after)
    normed[...] = (unit_b * gains[2:3, :] + gains[3:4, :]).astype(BF16)


def small_spec(width):
    last = 4 * width // LANES
    return pl.BlockSpec((width, LANES), lambda i: (0, last), pipeline_mode=pl.Buffered(1))


def attention_forward(x, mask, dense, experts):
    total, width = x.shape
    images, length = mask.shape
    rows = lambda i: (i, 0)
    return pl.pallas_call(
        partial(attention_kernel, experts),
        grid=(images,),
        in_specs=[
            pl.BlockSpec((length, width), rows),
            pl.BlockSpec((1, 1, length), lambda i: (i, 0, 0)),
            small_spec(width),
            pl.BlockSpec((width, 3 * width), lambda i: (0, 0), pipeline_mode=pl.Buffered(1)),
            pl.BlockSpec((width, width), lambda i: (0, 3), pipeline_mode=pl.Buffered(1)),
        ],
        out_specs=[
            pl.BlockSpec((length, 3 * width), rows),
            pl.BlockSpec((length, width), rows),
            pl.BlockSpec((1, HEADS, length), lambda i: (i, 0, 0)),
            pl.BlockSpec((length, width), rows),
            pl.BlockSpec((length, width), rows),
        ],
        out_shape=[
            jax.ShapeDtypeStruct((total, 3 * width), BF16),
            jax.ShapeDtypeStruct((total, width), BF16),
            jax.ShapeDtypeStruct((images, HEADS, length), F32),
            jax.ShapeDtypeStruct((total, width), F32),
            jax.ShapeDtypeStruct((total, width), BF16),
        ],
        scratch_shapes=[pltpu.VMEM((8, width), F32)],
        compiler_params=params(1),
        name="attention_forward",
        cost_estimate=cost(17),
    )(x, mask.reshape(images, 1, length), dense, dense, dense)


def experts_kernel(block, more, *refs):
    if more:
        mixed, own, router, w_in, w_out, b_in, b_out, *rest = refs
        old_mine, old_mate, old_router, back, sent, dw_mine, dw_mate, drouter, *rest = rest
        *rest, rows = rest
        ups, shift = mixed, block

        @pl.when(pl.program_id(0) == 0)
        def _():
            for i in range(mixed.shape[0]):
                rows[i * block : (i + 1) * block, :] = mixed[i, 0:block, :]

        outs = (back, sent, 0)
        old = (old_mine, old_mate, old_router)
    else:
        rows, ups, own, router, w_in, w_out, b_in, b_out, *rest = refs
        ret, dw_mine, dw_mate, drouter, *rest = rest
        outs = (ret, ret, block)
        shift, old = 0, None
    experts_body(
        block, rows, ups, shift, own, router, w_in, w_out, b_in, b_out, old,
        outs, dw_mine, dw_mate, drouter, *rest,
    )


def experts_body(
    block, rows, ups, shift, own, router, w_in, w_out, b_in, b_out, old,
    outs, dw_mine, dw_mate, drouter,
    gate, weighted, made, pushed, hid, pre_g, other, db,
):
    f = pl.program_id(0)
    last = pl.num_programs(0) - 1
    total, width = rows.shape
    steps = total // block
    lane = lane_iota(1, LANES)

    @pl.when(f == 0)
    def _():
        own_hot = own[...] > 0.0

        def step(i, acc):
            at = pl.ds(pl.multiple_of(i * block, block), block)
            logits = mm(rows[at, :], router[...])
            mine = jnp.sum(jnp.where(own_hot, logits, 0.0), axis=1, keepdims=True)
            named = ups[i, shift + block : shift + block + EXTRA, 0:block].astype(F32)
            rival = jnp.transpose(named)[:, 0:1].astype(jnp.int32)
            other[at, :] = rival
            theirs = jnp.sum(jnp.where(lane == rival, logits, 0.0), axis=1, keepdims=True)
            share = 1.0 / (1.0 + jnp.exp(theirs - mine))
            gate[at, 0:1] = share
            gate[at, 1:2] = 1.0 / (1.0 + jnp.exp(mine - theirs))
            scaled = (share * ups[i, shift : shift + block, :].astype(F32)).astype(BF16)
            weighted[at, :] = scaled
            return acc + jnp.sum(scaled.astype(F32), axis=0, keepdims=True)

        db[...] = jnp.zeros_like(db)
        db[1:2, :] = lax.fori_loop(0, steps, step, jnp.zeros((1, width), F32), unroll=4)

    chunk = w_in.shape[1]
    hidden_share = (dw_mine.shape[1] - EXTRA) // 2
    per = hidden_share // chunk
    place = f % per
    biases = b_in[0, 0:1, :].astype(F32)
    bias = biases[:, 0:chunk]
    for k in range(1, per):
        bias = jnp.where(place == k, biases[:, k * chunk : (k + 1) * chunk], bias)

    big = total // BIG_STEPS

    def body(i, acc):
        at = pl.ds(pl.multiple_of(i * big, big), big)
        here = rows[at, :]
        u = mm_nt(here, w_in[0]) + bias
        inner = ROOT + (ROOT * CUBIC) * (u * u)
        share = 0.5 + 0.5 * jnp.tanh(u * inner)
        raised = u * share
        hidden = raised.astype(BF16)
        slope = share + raised * (1.0 - share) * (6.0 * inner - 4.0 * ROOT)
        hid[at, :] = hidden
        grad = mm_nt(weighted[at, :], w_out[0]) * slope
        low = grad.astype(BF16)
        pre_g[at, :] = low
        part = mm(hidden, w_out[0])
        part_b = mm(low, w_in[0])

        @pl.when(f == 0)
        def _():
            made[at, :] = part
            pushed[at, :] = part_b

        @pl.when(f > 0)
        def _():
            made[at, :] += part
            pushed[at, :] += part_b

        return acc + jnp.sum(grad, axis=0, keepdims=True)

    db_here = lax.fori_loop(0, BIG_STEPS, body, jnp.zeros((1, chunk), F32))
    for k in range(per):

        @pl.when(place == k)
        def _():
            db[0:1, k * chunk : (k + 1) * chunk] = db_here

    dw_out_here = mm_tn(hid[...], weighted[...])
    dw_in_here = mm_tn(pre_g[...], rows[...])

    def put(target, prior):
        spots = (
            (pl.ds(pl.multiple_of(place * chunk, chunk), chunk), dw_in_here),
            (pl.ds(pl.multiple_of(hidden_share + place * chunk, chunk), chunk), dw_out_here),
            (pl.ds(2 * hidden_share, EXTRA), db[...]),
        )
        for spot, value in spots:
            if prior is not None:
                value = value + prior[0, spot, :].astype(F32)
            target[0, spot, :] = value.astype(BF16)

    quarters = (last + 1) // per

    @pl.when(f // per < quarters // 2)
    def _():
        put(dw_mine, old and old[0])

    @pl.when(f // per >= quarters // 2)
    def _():
        put(dw_mate, old and old[1])

    @pl.when(f == last)
    def _():
        own_row = own[...]
        back, sent, after = outs

        def step(i, carry):
            at = pl.ds(pl.multiple_of(i * block, block), block)
            produced = (made[at, :] + b_out[...]).astype(BF16).astype(F32)
            share = gate[at, 0:1]
            sent[i, after : after + block, :] = (share * produced).astype(BF16)
            inner = jnp.sum(produced * ups[i, shift : shift + block, :].astype(F32), axis=1, keepdims=True)
            pull = share * gate[at, 1:2] * inner
            rival = other[at, :]
            spread = (pull * (own_row - jnp.where(lane == rival, 1.0, 0.0))).astype(BF16)
            back[i, 0:block, :] = (pushed[at, :] + mm_nt(spread, router[...])).astype(BF16)
            hid[at, 0:LANES] = spread
            return carry

        lax.fori_loop(0, steps, step, 0, unroll=4)
        drouter[...] = mm_tn(rows[...], hid[:, 0:LANES]) + (0.0 if old is None else old[2][...])


def run_experts(given, block, own, dense, weights, b_out, old):
    experts, _, width = given[0].shape
    total = experts * block
    quarters, double, _ = weights.shape
    share = (double - EXTRA) // 2
    chunk = min(share, 512)
    per = share // chunk
    half = quarters // 2
    at = lambda f: (f // per, f % per, 0)
    out_at = lambda f: (f // per, per + f % per, 0)
    bias_at = lambda f: (f // per, 2 * share // EXTRA, 0)
    mine_at = lambda f: (jnp.minimum(f // per, half - 1), 0, 0)
    mate_at = lambda f: (jnp.maximum(f // per - half, 0), 0, 0)
    steps = quarters * per
    dw_shape = jax.ShapeDtypeStruct((half, double, width), BF16)
    sums = [
        pl.BlockSpec((1, double, width), mine_at),
        pl.BlockSpec((1, double, width), mate_at),
        whole((width, LANES)),
    ]
    if old:
        given_specs = [whole(given[0].shape)]
        ret_shapes = [(experts, block, width)] * 2
        more_scratch = [pltpu.VMEM((total, width), BF16)]
    else:
        given = (given[0].reshape(total, width), given[1])
        given_specs = [whole(given[0].shape), whole(given[1].shape)]
        ret_shapes = [(experts, 2 * block, width)]
        more_scratch = []
    return pl.pallas_call(
        partial(experts_kernel, block, bool(old)),
        grid=(steps,),
        in_specs=given_specs
        + [
            whole((1, LANES)),
            small_spec(width),
            pl.BlockSpec((1, chunk, width), at),
            pl.BlockSpec((1, chunk, width), out_at),
            pl.BlockSpec((1, EXTRA, width), bias_at),
            whole((1, width)),
        ]
        + (sums if old else []),
        out_specs=[whole(r) for r in ret_shapes] + sums,
        out_shape=[jax.ShapeDtypeStruct(r, BF16) for r in ret_shapes]
        + [dw_shape, dw_shape, jax.ShapeDtypeStruct((width, LANES), F32)],
        scratch_shapes=[
            pltpu.VMEM((total, 2), F32),
            pltpu.VMEM((total, width), BF16),
            pltpu.VMEM((total, width), F32),
            pltpu.VMEM((total, width), F32),
            pltpu.VMEM((total, chunk), BF16),
            pltpu.VMEM((total, chunk), BF16),
            pltpu.VMEM((total, 1), jnp.int32),
            pltpu.VMEM((EXTRA, width), F32),
        ]
        + more_scratch,
        compiler_params=params(1),
        name="experts",
        cost_estimate=cost(50),
    )(*given, own, dense, weights, weights, weights, b_out, *old)


def backward_kernel(
    experts, x, mask, small, wqkv, wout, triple, context, logs, residual, up, slot, ret_a, ret_b, drouter,
    input_grad, packed,
    tg, gains, dqkv, dwout, dgains, stack_k, stack_v, dq_t,
):
    step = pl.program_id(0)
    length, width = x.shape

    @pl.when(step == 0)
    def _():
        dqkv[...] = jnp.zeros_like(dqkv)
        dwout[...] = jnp.zeros_like(dwout)
        dgains[...] = jnp.zeros_like(dgains)
        gains[0:4, :] = gain_rows(small, experts)
        stack_k[...] = jnp.zeros_like(stack_k)
        stack_v[...] = jnp.zeros_like(stack_v)

    second_grad = gather_slots(slot, (ret_a, ret_b))
    unit_b, scale_b = norm_stats(residual[...])
    dgains[experts + 2 : experts + 3, :] += jnp.sum(second_grad * unit_b, axis=0, keepdims=True)
    dgains[experts + 3 : experts + 4, :] += jnp.sum(second_grad, axis=0, keepdims=True)
    residual_grad = up[...].astype(F32) + norm_back(second_grad, unit_b, scale_b, gains[2:3, :])
    residual_low = residual_grad.astype(BF16)
    dwout[...] += mm_tn(context[...], residual_low)
    context_grad = mm_nt(residual_low, wout[...]).astype(BF16)

    lane = lane_iota(1, LANES)
    head_width = width // HEADS
    scale = head_width ** (-0.5)
    per = LANES // head_width
    tall = stack_k.shape[0] // per
    hide_row = jnp.where(mask[0] > 0, 0.0, NEGATIVE)
    hide = jnp.transpose(jnp.broadcast_to(hide_row, (LANES, length)))[:, 0:1]
    hide = jnp.concatenate([hide, jnp.full((tall - length, 1), NEGATIVE, F32)], axis=0)
    for group in range(HEADS // per):
        begin = group * LANES
        queries = triple[:, begin : begin + LANES] * jnp.asarray(scale, BF16)
        keys = triple[:, width + begin : width + begin + LANES]
        values = triple[:, 2 * width + begin : 2 * width + begin + LANES]
        pulled = context_grad[:, begin : begin + LANES]
        for inner in range(per):
            inside = (lane >= inner * head_width) & (lane < (inner + 1) * head_width)
            only = jnp.where(inside, 1.0, 0.0).astype(BF16)
            stack_k[inner * tall : inner * tall + length, :] = keys * only
            stack_v[inner * tall : inner * tall + length, :] = values * only
        scores = mm_nt(stack_k[...], queries)
        prob_grad = mm_nt(stack_v[...], pulled)
        probs, score_grad = [], []
        for inner in range(per):
            rows = slice(inner * tall, (inner + 1) * tall)
            head = group * per + inner
            prob = jnp.exp(scores[rows, :] + (hide - logs[0, head : head + 1, :]))
            pull = prob_grad[rows, :]
            inner_sum = jnp.sum(prob * pull, axis=0, keepdims=True)
            probs.append(prob.astype(BF16))
            score_grad.append((prob * (pull - inner_sum)).astype(BF16))
        probs = jnp.concatenate(probs, axis=0)
        score_grad = jnp.concatenate(score_grad, axis=0)
        dk_all = mm(score_grad, queries)
        dv_all = mm(probs, pulled)
        dq_t[begin : begin + LANES, :] = mm(jnp.transpose(stack_k[...]), score_grad) * scale
        dk, dv = dk_all[0:length, :], dv_all[0:length, :]
        for inner in range(1, per):
            rows = slice(inner * tall, inner * tall + length)
            dk = jnp.where(lane >= inner * head_width, dk_all[rows, :], dk)
            dv = jnp.where(lane >= inner * head_width, dv_all[rows, :], dv)
        tg[:, width + begin : width + begin + LANES] = dk.astype(BF16)
        tg[:, 2 * width + begin : 2 * width + begin + LANES] = dv.astype(BF16)
    tg[:, 0:width] = jnp.transpose(dq_t[...]).astype(BF16)
    unit, scale_a = norm_stats(x[...].astype(F32))
    low = (unit * gains[0:1, :] + gains[1:2, :]).astype(BF16)
    dqkv[...] += mm_tn(low, tg[...])
    first_grad = mm_nt(tg[...], wqkv[...])
    dgains[experts + 0 : experts + 1, :] += jnp.sum(first_grad * unit, axis=0, keepdims=True)
    dgains[experts + 1 : experts + 2, :] += jnp.sum(first_grad, axis=0, keepdims=True)
    input_grad[...] = residual_grad + norm_back(first_grad, unit, scale_a, gains[0:1, :])

    @pl.when(step == pl.num_programs(0) - 1)
    def _():
        packed[:, : 3 * width] = dqkv[...].astype(BF16)
        packed[:, 3 * width : 4 * width] = dwout[...].astype(BF16)
        packed[:, 4 * width :] = (drouter[...] + jnp.transpose(dgains[...])).astype(BF16)


def attention_backward(
    x, mask, dense, triple, context, logs, residual, up, slot, ret, drouter, experts
):
    total, width = x.shape
    images, length = mask.shape
    rows = lambda i: (i, 0)
    return pl.pallas_call(
        partial(backward_kernel, experts),
        grid=(images,),
        in_specs=[
            pl.BlockSpec((length, width), rows),
            pl.BlockSpec((1, 1, length), lambda i: (i, 0, 0)),
            small_spec(width),
            pl.BlockSpec((width, 3 * width), lambda i: (0, 0), pipeline_mode=pl.Buffered(1)),
            pl.BlockSpec((width, width), lambda i: (0, 3), pipeline_mode=pl.Buffered(1)),
            pl.BlockSpec((length, 3 * width), rows),
            pl.BlockSpec((length, width), rows),
            pl.BlockSpec((1, HEADS, length), lambda i: (i, 0, 0)),
            pl.BlockSpec((length, width), rows),
            pl.BlockSpec((length, width), rows),
            pl.BlockSpec((length, 2), rows),
            *returned_specs(ret, 0),
            whole((width, LANES)),
        ],
        out_specs=[
            pl.BlockSpec((length, width), rows),
            whole((width, 4 * width + LANES)),
        ],
        out_shape=[
            jax.ShapeDtypeStruct((total, width), F32),
            jax.ShapeDtypeStruct((width, 4 * width + LANES), BF16),
        ],
        scratch_shapes=[
            pltpu.VMEM((length, 3 * width), BF16),
            pltpu.VMEM((8, width), F32),
            pltpu.VMEM((width, 3 * width), F32),
            pltpu.VMEM((width, width), F32),
            pltpu.VMEM((LANES, width), F32),
            pltpu.VMEM((stack_rows(length, width), LANES), BF16),
            pltpu.VMEM((stack_rows(length, width), LANES), BF16),
            pltpu.VMEM((width, length), F32),
        ],
        compiler_params=params(1),
        name="attention_backward",
        cost_estimate=cost(50),
    )(
        x, mask.reshape(images, 1, length), dense, dense, dense, triple, context, logs, residual,
        up, slot, *ret, drouter,
    )


def combine_kernel(slot, residual, ret_a, ret_b, out):
    out[...] = (residual[...] + gather_slots(slot, (ret_a, ret_b))).astype(BF16)


def combine(slot, residual, ret, block):
    total, width = residual.shape
    rows = lambda i: (i, 0)
    return pl.pallas_call(
        combine_kernel,
        grid=(total // block,),
        in_specs=[
            pl.BlockSpec((block, 2), rows),
            pl.BlockSpec((block, width), rows),
            *returned_specs(ret, 1),
        ],
        out_specs=pl.BlockSpec((block, width), rows),
        out_shape=jax.ShapeDtypeStruct((total, width), BF16),
        compiler_params=params(1),
        name="combine",
        cost_estimate=cost(10),
    )(slot, residual, *ret)


class PlainPlan:
    def __init__(self, seq, wt):
        self.seq, self.wt = seq, wt

    def own_id(self):
        return lax.axis_index("seq")

    def exchange(self, a):
        return lax.all_to_all(a, "seq", split_axis=0, concat_axis=0, tiled=True)

    def begin_dense(self, packed):
        return packed

    def gather_dense(self, packed, begun):
        return lax.all_gather(begun, "wt", axis=0, tiled=True)

    def begin_fetch(self, packed):
        return (packed,)

    def fetch(self, packed, begun):
        return lax.all_gather(begun[0], "wt", axis=0)

    def spread_out_bias(self, quarters):
        return quarters

    def begin_reduce(self, mine, mate):
        return (jnp.concatenate([mine, mate]).reshape(-1, mine.shape[-1]),)

    def reduce_expert(self, parts):
        (parts,) = parts
        return lax.psum_scatter(parts, "wt", scatter_dimension=0, tiled=True)

    def finish_expert(self, parts, received):
        return received.astype(F32)

    def begin_dense_sum(self, grads):
        return lax.psum_scatter(grads, "wt", scatter_dimension=0, tiled=True)

    def reduce_dense(self, part):
        return lax.psum(part, "seq").astype(F32)


class CubePlan:
    AXES = ("seq", "wt")

    def __init__(self, seq, wt):
        self.seq, self.wt = seq, wt
        self.levels = seq // 2
        places = [
            (z, y, x, c)
            for z in range(self.levels)
            for y in range(2)
            for x in range(2)
            for c in range(2)
        ]
        flat = self.flat
        self.cross = [(flat(*p), flat(p[0], p[1], 1 - p[2], p[3])) for p in places]
        self.core = [(flat(*p), flat(p[0], p[1], p[2], 1 - p[3])) for p in places]
        near = lambda p: p[2] == p[0] % 2
        away = lambda p: (p[0] ^ 2, p[1], 1 - p[0] % 2, p[3])
        home = lambda p: (p[0], p[1], p[0] % 2, p[3])
        self.first = [(flat(*p), flat(*(away(p) if near(p) else home(p)))) for p in places]
        self.second = [(flat(*p), flat(*away(p))) for p in places if not near(p)]
        self.groups = [
            [self.host(half, e, c) for e in range(seq)] for half in range(2) for c in range(2)
        ]

    def flat(self, z, y, x, c):
        return (z * 2 + y) * self.wt + x * 2 + c

    def host(self, half, expert, c):
        z, y = expert // 2, expert % 2
        if z // 2 == half:
            return self.flat(z, y, z % 2, c)
        return self.flat(z ^ 2, y, 1 - z % 2, c)

    def send(self, a, pairs):
        return lax.ppermute(a, self.AXES, pairs)

    def x_zero(self):
        return lax.axis_index("wt") < 2

    def odd_level(self):
        return lax.axis_index("seq") // 2 % 2 == 1

    def near(self):
        return self.x_zero() != self.odd_level()

    def core_zero(self):
        return lax.axis_index("wt") % 2 == 0

    def own_id(self):
        rank = lax.axis_index("seq")
        return jnp.where(self.near(), rank, rank ^ 4)

    def exchange(self, a):
        return lax.all_to_all(
            a, self.AXES, split_axis=0, concat_axis=0, axis_index_groups=self.groups, tiled=True
        )

    def begin_dense(self, packed):
        return self.send(packed, self.cross)

    def gather_dense(self, packed, far):
        mate = self.send(packed, self.core)
        far_mate = self.send(far, self.core)
        flip = self.x_zero()
        low, high = jnp.where(flip, packed, far), jnp.where(flip, far, packed)
        low_mate, high_mate = jnp.where(flip, mate, far_mate), jnp.where(flip, far_mate, mate)
        first = self.core_zero()
        return jnp.concatenate(
            [
                jnp.where(first, low, low_mate),
                jnp.where(first, low_mate, low),
                jnp.where(first, high, high_mate),
                jnp.where(first, high_mate, high),
            ],
            axis=0,
        )

    def begin_fetch(self, packed):
        return self.send(packed, self.first), self.send(packed, self.second)

    def fetch(self, packed, begun):
        got, got_b = begun
        flip = self.near()
        low = jnp.where(flip, packed, got)
        high = jnp.where(flip, got, got_b)
        return jnp.stack([low, high, self.send(low, self.core), self.send(high, self.core)])

    def spread_out_bias(self, quarters):
        mine, odd = self.core_zero(), self.odd_level()
        order = []
        for x in range(2):
            for c in range(2):
                same = mine == (c == 0)
                level = odd == (x == 1)
                order.append(
                    jnp.where(
                        same,
                        jnp.where(level, quarters[0], quarters[1]),
                        jnp.where(level, quarters[2], quarters[3]),
                    )
                )
        return jnp.stack(order)

    def begin_reduce(self, mine, mate):
        got = self.send(mate, self.core)
        low = (mine[0].astype(F32) + got[0].astype(F32)).astype(BF16)
        high = (mine[1].astype(F32) + got[1].astype(F32)).astype(BF16)
        return low, high, jnp.where(self.near(), high, low)

    def reduce_expert(self, parts):
        low, high, give = parts
        return self.send(give, self.first_back()), self.send(high, self.second)

    def finish_expert(self, parts, received):
        far, far_b = received
        return jnp.where(self.near(), parts[0], far_b).astype(F32) + far.astype(F32)

    def first_back(self):
        return [(b, a) for a, b in self.first]

    def begin_dense_sum(self, grads):
        share = grads.shape[0] // 4
        width = grads.shape[1]
        parts = [grads[i * share : (i + 1) * share] for i in range(4)]
        first = self.core_zero()
        keep = [jnp.where(first, parts[0], parts[1]), jnp.where(first, parts[2], parts[3])]
        give = [jnp.where(first, parts[1], parts[0]), jnp.where(first, parts[3], parts[2])]
        got = [self.send(v.astype(BF16), self.core).astype(F32) for v in give]
        low, high = keep[0].astype(F32) + got[0], keep[1].astype(F32) + got[1]
        flip = self.x_zero()
        out = self.send(jnp.where(flip, high, low).astype(BF16), self.cross)
        mine = jnp.where(flip, low, high) + out.astype(F32)
        return mine.astype(BF16)

    def reduce_dense(self, mine):
        share, width = mine.shape
        pieces = mine.reshape(self.seq, share // self.seq, width)
        swap = lambda v: lax.all_to_all(v, "seq", split_axis=0, concat_axis=0, tiled=True)
        total = jnp.sum(swap(pieces).astype(F32), axis=0, keepdims=True).astype(BF16)
        spread = swap(jnp.broadcast_to(total, pieces.shape))
        return spread.reshape(share, width).astype(F32)


def plan_of(seq, wt):
    return CubePlan(seq, wt) if (seq, wt) == (8, 4) else PlainPlan(seq, wt)


def local(
    inputs,
    key_mask,
    routes,
    priority,
    capacity,
    attention_gain,
    attention_shift,
    query_key_value,
    attention_out,
    mixture_gain,
    mixture_shift,
    router_weight,
    expert_in,
    expert_in_bias,
    expert_out,
    expert_out_bias,
    cotangent,
):
    total, width = inputs.shape
    experts = capacity.shape[0]
    cap = 8 * max(1, total // (4 * experts))
    share = query_key_value.shape[0]
    hidden_share = expert_in.shape[1]
    plan = plan_of(lax.axis_size("seq"), lax.axis_size("wt"))

    tie = lax.optimization_barrier
    front = (cap // 2 + EXTRA - 1) // EXTRA * EXTRA
    parts = (front, cap - front)
    packed, *shards = pack(
        query_key_value, attention_out, router_weight.T,
        (attention_gain, attention_shift, mixture_gain, mixture_shift),
        expert_in[0], expert_out[0], expert_in_bias, expert_out_bias,
    )
    fetched = [plan.begin_fetch(shard) for shard in shards]
    far = plan.begin_dense(packed)
    own = (jnp.arange(LANES) == plan.own_id()).astype(F32)[None, :]
    route_rows = routes.T
    slot, slot_rows = make_slots(route_rows, priority, capacity, parts)
    slot_rows, far = tie((slot_rows, far))
    pieces = ((0, front), (experts * front, cap - front))
    send = partial(dispatch, slot_rows, route_rows)
    ups_a, ups_b = send(cotangent, experts, pieces, True)
    dense = plan.gather_dense(packed, far)
    dense, ups_a, fetched[0] = tie((dense, ups_a, fetched[0]))
    ups_a = plan.exchange(ups_a)

    triple, context, logs, residual, normed = attention_forward(inputs, key_mask, dense, experts)
    (rows_a,) = send(normed, experts, pieces[:1], False)
    (mixed_b,) = send(normed, experts, pieces[1:], False, ups_b)
    rows_a, ups_a, fetched[1] = tie((rows_a, ups_a, fetched[1]))
    rows_a = plan.exchange(rows_a)
    weights = jnp.concatenate(
        [plan.fetch(*pair) for pair in zip(shards, fetched)], axis=1
    )
    b_out = plan.spread_out_bias(
        weights[:, 2 * hidden_share + 1, :share].astype(F32)
    ).reshape(1, width)
    rows_a, mixed_b, weights, b_out = tie((rows_a, mixed_b, weights, b_out))
    mixed_b = plan.exchange(mixed_b)
    ret_a, *sums = run_experts((rows_a, ups_a), parts[0], own, dense, weights, b_out, ())
    ret_a, mixed_b = tie((ret_a, mixed_b))
    ret_a = plan.exchange(ret_a)
    back_b, sent_b, *sums = run_experts(
        (mixed_b,), parts[1], own, dense, weights, b_out, tuple(sums)
    )
    back_b, ret_a = tie((back_b, ret_a))
    back_b = plan.exchange(back_b)
    halves = plan.begin_reduce(*sums[:2])
    back_b, sent_b, halves = tie((back_b, sent_b, halves))
    sent_b = plan.exchange(sent_b)
    received = plan.reduce_expert(halves)
    ret_a = ret_a.reshape(experts, 2, front, width)
    input_grad, grads = attention_backward(
        inputs, key_mask, dense, triple, context, logs, residual, cotangent, slot,
        (ret_a, back_b), sums[2], experts,
    )
    grads, received = tie((grads, received))
    mine = plan.begin_dense_sum(grads)
    mine, sent_b = tie((mine, sent_b))
    shard = plan.finish_expert(halves, received)
    done = plan.reduce_dense(mine)
    block_output = combine(slot, residual, (ret_a, sent_b), 400)
    base = 4 * width
    rank = lax.axis_index("wt")
    return (
        block_output,
        input_grad,
        done[:, base + experts],
        done[:, base + experts + 1],
        done[:, : 3 * width],
        done[:, 3 * width : base],
        done[:, base + experts + 2],
        done[:, base + experts + 3],
        done[:, base : base + experts],
        shard[None, :hidden_share],
        shard[2 * hidden_share, :hidden_share][None],
        shard[None, hidden_share : 2 * hidden_share],
        lax.dynamic_slice(shard[2 * hidden_share + 1], (rank * share,), (share,))[None],
    )


def solution(mesh):
    both = P(("seq", "wt"), None)
    placed = (
        both,
        both,
        both,
        both,
        P(),
        P("wt"),
        P("wt"),
        P("wt", None),
        P("wt", None),
        P("wt"),
        P("wt"),
        P("wt", None),
        P("seq", "wt", None),
        P("seq", "wt"),
        P("seq", "wt", None),
        P("seq", "wt"),
        both,
    )
    return jax.shard_map(
        local,
        mesh=mesh,
        in_specs=placed,
        out_specs=(
            both,
            both,
            P("wt"),
            P("wt"),
            P("wt", None),
            P("wt", None),
            P("wt"),
            P("wt"),
            P("wt", None),
            P("seq", "wt", None),
            P("seq", "wt"),
            P("seq", "wt", None),
            P("seq", "wt"),
        ),
        check_vma=False,
    )
```

```python
from functools import partial

import jax
import jax.numpy as jnp
from jax import lax
from jax.experimental import pallas as pl
from jax.experimental.pallas import tpu as pltpu
from jax.sharding import PartitionSpec as P

HEADS = 8
NEGATIVE = -1e30
EPSILON = 1e-06
LANES = 128
BIG_STEPS = 2
VMEM_BYTES = 60 * 1024 * 1024
F32 = jnp.float32
BF16 = jnp.bfloat16
ROOT = 0.7978845608028654
CUBIC = 0.044715

NT = (((1,), (1,)), ((), ()))
TN = (((0,), (0,)), ((), ()))


def mm(a, b):
    return jnp.dot(a, b, preferred_element_type=F32)


def mm_nt(a, b):
    return lax.dot_general(a, b, NT, preferred_element_type=F32)


def mm_tn(a, b):
    return lax.dot_general(a, b, TN, preferred_element_type=F32)


def params(steps=0):
    return pltpu.CompilerParams(
        dimension_semantics=("arbitrary",) * steps if steps else None,
        vmem_limit_bytes=VMEM_BYTES,
    )


def cost(micros):
    return pl.CostEstimate(
        flops=int(micros * 1.0e7), bytes_accessed=int(micros * 1.0e4), transcendentals=0
    )


def gain_rows(small, experts):
    turned = jnp.transpose(small[...].astype(F32))
    return turned[experts : experts + 4, :]


def whole(shape):
    zeros = (0,) * len(shape)
    return pl.BlockSpec(shape, lambda *_: zeros, pipeline_mode=pl.Buffered(1))


def gather_slots(slot, parts):
    found = None
    start = 0
    for piece in parts:
        rows = piece[...].reshape(-1, piece.shape[-1])
        lanes = lane_iota(1, rows.shape[0]) + start
        start += rows.shape[0]
        pick = jnp.where((lanes == slot[:, 0:1]) | (lanes == slot[:, 1:2]), 1.0, 0.0)
        piece = jnp.dot(pick.astype(BF16), rows, preferred_element_type=F32)
        found = piece if found is None else found + piece
    return found


def returned_specs(ret, which):
    both, alone = ret
    experts, _, size, width = both.shape
    spot = lambda *_: (0, which, 0, 0)
    return [
        pl.BlockSpec((experts, None, size, width), spot, pipeline_mode=pl.Buffered(1)),
        whole(alone.shape),
    ]


def lane_iota(rows, width):
    return lax.broadcasted_iota(jnp.int32, (rows, width), 1)


def norm_stats(values):
    row_mean = jnp.mean(values, axis=-1, keepdims=True)
    offsets = values - row_mean
    spread = jnp.mean(offsets * offsets, axis=-1, keepdims=True)
    scale = lax.rsqrt(spread + EPSILON)
    return offsets * scale, scale


def norm_back(grad, unit, scale, gain):
    weighted = grad * gain
    first = jnp.mean(weighted, axis=-1, keepdims=True)
    second = jnp.mean(weighted * unit, axis=-1, keepdims=True)
    return scale * (weighted - first - unit * second)


EXTRA = 16


def pack_kernel(wqkv, wout, router, ga, sa, gm, sm, w_in, w_out, b_in, b_out, dense, *refs):
    *pieces, tail = refs
    width = wout.shape[1]
    experts = router.shape[0]
    share = wout.shape[0]
    hidden = w_in.shape[0]
    dense[:, : 3 * width] = wqkv[...]
    dense[:, 3 * width : 4 * width] = wout[...]
    tail[...] = jnp.zeros_like(tail)
    tail[0:experts, 0:share] = router[...].astype(F32)
    for k, row in enumerate((ga, sa, gm, sm)):
        tail[experts + k : experts + k + 1, 0:share] = row[...].astype(F32)
    columns = jnp.transpose(tail[0:LANES, 0:LANES])[:share, :]
    dense[:, 4 * width :] = columns.astype(BF16)
    sources = ((w_in, 0), (w_out, hidden))
    start = 0
    for piece in pieces:
        stop = start + piece.shape[0]
        for source, base in sources:
            low, high = max(start, base), min(stop, base + hidden)
            if low < high:
                piece[low - start : high - start, :] = source[low - base : high - base, :]
        start = stop
    tail[0:EXTRA, :] = jnp.zeros((EXTRA, width), F32)
    tail[0:1, 0:hidden] = b_in[...].astype(F32)
    tail[1:2, 0:share] = b_out[...].astype(F32)
    pieces[-1][pieces[-1].shape[0] - EXTRA :, :] = tail[0:EXTRA, :].astype(BF16)


def pack(wqkv, wout, router, gains, w_in, w_out, b_in, b_out):
    share, width = wout.shape
    hidden = w_in.shape[0]
    double = 2 * hidden + EXTRA
    cuts = [0] + [double * part // 100 // EXTRA * EXTRA for part in (55,)] + [double]
    sizes = [high - low for low, high in zip(cuts, cuts[1:])]
    return pl.pallas_call(
        pack_kernel,
        out_shape=[
            jax.ShapeDtypeStruct((share, 4 * width + LANES), BF16),
            *[jax.ShapeDtypeStruct((n, width), BF16) for n in sizes],
        ],
        scratch_shapes=[pltpu.VMEM((LANES, width), F32)],
        compiler_params=params(),
        name="pack",
        cost_estimate=cost(3),
    )(wqkv, wout, router, *[g[None, :] for g in gains], w_in, w_out, b_in, b_out)


def slots_kernel(parts, block, prow, routes, capacity, out, out_rows, poscol, hot, limits, wide):
    total = routes.shape[1]
    experts = capacity.shape[1]
    steps = total // block
    half = LANES // 2
    sub = lax.broadcasted_iota(jnp.int32, (LANES, 1), 0)
    hot_t = jnp.where((routes[0:1, :] == sub) | (routes[1:2, :] + half == sub), 1.0, 0.0)
    hot[...] = jnp.transpose(hot_t).astype(BF16)
    limits[...] = jnp.zeros_like(limits)
    limits[:, 0:experts] = capacity[...].astype(F32)
    limits[:, half : half + experts] = capacity[...].astype(F32)
    lane = lane_iota(1, LANES)
    index = lax.broadcasted_iota(jnp.int32, (total, LANES), 0)
    digits = jnp.where(
        lane_iota(total, LANES) == 0, index // 8, jnp.where(lane_iota(total, LANES) == 1, index % 8, 0)
    ).astype(F32).astype(BF16)

    def find(i, carry):
        at = pl.ds(pl.multiple_of(i * block, block), block)
        token = lax.broadcasted_iota(jnp.int32, (block, 1), 0) + i * block
        hit = jnp.where(prow[...] == token, 1.0, 0.0).astype(BF16)
        poscol[at, :] = mm(hit, digits)
        return carry

    lax.fori_loop(0, steps, find, 0)
    turned = jnp.transpose(poscol[...])
    posrow = turned[0:1, :] * 8.0 + turned[1:2, :]
    low_lanes = lane < half
    seen = jnp.sum(hot[...].astype(F32), axis=0, keepdims=True)
    seen_b = jnp.where(low_lanes, 0.0, pltpu.roll(jnp.broadcast_to(seen, (8, LANES)), half, 1)[0:1, :])
    expert = jnp.where(low_lanes, lane, lane - half)
    front, rest = parts
    base = (expert * front + 1).astype(F32)
    base_b = (experts * front + expert * rest - front + 1).astype(F32)

    def step(i, carry):
        at = pl.ds(pl.multiple_of(i * block, block), block)
        mine = poscol[at, 0:1] * 8.0 + poscol[at, 1:2]
        earlier = jnp.where(posrow < mine, 1.0, 0.0).astype(BF16)
        own = hot[at, :].astype(F32)
        place = mm(earlier, hot[...]) + seen_b
        number = place + jnp.where(place < front, base, base_b)
        value = jnp.where(place < limits[...], number, 0.0) * own
        slot_a = jnp.sum(jnp.where(low_lanes, value, 0.0), axis=1, keepdims=True) - 1.0
        slot_b = jnp.sum(jnp.where(low_lanes, 0.0, value), axis=1, keepdims=True) - 1.0
        wide[at, :] = jnp.where(lane == 0, slot_a, slot_b)
        out[at, :] = jnp.where(lane_iota(1, 2) == 0, slot_a, slot_b).astype(jnp.int32)
        return carry

    lax.fori_loop(0, steps, step, 0)
    out_rows[...] = jnp.transpose(wide[...])[0:2, :].astype(jnp.int32)


def make_slots(route_rows, priority, capacity, parts):
    total = route_rows.shape[1]
    return pl.pallas_call(
        partial(slots_kernel, parts, 400),
        out_shape=[
            jax.ShapeDtypeStruct((total, 2), jnp.int32),
            jax.ShapeDtypeStruct((2, total), jnp.int32),
        ],
        scratch_shapes=[
            pltpu.VMEM((total, LANES), F32),
            pltpu.VMEM((total, LANES), BF16),
            pltpu.VMEM((1, LANES), F32),
            pltpu.VMEM((total, LANES), F32),
        ],
        compiler_params=params(),
        name="slots",
        cost_estimate=cost(8),
    )(priority, route_rows, capacity[None, :])


def dispatch_kernel(start, size, with_other, slot_rows, route_rows, *refs):
    *sources, out = refs
    group = out.shape[0]
    tall = group * size
    width = out.shape[2]
    place = lax.broadcasted_iota(jnp.int32, (tall, 1), 0) + (start + pl.program_id(0) * tall)
    hit_a = slot_rows[0:1, :] == place
    hit_b = slot_rows[1:2, :] == place
    pick = jnp.where(hit_a | hit_b, 1.0, 0.0).astype(BF16)
    for k, source in enumerate(sources):
        found = mm(pick, source[...]).astype(BF16)
        out[:, k * size : (k + 1) * size, :] = found.reshape(group, size, width)
    if with_other:
        named = route_rows[...].astype(F32) + 1.0
        found = jnp.where(hit_a, named[1:2, :], jnp.where(hit_b, named[0:1, :], 0.0))
        column = jnp.sum(found, axis=1, keepdims=True) - 1.0
        last = len(sources) * size
        for g in range(group):
            turned = jnp.transpose(
                jnp.broadcast_to(column[g * size : (g + 1) * size, :], (size, LANES))
            )
            out[g, last : last + EXTRA, 0:size] = turned[0:EXTRA, :].astype(BF16)


def dispatch(slot_rows, route_rows, sources, experts, piece, with_other):
    total, width = sources[0].shape
    start, size = piece
    tall = size * len(sources) + (EXTRA if with_other else 0)
    group = 1 if with_other else 2
    return pl.pallas_call(
        partial(dispatch_kernel, start, size, with_other),
        grid=(experts // group,),
        in_specs=[
            whole((2, total)),
            whole((2, total)),
            *[whole((total, width)) for _ in sources],
        ],
        out_specs=pl.BlockSpec((group, tall, width), lambda e: (e, 0, 0)),
        out_shape=jax.ShapeDtypeStruct((experts, tall, width), BF16),
        compiler_params=params(1),
        name="dispatch",
        cost_estimate=cost(10),
    )(slot_rows, route_rows, *sources)


def stack_rows(length, width):
    return LANES * HEADS // width * ((length + 15) // 16 * 16)


def attention_kernel(
    experts, x, mask, small, wqkv, wout, triple, context, logs, residual, normed, gains
):
    @pl.when(pl.program_id(0) == 0)
    def _():
        gains[0:4, :] = gain_rows(small, experts)

    width = x.shape[1]
    length = x.shape[0]
    x_wide = x[...].astype(F32)
    unit, _ = norm_stats(x_wide)
    low = (unit * gains[0:1, :] + gains[1:2, :]).astype(BF16)
    mixed = mm(low, wqkv[...]).astype(BF16)
    triple[...] = mixed
    bias = jnp.where(mask[0] > 0, 0.0, NEGATIVE)
    lane = lane_iota(1, LANES)
    head_width = width // HEADS
    scale = head_width ** (-0.5)
    per = LANES // head_width
    gathered = jnp.zeros((length, LANES), F32)
    lanes_all = lane_iota(length, LANES)
    for group in range(HEADS // per):
        begin = group * LANES
        queries = mixed[:, begin : begin + LANES]
        keys = mixed[:, width + begin : width + begin + LANES]
        values = mixed[:, 2 * width + begin : 2 * width + begin + LANES]
        merged = jnp.zeros((length, LANES), F32)
        for inner in range(per):
            inside = (lane >= inner * head_width) & (lane < (inner + 1) * head_width)
            chosen = queries * jnp.where(inside, scale, 0.0).astype(BF16)
            scores = mm_nt(chosen, keys) + bias
            peak = jnp.max(scores, axis=-1, keepdims=True)
            raised = jnp.exp(scores - peak)
            sums = jnp.sum(raised, axis=-1, keepdims=True)
            found = mm(raised.astype(BF16), values) * (1.0 / sums)
            merged = jnp.where(inside, found, merged)
            gathered = jnp.where(
                lanes_all == group * per + inner, peak + jnp.log(sums), gathered
            )
        context[:, begin : begin + LANES] = merged.astype(BF16)
    logs[0] = jnp.transpose(gathered)[:HEADS, :]
    after = x_wide + mm(context[...], wout[...])
    residual[...] = after
    unit_b, _ = norm_stats(after)
    normed[...] = (unit_b * gains[2:3, :] + gains[3:4, :]).astype(BF16)


def small_spec(width):
    last = 4 * width // LANES
    return pl.BlockSpec((width, LANES), lambda i: (0, last), pipeline_mode=pl.Buffered(1))


def attention_forward(x, mask, dense, experts):
    total, width = x.shape
    images, length = mask.shape
    rows = lambda i: (i, 0)
    return pl.pallas_call(
        partial(attention_kernel, experts),
        grid=(images,),
        in_specs=[
            pl.BlockSpec((length, width), rows),
            pl.BlockSpec((1, 1, length), lambda i: (i, 0, 0)),
            small_spec(width),
            pl.BlockSpec((width, 3 * width), lambda i: (0, 0), pipeline_mode=pl.Buffered(1)),
            pl.BlockSpec((width, width), lambda i: (0, 3), pipeline_mode=pl.Buffered(1)),
        ],
        out_specs=[
            pl.BlockSpec((length, 3 * width), rows),
            pl.BlockSpec((length, width), rows),
            pl.BlockSpec((1, HEADS, length), lambda i: (i, 0, 0)),
            pl.BlockSpec((length, width), rows),
            pl.BlockSpec((length, width), rows),
        ],
        out_shape=[
            jax.ShapeDtypeStruct((total, 3 * width), BF16),
            jax.ShapeDtypeStruct((total, width), BF16),
            jax.ShapeDtypeStruct((images, HEADS, length), F32),
            jax.ShapeDtypeStruct((total, width), F32),
            jax.ShapeDtypeStruct((total, width), BF16),
        ],
        scratch_shapes=[pltpu.VMEM((8, width), F32)],
        compiler_params=params(1),
        name="attention_forward",
        cost_estimate=cost(17),
    )(x, mask.reshape(images, 1, length), dense, dense, dense)


def experts_kernel(block, more, *refs):
    if more:
        mixed, own, router, w_in, w_out, b_in, b_out, *rest = refs
        old_mine, old_mate, old_router, back, sent, dw_mine, dw_mate, drouter, *rest = rest
        *rest, rows = rest
        ups, shift = mixed, block

        @pl.when(pl.program_id(0) == 0)
        def _():
            for i in range(mixed.shape[0]):
                rows[i * block : (i + 1) * block, :] = mixed[i, 0:block, :]

        outs = (back, sent, 0)
        old = (old_mine, old_mate, old_router)
    else:
        rows, ups, own, router, w_in, w_out, b_in, b_out, *rest = refs
        ret, dw_mine, dw_mate, drouter, *rest = rest
        outs = (ret, ret, block)
        shift, old = 0, None
    experts_body(
        block, rows, ups, shift, own, router, w_in, w_out, b_in, b_out, old,
        outs, dw_mine, dw_mate, drouter, *rest,
    )


def experts_body(
    block, rows, ups, shift, own, router, w_in, w_out, b_in, b_out, old,
    outs, dw_mine, dw_mate, drouter,
    gate, weighted, made, pushed, hid, pre_g, other, db,
):
    f = pl.program_id(0)
    last = pl.num_programs(0) - 1
    total, width = rows.shape
    steps = total // block
    lane = lane_iota(1, LANES)

    @pl.when(f == 0)
    def _():
        own_hot = own[...] > 0.0

        def step(i, acc):
            at = pl.ds(pl.multiple_of(i * block, block), block)
            logits = mm(rows[at, :], router[...])
            mine = jnp.sum(jnp.where(own_hot, logits, 0.0), axis=1, keepdims=True)
            named = ups[i, shift + block : shift + block + EXTRA, 0:block].astype(F32)
            rival = jnp.transpose(named)[:, 0:1].astype(jnp.int32)
            other[at, :] = rival
            theirs = jnp.sum(jnp.where(lane == rival, logits, 0.0), axis=1, keepdims=True)
            share = 1.0 / (1.0 + jnp.exp(theirs - mine))
            gate[at, 0:1] = share
            gate[at, 1:2] = 1.0 / (1.0 + jnp.exp(mine - theirs))
            scaled = (share * ups[i, shift : shift + block, :].astype(F32)).astype(BF16)
            weighted[at, :] = scaled
            return acc + jnp.sum(scaled.astype(F32), axis=0, keepdims=True)

        db[...] = jnp.zeros_like(db)
        db[1:2, :] = lax.fori_loop(0, steps, step, jnp.zeros((1, width), F32), unroll=4)

    chunk = w_in.shape[1]
    hidden_share = (dw_mine.shape[1] - EXTRA) // 2
    per = hidden_share // chunk
    place = f % per
    biases = b_in[0, 0:1, :].astype(F32)
    bias = biases[:, 0:chunk]
    for k in range(1, per):
        bias = jnp.where(place == k, biases[:, k * chunk : (k + 1) * chunk], bias)

    big = total // BIG_STEPS

    def body(i, acc):
        at = pl.ds(pl.multiple_of(i * big, big), big)
        here = rows[at, :]
        u = mm_nt(here, w_in[0]) + bias
        inner = ROOT + (ROOT * CUBIC) * (u * u)
        share = 0.5 + 0.5 * jnp.tanh(u * inner)
        raised = u * share
        hidden = raised.astype(BF16)
        slope = share + raised * (1.0 - share) * (6.0 * inner - 4.0 * ROOT)
        hid[at, :] = hidden
        grad = mm_nt(weighted[at, :], w_out[0]) * slope
        low = grad.astype(BF16)
        pre_g[at, :] = low
        part = mm(hidden, w_out[0])
        part_b = mm(low, w_in[0])

        @pl.when(f == 0)
        def _():
            made[at, :] = part
            pushed[at, :] = part_b

        @pl.when(f > 0)
        def _():
            made[at, :] += part
            pushed[at, :] += part_b

        return acc + jnp.sum(grad, axis=0, keepdims=True)

    db_here = lax.fori_loop(0, BIG_STEPS, body, jnp.zeros((1, chunk), F32))
    for k in range(per):

        @pl.when(place == k)
        def _():
            db[0:1, k * chunk : (k + 1) * chunk] = db_here

    dw_out_here = mm_tn(hid[...], weighted[...])
    dw_in_here = mm_tn(pre_g[...], rows[...])

    def put(target, prior):
        spots = (
            (pl.ds(pl.multiple_of(place * chunk, chunk), chunk), dw_in_here),
            (pl.ds(pl.multiple_of(hidden_share + place * chunk, chunk), chunk), dw_out_here),
            (pl.ds(2 * hidden_share, EXTRA), db[...]),
        )
        for spot, value in spots:
            if prior is not None:
                value = value + prior[0, spot, :].astype(F32)
            target[0, spot, :] = value.astype(BF16)

    quarters = (last + 1) // per

    @pl.when(f // per < quarters // 2)
    def _():
        put(dw_mine, old and old[0])

    @pl.when(f // per >= quarters // 2)
    def _():
        put(dw_mate, old and old[1])

    @pl.when(f == last)
    def _():
        own_row = own[...]
        back, sent, after = outs

        def step(i, carry):
            at = pl.ds(pl.multiple_of(i * block, block), block)
            produced = (made[at, :] + b_out[...]).astype(BF16).astype(F32)
            share = gate[at, 0:1]
            sent[i, after : after + block, :] = (share * produced).astype(BF16)
            inner = jnp.sum(produced * ups[i, shift : shift + block, :].astype(F32), axis=1, keepdims=True)
            pull = share * gate[at, 1:2] * inner
            rival = other[at, :]
            spread = (pull * (own_row - jnp.where(lane == rival, 1.0, 0.0))).astype(BF16)
            back[i, 0:block, :] = (pushed[at, :] + mm_nt(spread, router[...])).astype(BF16)
            hid[at, 0:LANES] = spread
            return carry

        lax.fori_loop(0, steps, step, 0, unroll=4)
        drouter[...] = mm_tn(rows[...], hid[:, 0:LANES]) + (0.0 if old is None else old[2][...])


def run_experts(given, block, own, dense, weights, b_out, old):
    experts, _, width = given[0].shape
    total = experts * block
    quarters, double, _ = weights.shape
    share = (double - EXTRA) // 2
    chunk = min(share, 512)
    per = share // chunk
    half = quarters // 2
    at = lambda f: (f // per, f % per, 0)
    out_at = lambda f: (f // per, per + f % per, 0)
    bias_at = lambda f: (f // per, 2 * share // EXTRA, 0)
    mine_at = lambda f: (jnp.minimum(f // per, half - 1), 0, 0)
    mate_at = lambda f: (jnp.maximum(f // per - half, 0), 0, 0)
    steps = quarters * per
    dw_shape = jax.ShapeDtypeStruct((half, double, width), BF16)
    sums = [
        pl.BlockSpec((1, double, width), mine_at),
        pl.BlockSpec((1, double, width), mate_at),
        whole((width, LANES)),
    ]
    if old:
        given_specs = [whole(given[0].shape)]
        ret_shapes = [(experts, block, width)] * 2
        more_scratch = [pltpu.VMEM((total, width), BF16)]
    else:
        given = (given[0].reshape(total, width), given[1])
        given_specs = [whole(given[0].shape), whole(given[1].shape)]
        ret_shapes = [(experts, 2 * block, width)]
        more_scratch = []
    return pl.pallas_call(
        partial(experts_kernel, block, bool(old)),
        grid=(steps,),
        in_specs=given_specs
        + [
            whole((1, LANES)),
            small_spec(width),
            pl.BlockSpec((1, chunk, width), at),
            pl.BlockSpec((1, chunk, width), out_at),
            pl.BlockSpec((1, EXTRA, width), bias_at),
            whole((1, width)),
        ]
        + (sums if old else []),
        out_specs=[whole(r) for r in ret_shapes] + sums,
        out_shape=[jax.ShapeDtypeStruct(r, BF16) for r in ret_shapes]
        + [dw_shape, dw_shape, jax.ShapeDtypeStruct((width, LANES), F32)],
        scratch_shapes=[
            pltpu.VMEM((total, 2), F32),
            pltpu.VMEM((total, width), BF16),
            pltpu.VMEM((total, width), F32),
            pltpu.VMEM((total, width), F32),
            pltpu.VMEM((total, chunk), BF16),
            pltpu.VMEM((total, chunk), BF16),
            pltpu.VMEM((total, 1), jnp.int32),
            pltpu.VMEM((EXTRA, width), F32),
        ]
        + more_scratch,
        compiler_params=params(1),
        name="experts",
        cost_estimate=cost(50),
    )(*given, own, dense, weights, weights, weights, b_out, *old)


def backward_kernel(
    experts, x, mask, small, wqkv, wout, triple, context, logs, residual, up, slot, ret_a, ret_b, drouter, parity,
    input_grad, keep, give_a, give_b,
    tg, gains, dqkv, dwout, dgains, stack_k, stack_v, dq_t,
):
    step = pl.program_id(0)
    length, width = x.shape

    @pl.when(step == 0)
    def _():
        dqkv[...] = jnp.zeros_like(dqkv)
        dwout[...] = jnp.zeros_like(dwout)
        dgains[...] = jnp.zeros_like(dgains)
        gains[0:4, :] = gain_rows(small, experts)
        stack_k[...] = jnp.zeros_like(stack_k)
        stack_v[...] = jnp.zeros_like(stack_v)

    second_grad = gather_slots(slot, (ret_a, ret_b))
    unit_b, scale_b = norm_stats(residual[...])
    dgains[experts + 2 : experts + 3, :] += jnp.sum(second_grad * unit_b, axis=0, keepdims=True)
    dgains[experts + 3 : experts + 4, :] += jnp.sum(second_grad, axis=0, keepdims=True)
    residual_grad = up[...].astype(F32) + norm_back(second_grad, unit_b, scale_b, gains[2:3, :])
    residual_low = residual_grad.astype(BF16)
    dwout[...] += mm_tn(context[...], residual_low)
    context_grad = mm_nt(residual_low, wout[...]).astype(BF16)

    lane = lane_iota(1, LANES)
    head_width = width // HEADS
    scale = head_width ** (-0.5)
    per = LANES // head_width
    tall = stack_k.shape[0] // per
    hide_row = jnp.where(mask[0] > 0, 0.0, NEGATIVE)
    hide = jnp.transpose(jnp.broadcast_to(hide_row, (LANES, length)))[:, 0:1]
    hide = jnp.concatenate([hide, jnp.full((tall - length, 1), NEGATIVE, F32)], axis=0)
    for group in range(HEADS // per):
        begin = group * LANES
        queries = triple[:, begin : begin + LANES] * jnp.asarray(scale, BF16)
        keys = triple[:, width + begin : width + begin + LANES]
        values = triple[:, 2 * width + begin : 2 * width + begin + LANES]
        pulled = context_grad[:, begin : begin + LANES]
        for inner in range(per):
            inside = (lane >= inner * head_width) & (lane < (inner + 1) * head_width)
            only = jnp.where(inside, 1.0, 0.0).astype(BF16)
            stack_k[inner * tall : inner * tall + length, :] = keys * only
            stack_v[inner * tall : inner * tall + length, :] = values * only
        scores = mm_nt(stack_k[...], queries)
        prob_grad = mm_nt(stack_v[...], pulled)
        probs, score_grad = [], []
        for inner in range(per):
            rows = slice(inner * tall, (inner + 1) * tall)
            head = group * per + inner
            prob = jnp.exp(scores[rows, :] + (hide - logs[0, head : head + 1, :]))
            pull = prob_grad[rows, :]
            inner_sum = jnp.sum(prob * pull, axis=0, keepdims=True)
            probs.append(prob.astype(BF16))
            score_grad.append((prob * (pull - inner_sum)).astype(BF16))
        probs = jnp.concatenate(probs, axis=0)
        score_grad = jnp.concatenate(score_grad, axis=0)
        dk_all = mm(score_grad, queries)
        dv_all = mm(probs, pulled)
        dq_t[begin : begin + LANES, :] = mm(jnp.transpose(stack_k[...]), score_grad) * scale
        dk, dv = dk_all[0:length, :], dv_all[0:length, :]
        for inner in range(1, per):
            rows = slice(inner * tall, inner * tall + length)
            dk = jnp.where(lane >= inner * head_width, dk_all[rows, :], dk)
            dv = jnp.where(lane >= inner * head_width, dv_all[rows, :], dv)
        tg[:, width + begin : width + begin + LANES] = dk.astype(BF16)
        tg[:, 2 * width + begin : 2 * width + begin + LANES] = dv.astype(BF16)
    tg[:, 0:width] = jnp.transpose(dq_t[...]).astype(BF16)
    unit, scale_a = norm_stats(x[...].astype(F32))
    low = (unit * gains[0:1, :] + gains[1:2, :]).astype(BF16)
    dqkv[...] += mm_tn(low, tg[...])
    first_grad = mm_nt(tg[...], wqkv[...])
    dgains[experts + 0 : experts + 1, :] += jnp.sum(first_grad * unit, axis=0, keepdims=True)
    dgains[experts + 1 : experts + 2, :] += jnp.sum(first_grad, axis=0, keepdims=True)
    input_grad[...] = residual_grad + norm_back(first_grad, unit, scale_a, gains[0:1, :])

    @pl.when(step == pl.num_programs(0) - 1)
    def _():
        tail = drouter[...] + jnp.transpose(dgains[...])
        share = width // 4
        odd = parity[0, 0]
        for part in range(4):
            rows = slice(part * share, (part + 1) * share)
            spot = slice(part // 2 * share, (part // 2 + 1) * share)

            def put(target, spot):
                target[spot, : 3 * width] = dqkv[rows, :].astype(BF16)
                target[spot, 3 * width : 4 * width] = dwout[rows, :].astype(BF16)
                target[spot, 4 * width :] = tail[rows, :].astype(BF16)

            @pl.when(odd == part % 2)
            def _():
                put(keep, spot)

            @pl.when(odd != part % 2)
            def _():
                put(give_b if part // 2 else give_a, slice(0, share))


def attention_backward(
    x, mask, dense, triple, context, logs, residual, up, slot, ret, drouter, parity,
    experts,
):
    total, width = x.shape
    images, length = mask.shape
    rows = lambda i: (i, 0)
    return pl.pallas_call(
        partial(backward_kernel, experts),
        grid=(images,),
        in_specs=[
            pl.BlockSpec((length, width), rows),
            pl.BlockSpec((1, 1, length), lambda i: (i, 0, 0)),
            small_spec(width),
            pl.BlockSpec((width, 3 * width), lambda i: (0, 0), pipeline_mode=pl.Buffered(1)),
            pl.BlockSpec((width, width), lambda i: (0, 3), pipeline_mode=pl.Buffered(1)),
            pl.BlockSpec((length, 3 * width), rows),
            pl.BlockSpec((length, width), rows),
            pl.BlockSpec((1, HEADS, length), lambda i: (i, 0, 0)),
            pl.BlockSpec((length, width), rows),
            pl.BlockSpec((length, width), rows),
            pl.BlockSpec((length, 2), rows),
            *returned_specs(ret, 0),
            whole((width, LANES)),
            pl.BlockSpec(memory_space=pltpu.SMEM),
        ],
        out_specs=[
            pl.BlockSpec((length, width), rows),
            whole((width // 2, 4 * width + LANES)),
            whole((width // 4, 4 * width + LANES)),
            whole((width // 4, 4 * width + LANES)),
        ],
        out_shape=[
            jax.ShapeDtypeStruct((total, width), F32),
            jax.ShapeDtypeStruct((width // 2, 4 * width + LANES), BF16),
            jax.ShapeDtypeStruct((width // 4, 4 * width + LANES), BF16),
            jax.ShapeDtypeStruct((width // 4, 4 * width + LANES), BF16),
        ],
        scratch_shapes=[
            pltpu.VMEM((length, 3 * width), BF16),
            pltpu.VMEM((8, width), F32),
            pltpu.VMEM((width, 3 * width), F32),
            pltpu.VMEM((width, width), F32),
            pltpu.VMEM((LANES, width), F32),
            pltpu.VMEM((stack_rows(length, width), LANES), BF16),
            pltpu.VMEM((stack_rows(length, width), LANES), BF16),
            pltpu.VMEM((width, length), F32),
        ],
        compiler_params=params(1),
        name="attention_backward",
        cost_estimate=cost(50),
    )(
        x, mask.reshape(images, 1, length), dense, dense, dense, triple, context, logs, residual,
        up, slot, *ret, drouter, parity,
    )


def combine_kernel(slot, residual, ret_a, ret_b, out):
    out[...] = (residual[...] + gather_slots(slot, (ret_a, ret_b))).astype(BF16)


def combine(slot, residual, ret, block):
    total, width = residual.shape
    rows = lambda i: (i, 0)
    return pl.pallas_call(
        combine_kernel,
        grid=(total // block,),
        in_specs=[
            pl.BlockSpec((block, 2), rows),
            pl.BlockSpec((block, width), rows),
            *returned_specs(ret, 1),
        ],
        out_specs=pl.BlockSpec((block, width), rows),
        out_shape=jax.ShapeDtypeStruct((total, width), BF16),
        compiler_params=params(1),
        name="combine",
        cost_estimate=cost(10),
    )(slot, residual, *ret)


def unpack_kernel(experts, total, wqkv, wout, router, *gains):
    width = wout.shape[1]
    wqkv[...] = total[:, : 3 * width].astype(F32)
    wout[...] = total[:, 3 * width : 4 * width].astype(F32)
    turned = jnp.transpose(total[:, 4 * width :].astype(F32))
    router[...] = turned[0:experts, :]
    for k, gain in enumerate(gains):
        gain[...] = turned[experts + k : experts + k + 1, :]


def unpack(total, experts):
    share = total.shape[0]
    width = (total.shape[1] - LANES) // 4
    shapes = [(share, 3 * width), (share, width), (experts, share)] + [(1, share)] * 4
    return pl.pallas_call(
        partial(unpack_kernel, experts),
        out_shape=[jax.ShapeDtypeStruct(shape, F32) for shape in shapes],
        compiler_params=params(),
        name="unpack",
        cost_estimate=cost(2),
    )(total)


class PlainPlan:
    def __init__(self, seq, wt):
        self.seq, self.wt = seq, wt

    def own_id(self):
        return lax.axis_index("seq")

    def exchange(self, a):
        return lax.all_to_all(a, "seq", split_axis=0, concat_axis=0, tiled=True)

    def begin_dense(self, packed):
        return packed

    def gather_dense(self, packed, begun):
        return lax.all_gather(begun, "wt", axis=0, tiled=True)

    def begin_fetch(self, packed):
        return (packed,)

    def fetch(self, packed, begun):
        return lax.all_gather(begun[0], "wt", axis=0)

    def spread_out_bias(self, quarters):
        return quarters

    def begin_reduce(self, mine, mate):
        return (jnp.concatenate([mine, mate]).reshape(-1, mine.shape[-1]),)

    def reduce_expert(self, parts):
        (parts,) = parts
        return lax.psum_scatter(parts, "wt", scatter_dimension=0, tiled=True)

    def finish_expert(self, parts, received):
        return received.astype(F32)

    def parity(self):
        return jnp.zeros((1, 1), jnp.int32)

    def begin_dense_sum(self, keep, give_a, give_b):
        half = keep.shape[0] // 2
        grads = jnp.concatenate([keep[:half], give_a, keep[half:], give_b])
        return lax.psum_scatter(grads, "wt", scatter_dimension=0, tiled=True)

    def reduce_dense(self, part):
        return lax.psum(part, "seq")


class CubePlan:
    AXES = ("seq", "wt")

    def __init__(self, seq, wt):
        self.seq, self.wt = seq, wt
        self.levels = seq // 2
        places = [
            (z, y, x, c)
            for z in range(self.levels)
            for y in range(2)
            for x in range(2)
            for c in range(2)
        ]
        flat = self.flat
        self.cross = [(flat(*p), flat(p[0], p[1], 1 - p[2], p[3])) for p in places]
        self.core = [(flat(*p), flat(p[0], p[1], p[2], 1 - p[3])) for p in places]
        near = lambda p: p[2] == p[0] % 2
        away = lambda p: (p[0] ^ 2, p[1], 1 - p[0] % 2, p[3])
        home = lambda p: (p[0], p[1], p[0] % 2, p[3])
        self.first = [(flat(*p), flat(*(away(p) if near(p) else home(p)))) for p in places]
        self.second = [(flat(*p), flat(*away(p))) for p in places if not near(p)]
        self.groups = [
            [self.host(half, e, c) for e in range(seq)] for half in range(2) for c in range(2)
        ]

    def flat(self, z, y, x, c):
        return (z * 2 + y) * self.wt + x * 2 + c

    def host(self, half, expert, c):
        z, y = expert // 2, expert % 2
        if z // 2 == half:
            return self.flat(z, y, z % 2, c)
        return self.flat(z ^ 2, y, 1 - z % 2, c)

    def send(self, a, pairs):
        return lax.ppermute(a, self.AXES, pairs)

    def x_zero(self):
        return lax.axis_index("wt") < 2

    def odd_level(self):
        return lax.axis_index("seq") // 2 % 2 == 1

    def near(self):
        return self.x_zero() != self.odd_level()

    def core_zero(self):
        return lax.axis_index("wt") % 2 == 0

    def own_id(self):
        rank = lax.axis_index("seq")
        return jnp.where(self.near(), rank, rank ^ 4)

    def exchange(self, a):
        return lax.all_to_all(
            a, self.AXES, split_axis=0, concat_axis=0, axis_index_groups=self.groups, tiled=True
        )

    def begin_dense(self, packed):
        return self.send(packed, self.cross)

    def gather_dense(self, packed, far):
        mate = self.send(packed, self.core)
        far_mate = self.send(far, self.core)
        flip = self.x_zero()
        low, high = jnp.where(flip, packed, far), jnp.where(flip, far, packed)
        low_mate, high_mate = jnp.where(flip, mate, far_mate), jnp.where(flip, far_mate, mate)
        first = self.core_zero()
        return jnp.concatenate(
            [
                jnp.where(first, low, low_mate),
                jnp.where(first, low_mate, low),
                jnp.where(first, high, high_mate),
                jnp.where(first, high_mate, high),
            ],
            axis=0,
        )

    def begin_fetch(self, packed):
        return self.send(packed, self.first), self.send(packed, self.second)

    def fetch(self, packed, begun):
        got, got_b = begun
        flip = self.near()
        low = jnp.where(flip, packed, got)
        high = jnp.where(flip, got, got_b)
        return jnp.stack([low, high, self.send(low, self.core), self.send(high, self.core)])

    def spread_out_bias(self, quarters):
        mine, odd = self.core_zero(), self.odd_level()
        order = []
        for x in range(2):
            for c in range(2):
                same = mine == (c == 0)
                level = odd == (x == 1)
                order.append(
                    jnp.where(
                        same,
                        jnp.where(level, quarters[0], quarters[1]),
                        jnp.where(level, quarters[2], quarters[3]),
                    )
                )
        return jnp.stack(order)

    def begin_reduce(self, mine, mate):
        got = self.send(mate, self.core)
        low = (mine[0].astype(F32) + got[0].astype(F32)).astype(BF16)
        high = (mine[1].astype(F32) + got[1].astype(F32)).astype(BF16)
        return low, high, jnp.where(self.near(), high, low)

    def reduce_expert(self, parts):
        low, high, give = parts
        return self.send(give, self.first_back()), self.send(high, self.second)

    def finish_expert(self, parts, received):
        far, far_b = received
        return jnp.where(self.near(), parts[0], far_b).astype(F32) + far.astype(F32)

    def first_back(self):
        return [(b, a) for a, b in self.first]

    def parity(self):
        return (lax.axis_index("wt") % 2).reshape(1, 1)

    def begin_dense_sum(self, keep, *give):
        share = keep.shape[0] // 2
        low, high = (
            keep[k * share : (k + 1) * share].astype(F32) + self.send(v, self.core).astype(F32)
            for k, v in enumerate(give)
        )
        flip = self.x_zero()
        out = self.send(jnp.where(flip, high, low).astype(BF16), self.cross)
        mine = jnp.where(flip, low, high) + out.astype(F32)
        return mine.astype(BF16)

    def reduce_dense(self, mine):
        share, width = mine.shape
        pieces = mine.reshape(self.seq, share // self.seq, width)
        swap = lambda v: lax.all_to_all(v, "seq", split_axis=0, concat_axis=0, tiled=True)
        total = jnp.sum(swap(pieces).astype(F32), axis=0, keepdims=True).astype(BF16)
        spread = swap(jnp.broadcast_to(total, pieces.shape))
        return spread.reshape(share, width)


def plan_of(seq, wt):
    return CubePlan(seq, wt) if (seq, wt) == (8, 4) else PlainPlan(seq, wt)


def local(
    inputs,
    key_mask,
    routes,
    priority,
    capacity,
    attention_gain,
    attention_shift,
    query_key_value,
    attention_out,
    mixture_gain,
    mixture_shift,
    router_weight,
    expert_in,
    expert_in_bias,
    expert_out,
    expert_out_bias,
    cotangent,
):
    total, width = inputs.shape
    experts = capacity.shape[0]
    cap = 8 * max(1, total // (4 * experts))
    share = query_key_value.shape[0]
    hidden_share = expert_in.shape[1]
    plan = plan_of(lax.axis_size("seq"), lax.axis_size("wt"))

    tie = lax.optimization_barrier
    front = (cap // 2 + EXTRA - 1) // EXTRA * EXTRA
    parts = (front, cap - front)
    packed, *shards = pack(
        query_key_value, attention_out, router_weight.T,
        (attention_gain, attention_shift, mixture_gain, mixture_shift),
        expert_in[0], expert_out[0], expert_in_bias, expert_out_bias,
    )
    fetched = [plan.begin_fetch(shard) for shard in shards]
    far = plan.begin_dense(packed)
    own = (jnp.arange(LANES) == plan.own_id()).astype(F32)[None, :]
    route_rows = routes.T
    slot, slot_rows = make_slots(route_rows, priority, capacity, parts)
    slot_rows, far, fetched[0] = tie((slot_rows, far, fetched[0]))
    pieces = ((0, front), (experts * front, cap - front))
    send = partial(dispatch, slot_rows, route_rows)
    ups_a = send((cotangent,), experts, pieces[0], True)
    dense = plan.gather_dense(packed, far)
    dense, ups_a = tie((dense, ups_a))
    ups_a = plan.exchange(ups_a)

    triple, context, logs, residual, normed = attention_forward(inputs, key_mask, dense, experts)
    rows_a = send((normed,), experts, pieces[0], False)
    mixed_b = send((normed, cotangent), experts, pieces[1], True)
    rows_a, ups_a, fetched[1] = tie((rows_a, ups_a, fetched[1]))
    rows_a = plan.exchange(rows_a)
    weights = jnp.concatenate(
        [plan.fetch(*pair) for pair in zip(shards, fetched)], axis=1
    )
    b_out = plan.spread_out_bias(
        weights[:, 2 * hidden_share + 1, :share].astype(F32)
    ).reshape(1, width)
    rows_a, mixed_b, weights, b_out = tie((rows_a, mixed_b, weights, b_out))
    mixed_b = plan.exchange(mixed_b)
    ret_a, *sums = run_experts((rows_a, ups_a), parts[0], own, dense, weights, b_out, ())
    ret_a, mixed_b = tie((ret_a, mixed_b))
    ret_a = plan.exchange(ret_a)
    back_b, sent_b, *sums = run_experts(
        (mixed_b,), parts[1], own, dense, weights, b_out, tuple(sums)
    )
    back_b, ret_a = tie((back_b, ret_a))
    back_b = plan.exchange(back_b)
    halves = plan.begin_reduce(*sums[:2])
    back_b, sent_b, halves = tie((back_b, sent_b, halves))
    sent_b = plan.exchange(sent_b)
    received = plan.reduce_expert(halves)
    ret_a = ret_a.reshape(experts, 2, front, width)
    input_grad, *grads = attention_backward(
        inputs, key_mask, dense, triple, context, logs, residual, cotangent, slot,
        (ret_a, back_b), sums[2], plan.parity(), experts,
    )
    grads, received = tie((grads, received))
    mine = plan.begin_dense_sum(*grads)
    mine, sent_b = tie((mine, sent_b))
    shard = plan.finish_expert(halves, received)
    done = plan.reduce_dense(mine)
    block_output = combine(slot, residual, (ret_a, sent_b), 200)
    dqkv, dwout, drouter, *dgains = unpack(done, experts)
    dgains = [g.reshape(share) for g in dgains]
    rank = lax.axis_index("wt")
    return (
        block_output,
        input_grad,
        dgains[0],
        dgains[1],
        dqkv,
        dwout,
        dgains[2],
        dgains[3],
        drouter.T,
        shard[None, :hidden_share],
        shard[2 * hidden_share, :hidden_share][None],
        shard[None, hidden_share : 2 * hidden_share],
        lax.dynamic_slice(shard[2 * hidden_share + 1], (rank * share,), (share,))[None],
    )


def solution(mesh):
    both = P(("seq", "wt"), None)
    placed = (
        both,
        both,
        both,
        both,
        P(),
        P("wt"),
        P("wt"),
        P("wt", None),
        P("wt", None),
        P("wt"),
        P("wt"),
        P("wt", None),
        P("seq", "wt", None),
        P("seq", "wt"),
        P("seq", "wt", None),
        P("seq", "wt"),
        both,
    )
    return jax.shard_map(
        local,
        mesh=mesh,
        in_specs=placed,
        out_specs=(
            both,
            both,
            P("wt"),
            P("wt"),
            P("wt", None),
            P("wt", None),
            P("wt"),
            P("wt"),
            P("wt", None),
            P("seq", "wt", None),
            P("seq", "wt"),
            P("seq", "wt", None),
            P("seq", "wt"),
        ),
        check_vma=False,
    )
```

```python
from functools import partial

import jax
import jax.numpy as jnp
from jax import lax
from jax.experimental import pallas as pl
from jax.experimental.pallas import tpu as pltpu
from jax.sharding import PartitionSpec as P

HEADS = 8
NEGATIVE = -1e30
EPSILON = 1e-06
LANES = 128
BIG_STEPS = 2
VMEM_BYTES = 60 * 1024 * 1024
F32 = jnp.float32
BF16 = jnp.bfloat16
ROOT = 0.7978845608028654
CUBIC = 0.044715

NT = (((1,), (1,)), ((), ()))
TN = (((0,), (0,)), ((), ()))


def mm(a, b):
    return jnp.dot(a, b, preferred_element_type=F32)


def mm_nt(a, b):
    return lax.dot_general(a, b, NT, preferred_element_type=F32)


def mm_tn(a, b):
    return lax.dot_general(a, b, TN, preferred_element_type=F32)


def params(steps=0):
    return pltpu.CompilerParams(
        dimension_semantics=("arbitrary",) * steps if steps else None,
        vmem_limit_bytes=VMEM_BYTES,
    )


def cost(micros):
    return pl.CostEstimate(
        flops=int(micros * 1.0e7), bytes_accessed=int(micros * 1.0e4), transcendentals=0
    )


def gain_rows(small, experts):
    turned = jnp.transpose(small[...].astype(F32))
    return turned[experts : experts + 4, :]


def whole(shape):
    zeros = (0,) * len(shape)
    return pl.BlockSpec(shape, lambda *_: zeros, pipeline_mode=pl.Buffered(1))


def gather_slots(slot, parts):
    found = None
    start = 0
    for piece in parts:
        rows = piece[...].reshape(-1, piece.shape[-1])
        lanes = lane_iota(1, rows.shape[0]) + start
        start += rows.shape[0]
        pick = jnp.where((lanes == slot[:, 0:1]) | (lanes == slot[:, 1:2]), 1.0, 0.0)
        piece = jnp.dot(pick.astype(BF16), rows, preferred_element_type=F32)
        found = piece if found is None else found + piece
    return found


def returned_specs(ret, which):
    both, alone = ret
    experts, _, size, width = both.shape
    spot = lambda *_: (0, which, 0, 0)
    return [
        pl.BlockSpec((experts, None, size, width), spot, pipeline_mode=pl.Buffered(1)),
        whole(alone.shape),
    ]


def lane_iota(rows, width):
    return lax.broadcasted_iota(jnp.int32, (rows, width), 1)


def norm_stats(values):
    row_mean = jnp.mean(values, axis=-1, keepdims=True)
    offsets = values - row_mean
    spread = jnp.mean(offsets * offsets, axis=-1, keepdims=True)
    scale = lax.rsqrt(spread + EPSILON)
    return offsets * scale, scale


def norm_back(grad, unit, scale, gain):
    weighted = grad * gain
    first = jnp.mean(weighted, axis=-1, keepdims=True)
    second = jnp.mean(weighted * unit, axis=-1, keepdims=True)
    return scale * (weighted - first - unit * second)


EXTRA = 16


def pack_kernel(wqkv, wout, router, ga, sa, gm, sm, w_in, w_out, b_in, b_out, dense, *refs):
    *pieces, tail = refs
    width = wout.shape[1]
    experts = router.shape[0]
    share = wout.shape[0]
    hidden = w_in.shape[0]
    dense[:, : 3 * width] = wqkv[...]
    dense[:, 3 * width : 4 * width] = wout[...]
    tail[...] = jnp.zeros_like(tail)
    tail[0:experts, 0:share] = router[...].astype(F32)
    for k, row in enumerate((ga, sa, gm, sm)):
        tail[experts + k : experts + k + 1, 0:share] = row[...].astype(F32)
    columns = jnp.transpose(tail[0:LANES, 0:LANES])[:share, :]
    dense[:, 4 * width :] = columns.astype(BF16)
    sources = ((w_in, 0), (w_out, hidden))
    start = 0
    for piece in pieces:
        stop = start + piece.shape[0]
        for source, base in sources:
            low, high = max(start, base), min(stop, base + hidden)
            if low < high:
                piece[low - start : high - start, :] = source[low - base : high - base, :]
        start = stop
    tail[0:EXTRA, :] = jnp.zeros((EXTRA, width), F32)
    tail[0:1, 0:hidden] = b_in[...].astype(F32)
    tail[1:2, 0:share] = b_out[...].astype(F32)
    pieces[-1][pieces[-1].shape[0] - EXTRA :, :] = tail[0:EXTRA, :].astype(BF16)


def pack(wqkv, wout, router, gains, w_in, w_out, b_in, b_out):
    share, width = wout.shape
    hidden = w_in.shape[0]
    double = 2 * hidden + EXTRA
    cuts = [0] + [double * part // 100 // EXTRA * EXTRA for part in (47,)] + [double]
    sizes = [high - low for low, high in zip(cuts, cuts[1:])]
    return pl.pallas_call(
        pack_kernel,
        out_shape=[
            jax.ShapeDtypeStruct((share, 4 * width + LANES), BF16),
            *[jax.ShapeDtypeStruct((n, width), BF16) for n in sizes],
        ],
        scratch_shapes=[pltpu.VMEM((LANES, width), F32)],
        compiler_params=params(),
        name="pack",
        cost_estimate=cost(3),
    )(wqkv, wout, router, *[g[None, :] for g in gains], w_in, w_out, b_in, b_out)


def slots_kernel(parts, block, prow, routes, capacity, out, out_rows, poscol, hot, limits, wide):
    total = routes.shape[1]
    experts = capacity.shape[1]
    steps = total // block
    half = LANES // 2
    sub = lax.broadcasted_iota(jnp.int32, (LANES, 1), 0)
    hot_t = jnp.where((routes[0:1, :] == sub) | (routes[1:2, :] + half == sub), 1.0, 0.0)
    hot[...] = jnp.transpose(hot_t).astype(BF16)
    limits[...] = jnp.zeros_like(limits)
    limits[:, 0:experts] = capacity[...].astype(F32)
    limits[:, half : half + experts] = capacity[...].astype(F32)
    lane = lane_iota(1, LANES)
    index = lax.broadcasted_iota(jnp.int32, (total, LANES), 0)
    digits = jnp.where(
        lane_iota(total, LANES) == 0, index // 8, jnp.where(lane_iota(total, LANES) == 1, index % 8, 0)
    ).astype(F32).astype(BF16)

    def find(i, carry):
        at = pl.ds(pl.multiple_of(i * block, block), block)
        token = lax.broadcasted_iota(jnp.int32, (block, 1), 0) + i * block
        hit = jnp.where(prow[...] == token, 1.0, 0.0).astype(BF16)
        poscol[at, :] = mm(hit, digits)
        return carry

    lax.fori_loop(0, steps, find, 0)
    turned = jnp.transpose(poscol[...])
    posrow = turned[0:1, :] * 8.0 + turned[1:2, :]
    low_lanes = lane < half
    seen = jnp.sum(hot[...].astype(F32), axis=0, keepdims=True)
    seen_b = jnp.where(low_lanes, 0.0, pltpu.roll(jnp.broadcast_to(seen, (8, LANES)), half, 1)[0:1, :])
    expert = jnp.where(low_lanes, lane, lane - half)
    front, rest = parts
    base = (expert * front + 1).astype(F32)
    base_b = (experts * front + expert * rest - front + 1).astype(F32)

    def step(i, carry):
        at = pl.ds(pl.multiple_of(i * block, block), block)
        mine = poscol[at, 0:1] * 8.0 + poscol[at, 1:2]
        earlier = jnp.where(posrow < mine, 1.0, 0.0).astype(BF16)
        own = hot[at, :].astype(F32)
        place = mm(earlier, hot[...]) + seen_b
        number = place + jnp.where(place < front, base, base_b)
        value = jnp.where(place < limits[...], number, 0.0) * own
        slot_a = jnp.sum(jnp.where(low_lanes, value, 0.0), axis=1, keepdims=True) - 1.0
        slot_b = jnp.sum(jnp.where(low_lanes, 0.0, value), axis=1, keepdims=True) - 1.0
        wide[at, :] = jnp.where(lane == 0, slot_a, slot_b)
        out[at, :] = jnp.where(lane_iota(1, 2) == 0, slot_a, slot_b).astype(jnp.int32)
        return carry

    lax.fori_loop(0, steps, step, 0)
    out_rows[...] = jnp.transpose(wide[...])[0:2, :].astype(jnp.int32)


def make_slots(route_rows, priority, capacity, parts):
    total = route_rows.shape[1]
    return pl.pallas_call(
        partial(slots_kernel, parts, 400),
        out_shape=[
            jax.ShapeDtypeStruct((total, 2), jnp.int32),
            jax.ShapeDtypeStruct((2, total), jnp.int32),
        ],
        scratch_shapes=[
            pltpu.VMEM((total, LANES), F32),
            pltpu.VMEM((total, LANES), BF16),
            pltpu.VMEM((1, LANES), F32),
            pltpu.VMEM((total, LANES), F32),
        ],
        compiler_params=params(),
        name="slots",
        cost_estimate=cost(8),
    )(priority, route_rows, capacity[None, :])


def dispatch_kernel(start, size, with_other, slot_rows, route_rows, *refs):
    *sources, out = refs
    group = out.shape[0]
    tall = group * size
    width = out.shape[2]
    place = lax.broadcasted_iota(jnp.int32, (tall, 1), 0) + (start + pl.program_id(0) * tall)
    hit_a = slot_rows[0:1, :] == place
    hit_b = slot_rows[1:2, :] == place
    pick = jnp.where(hit_a | hit_b, 1.0, 0.0).astype(BF16)
    for k, source in enumerate(sources):
        found = mm(pick, source[...]).astype(BF16)
        out[:, k * size : (k + 1) * size, :] = found.reshape(group, size, width)
    if with_other:
        named = route_rows[...].astype(F32) + 1.0
        found = jnp.where(hit_a, named[1:2, :], jnp.where(hit_b, named[0:1, :], 0.0))
        column = jnp.sum(found, axis=1, keepdims=True) - 1.0
        last = len(sources) * size
        for g in range(group):
            turned = jnp.transpose(
                jnp.broadcast_to(column[g * size : (g + 1) * size, :], (size, LANES))
            )
            out[g, last : last + EXTRA, 0:size] = turned[0:EXTRA, :].astype(BF16)


def dispatch(slot_rows, route_rows, sources, experts, piece, with_other):
    total, width = sources[0].shape
    start, size = piece
    tall = size * len(sources) + (EXTRA if with_other else 0)
    group = 1 if with_other else 2
    return pl.pallas_call(
        partial(dispatch_kernel, start, size, with_other),
        grid=(experts // group,),
        in_specs=[
            whole((2, total)),
            whole((2, total)),
            *[whole((total, width)) for _ in sources],
        ],
        out_specs=pl.BlockSpec((group, tall, width), lambda e: (e, 0, 0)),
        out_shape=jax.ShapeDtypeStruct((experts, tall, width), BF16),
        compiler_params=params(1),
        name="dispatch",
        cost_estimate=cost(10),
    )(slot_rows, route_rows, *sources)


def stack_rows(length, width):
    return LANES * HEADS // width * ((length + 15) // 16 * 16)


def attention_kernel(
    experts, x, mask, small, wqkv, wout, triple, context, logs, residual, normed, gains
):
    @pl.when(pl.program_id(0) == 0)
    def _():
        gains[0:4, :] = gain_rows(small, experts)

    width = x.shape[1]
    length = x.shape[0]
    x_wide = x[...].astype(F32)
    unit, _ = norm_stats(x_wide)
    low = (unit * gains[0:1, :] + gains[1:2, :]).astype(BF16)
    mixed = mm(low, wqkv[...]).astype(BF16)
    triple[...] = mixed
    bias = jnp.where(mask[0] > 0, 0.0, NEGATIVE)
    lane = lane_iota(1, LANES)
    head_width = width // HEADS
    scale = head_width ** (-0.5)
    per = LANES // head_width
    gathered = jnp.zeros((length, LANES), F32)
    lanes_all = lane_iota(length, LANES)
    for group in range(HEADS // per):
        begin = group * LANES
        queries = mixed[:, begin : begin + LANES]
        keys = mixed[:, width + begin : width + begin + LANES]
        values = mixed[:, 2 * width + begin : 2 * width + begin + LANES]
        merged = jnp.zeros((length, LANES), F32)
        for inner in range(per):
            inside = (lane >= inner * head_width) & (lane < (inner + 1) * head_width)
            chosen = queries * jnp.where(inside, scale, 0.0).astype(BF16)
            scores = mm_nt(chosen, keys) + bias
            peak = jnp.max(scores, axis=-1, keepdims=True)
            raised = jnp.exp(scores - peak)
            sums = jnp.sum(raised, axis=-1, keepdims=True)
            found = mm(raised.astype(BF16), values) * (1.0 / sums)
            merged = jnp.where(inside, found, merged)
            gathered = jnp.where(
                lanes_all == group * per + inner, peak + jnp.log(sums), gathered
            )
        context[:, begin : begin + LANES] = merged.astype(BF16)
    logs[0] = jnp.transpose(gathered)[:HEADS, :]
    after = x_wide + mm(context[...], wout[...])
    residual[...] = after
    unit_b, _ = norm_stats(after)
    normed[...] = (unit_b * gains[2:3, :] + gains[3:4, :]).astype(BF16)


def small_spec(width):
    last = 4 * width // LANES
    return pl.BlockSpec((width, LANES), lambda i: (0, last), pipeline_mode=pl.Buffered(1))


def attention_forward(x, mask, dense, experts):
    total, width = x.shape
    images, length = mask.shape
    rows = lambda i: (i, 0)
    return pl.pallas_call(
        partial(attention_kernel, experts),
        grid=(images,),
        in_specs=[
            pl.BlockSpec((length, width), rows),
            pl.BlockSpec((1, 1, length), lambda i: (i, 0, 0)),
            small_spec(width),
            pl.BlockSpec((width, 3 * width), lambda i: (0, 0), pipeline_mode=pl.Buffered(1)),
            pl.BlockSpec((width, width), lambda i: (0, 3), pipeline_mode=pl.Buffered(1)),
        ],
        out_specs=[
            pl.BlockSpec((length, 3 * width), rows),
            pl.BlockSpec((length, width), rows),
            pl.BlockSpec((1, HEADS, length), lambda i: (i, 0, 0)),
            pl.BlockSpec((length, width), rows),
            pl.BlockSpec((length, width), rows),
        ],
        out_shape=[
            jax.ShapeDtypeStruct((total, 3 * width), BF16),
            jax.ShapeDtypeStruct((total, width), BF16),
            jax.ShapeDtypeStruct((images, HEADS, length), F32),
            jax.ShapeDtypeStruct((total, width), F32),
            jax.ShapeDtypeStruct((total, width), BF16),
        ],
        scratch_shapes=[pltpu.VMEM((8, width), F32)],
        compiler_params=params(1),
        name="attention_forward",
        cost_estimate=cost(17),
    )(x, mask.reshape(images, 1, length), dense, dense, dense)


def experts_kernel(block, more, *refs):
    if more:
        mixed, own, router, w_in, w_out, b_in, b_out, *rest = refs
        old_mine, old_mate, old_router, back, sent, dw_mine, dw_mate, drouter, *rest = rest
        *rest, rows = rest
        ups, shift = mixed, block

        @pl.when(pl.program_id(0) == 0)
        def _():
            for i in range(mixed.shape[0]):
                rows[i * block : (i + 1) * block, :] = mixed[i, 0:block, :]

        outs = (back, sent, 0)
        old = (old_mine, old_mate, old_router)
    else:
        rows, ups, own, router, w_in, w_out, b_in, b_out, *rest = refs
        ret, dw_mine, dw_mate, drouter, *rest = rest
        outs = (ret, ret, block)
        shift, old = 0, None
    experts_body(
        block, rows, ups, shift, own, router, w_in, w_out, b_in, b_out, old,
        outs, dw_mine, dw_mate, drouter, *rest,
    )


def experts_body(
    block, rows, ups, shift, own, router, w_in, w_out, b_in, b_out, old,
    outs, dw_mine, dw_mate, drouter,
    gate, weighted, made, pushed, hid, pre_g, other, db,
):
    f = pl.program_id(0)
    last = pl.num_programs(0) - 1
    total, width = rows.shape
    steps = total // block
    lane = lane_iota(1, LANES)

    @pl.when(f == 0)
    def _():
        own_hot = own[...] > 0.0

        def step(i, acc):
            at = pl.ds(pl.multiple_of(i * block, block), block)
            logits = mm(rows[at, :], router[...])
            mine = jnp.sum(jnp.where(own_hot, logits, 0.0), axis=1, keepdims=True)
            named = ups[i, shift + block : shift + block + EXTRA, 0:block].astype(F32)
            rival = jnp.transpose(named)[:, 0:1].astype(jnp.int32)
            other[at, :] = rival
            theirs = jnp.sum(jnp.where(lane == rival, logits, 0.0), axis=1, keepdims=True)
            share = 1.0 / (1.0 + jnp.exp(theirs - mine))
            gate[at, 0:1] = share
            gate[at, 1:2] = 1.0 / (1.0 + jnp.exp(mine - theirs))
            scaled = (share * ups[i, shift : shift + block, :].astype(F32)).astype(BF16)
            weighted[at, :] = scaled
            return acc + jnp.sum(scaled.astype(F32), axis=0, keepdims=True)

        db[...] = jnp.zeros_like(db)
        db[1:2, :] = lax.fori_loop(0, steps, step, jnp.zeros((1, width), F32), unroll=4)

    chunk = w_in.shape[1]
    hidden_share = (dw_mine.shape[1] - EXTRA) // 2
    per = hidden_share // chunk
    place = f % per
    biases = b_in[0, 0:1, :].astype(F32)
    bias = biases[:, 0:chunk]
    for k in range(1, per):
        bias = jnp.where(place == k, biases[:, k * chunk : (k + 1) * chunk], bias)

    big = total // BIG_STEPS

    def body(i, acc):
        at = pl.ds(pl.multiple_of(i * big, big), big)
        here = rows[at, :]
        u = mm_nt(here, w_in[0]) + bias
        inner = ROOT + (ROOT * CUBIC) * (u * u)
        share = 0.5 + 0.5 * jnp.tanh(u * inner)
        raised = u * share
        hidden = raised.astype(BF16)
        slope = share + raised * (1.0 - share) * (6.0 * inner - 4.0 * ROOT)
        hid[at, :] = hidden
        grad = mm_nt(weighted[at, :], w_out[0]) * slope
        low = grad.astype(BF16)
        pre_g[at, :] = low
        part = mm(hidden, w_out[0])
        part_b = mm(low, w_in[0])

        @pl.when(f == 0)
        def _():
            made[at, :] = part
            pushed[at, :] = part_b

        @pl.when(f > 0)
        def _():
            made[at, :] += part
            pushed[at, :] += part_b

        return acc + jnp.sum(grad, axis=0, keepdims=True)

    db_here = lax.fori_loop(0, BIG_STEPS, body, jnp.zeros((1, chunk), F32))
    for k in range(per):

        @pl.when(place == k)
        def _():
            db[0:1, k * chunk : (k + 1) * chunk] = db_here

    dw_out_here = mm_tn(hid[...], weighted[...])
    dw_in_here = mm_tn(pre_g[...], rows[...])

    def put(target, prior):
        spots = (
            (pl.ds(pl.multiple_of(place * chunk, chunk), chunk), dw_in_here),
            (pl.ds(pl.multiple_of(hidden_share + place * chunk, chunk), chunk), dw_out_here),
            (pl.ds(2 * hidden_share, EXTRA), db[...]),
        )
        for spot, value in spots:
            if prior is not None:
                value = value + prior[0, spot, :].astype(F32)
            target[0, spot, :] = value.astype(BF16)

    quarters = (last + 1) // per

    @pl.when(f // per < quarters // 2)
    def _():
        put(dw_mine, old and old[0])

    @pl.when(f // per >= quarters // 2)
    def _():
        put(dw_mate, old and old[1])

    @pl.when(f == last)
    def _():
        own_row = own[...]
        back, sent, after = outs

        def step(i, carry):
            at = pl.ds(pl.multiple_of(i * block, block), block)
            produced = (made[at, :] + b_out[...]).astype(BF16).astype(F32)
            share = gate[at, 0:1]
            sent[i, after : after + block, :] = (share * produced).astype(BF16)
            inner = jnp.sum(produced * ups[i, shift : shift + block, :].astype(F32), axis=1, keepdims=True)
            pull = share * gate[at, 1:2] * inner
            rival = other[at, :]
            spread = (pull * (own_row - jnp.where(lane == rival, 1.0, 0.0))).astype(BF16)
            back[i, 0:block, :] = (pushed[at, :] + mm_nt(spread, router[...])).astype(BF16)
            hid[at, 0:LANES] = spread
            return carry

        lax.fori_loop(0, steps, step, 0, unroll=8)
        drouter[...] = mm_tn(rows[...], hid[:, 0:LANES]) + (0.0 if old is None else old[2][...])


def run_experts(given, block, own, dense, weights, b_out, old):
    experts, _, width = given[0].shape
    total = experts * block
    quarters, double, _ = weights.shape
    share = (double - EXTRA) // 2
    chunk = min(share, 512)
    per = share // chunk
    half = quarters // 2
    at = lambda f: (f // per, f % per, 0)
    out_at = lambda f: (f // per, per + f % per, 0)
    bias_at = lambda f: (f // per, 2 * share // EXTRA, 0)
    mine_at = lambda f: (jnp.minimum(f // per, half - 1), 0, 0)
    mate_at = lambda f: (jnp.maximum(f // per - half, 0), 0, 0)
    steps = quarters * per
    dw_shape = jax.ShapeDtypeStruct((half, double, width), BF16)
    sums = [
        pl.BlockSpec((1, double, width), mine_at),
        pl.BlockSpec((1, double, width), mate_at),
        whole((width, LANES)),
    ]
    if old:
        given_specs = [whole(given[0].shape)]
        ret_shapes = [(experts, block, width)] * 2
        more_scratch = [pltpu.VMEM((total, width), BF16)]
    else:
        given = (given[0].reshape(total, width), given[1])
        given_specs = [whole(given[0].shape), whole(given[1].shape)]
        ret_shapes = [(experts, 2 * block, width)]
        more_scratch = []
    return pl.pallas_call(
        partial(experts_kernel, block, bool(old)),
        grid=(steps,),
        in_specs=given_specs
        + [
            whole((1, LANES)),
            small_spec(width),
            pl.BlockSpec((1, chunk, width), at),
            pl.BlockSpec((1, chunk, width), out_at),
            pl.BlockSpec((1, EXTRA, width), bias_at),
            whole((1, width)),
        ]
        + (sums if old else []),
        out_specs=[whole(r) for r in ret_shapes] + sums,
        out_shape=[jax.ShapeDtypeStruct(r, BF16) for r in ret_shapes]
        + [dw_shape, dw_shape, jax.ShapeDtypeStruct((width, LANES), F32)],
        scratch_shapes=[
            pltpu.VMEM((total, 2), F32),
            pltpu.VMEM((total, width), BF16),
            pltpu.VMEM((total, width), F32),
            pltpu.VMEM((total, width), F32),
            pltpu.VMEM((total, chunk), BF16),
            pltpu.VMEM((total, chunk), BF16),
            pltpu.VMEM((total, 1), jnp.int32),
            pltpu.VMEM((EXTRA, width), F32),
        ]
        + more_scratch,
        compiler_params=params(1),
        name="experts",
        cost_estimate=cost(50),
    )(*given, own, dense, weights, weights, weights, b_out, *old)


def backward_kernel(
    experts, x, mask, small, wqkv, wout, triple, context, logs, residual, up, slot, ret_a, ret_b, drouter, parity,
    input_grad, keep, give_a, give_b,
    tg, gains, dqkv, dwout, dgains, stack_k, stack_v, dq_t,
):
    step = pl.program_id(0)
    length, width = x.shape

    @pl.when(step == 0)
    def _():
        dqkv[...] = jnp.zeros_like(dqkv)
        dwout[...] = jnp.zeros_like(dwout)
        dgains[...] = jnp.zeros_like(dgains)
        gains[0:4, :] = gain_rows(small, experts)
        stack_k[...] = jnp.zeros_like(stack_k)
        stack_v[...] = jnp.zeros_like(stack_v)

    second_grad = gather_slots(slot, (ret_a, ret_b))
    unit_b, scale_b = norm_stats(residual[...])
    dgains[experts + 2 : experts + 3, :] += jnp.sum(second_grad * unit_b, axis=0, keepdims=True)
    dgains[experts + 3 : experts + 4, :] += jnp.sum(second_grad, axis=0, keepdims=True)
    residual_grad = up[...].astype(F32) + norm_back(second_grad, unit_b, scale_b, gains[2:3, :])
    residual_low = residual_grad.astype(BF16)
    dwout[...] += mm_tn(context[...], residual_low)
    context_grad = mm_nt(residual_low, wout[...]).astype(BF16)

    lane = lane_iota(1, LANES)
    head_width = width // HEADS
    scale = head_width ** (-0.5)
    per = LANES // head_width
    tall = stack_k.shape[0] // per
    hide_row = jnp.where(mask[0] > 0, 0.0, NEGATIVE)
    hide = jnp.transpose(jnp.broadcast_to(hide_row, (LANES, length)))[:, 0:1]
    hide = jnp.concatenate([hide, jnp.full((tall - length, 1), NEGATIVE, F32)], axis=0)
    for group in range(HEADS // per):
        begin = group * LANES
        queries = triple[:, begin : begin + LANES] * jnp.asarray(scale, BF16)
        keys = triple[:, width + begin : width + begin + LANES]
        values = triple[:, 2 * width + begin : 2 * width + begin + LANES]
        pulled = context_grad[:, begin : begin + LANES]
        for inner in range(per):
            inside = (lane >= inner * head_width) & (lane < (inner + 1) * head_width)
            only = jnp.where(inside, 1.0, 0.0).astype(BF16)
            stack_k[inner * tall : inner * tall + length, :] = keys * only
            stack_v[inner * tall : inner * tall + length, :] = values * only
        scores = mm_nt(stack_k[...], queries)
        prob_grad = mm_nt(stack_v[...], pulled)
        probs, score_grad = [], []
        for inner in range(per):
            rows = slice(inner * tall, (inner + 1) * tall)
            head = group * per + inner
            prob = jnp.exp(scores[rows, :] + (hide - logs[0, head : head + 1, :]))
            pull = prob_grad[rows, :]
            inner_sum = jnp.sum(prob * pull, axis=0, keepdims=True)
            probs.append(prob.astype(BF16))
            score_grad.append((prob * (pull - inner_sum)).astype(BF16))
        probs = jnp.concatenate(probs, axis=0)
        score_grad = jnp.concatenate(score_grad, axis=0)
        dk_all = mm(score_grad, queries)
        dv_all = mm(probs, pulled)
        dq_t[begin : begin + LANES, :] = mm(jnp.transpose(stack_k[...]), score_grad) * scale
        dk, dv = dk_all[0:length, :], dv_all[0:length, :]
        for inner in range(1, per):
            rows = slice(inner * tall, inner * tall + length)
            dk = jnp.where(lane >= inner * head_width, dk_all[rows, :], dk)
            dv = jnp.where(lane >= inner * head_width, dv_all[rows, :], dv)
        tg[:, width + begin : width + begin + LANES] = dk.astype(BF16)
        tg[:, 2 * width + begin : 2 * width + begin + LANES] = dv.astype(BF16)
    tg[:, 0:width] = jnp.transpose(dq_t[...]).astype(BF16)
    unit, scale_a = norm_stats(x[...].astype(F32))
    low = (unit * gains[0:1, :] + gains[1:2, :]).astype(BF16)
    dqkv[...] += mm_tn(low, tg[...])
    first_grad = mm_nt(tg[...], wqkv[...])
    dgains[experts + 0 : experts + 1, :] += jnp.sum(first_grad * unit, axis=0, keepdims=True)
    dgains[experts + 1 : experts + 2, :] += jnp.sum(first_grad, axis=0, keepdims=True)
    input_grad[...] = residual_grad + norm_back(first_grad, unit, scale_a, gains[0:1, :])

    @pl.when(step == pl.num_programs(0) - 1)
    def _():
        tail = drouter[...] + jnp.transpose(dgains[...])
        share = width // 4
        odd = parity[0, 0]
        for part in range(4):
            rows = slice(part * share, (part + 1) * share)
            spot = slice(part // 2 * share, (part // 2 + 1) * share)

            def put(target, spot):
                target[spot, : 3 * width] = dqkv[rows, :].astype(BF16)
                target[spot, 3 * width : 4 * width] = dwout[rows, :].astype(BF16)
                target[spot, 4 * width :] = tail[rows, :].astype(BF16)

            @pl.when(odd == part % 2)
            def _():
                put(keep, spot)

            @pl.when(odd != part % 2)
            def _():
                put(give_b if part // 2 else give_a, slice(0, share))


def attention_backward(
    x, mask, dense, triple, context, logs, residual, up, slot, ret, drouter, parity,
    experts,
):
    total, width = x.shape
    images, length = mask.shape
    rows = lambda i: (i, 0)
    return pl.pallas_call(
        partial(backward_kernel, experts),
        grid=(images,),
        in_specs=[
            pl.BlockSpec((length, width), rows),
            pl.BlockSpec((1, 1, length), lambda i: (i, 0, 0)),
            small_spec(width),
            pl.BlockSpec((width, 3 * width), lambda i: (0, 0), pipeline_mode=pl.Buffered(1)),
            pl.BlockSpec((width, width), lambda i: (0, 3), pipeline_mode=pl.Buffered(1)),
            pl.BlockSpec((length, 3 * width), rows),
            pl.BlockSpec((length, width), rows),
            pl.BlockSpec((1, HEADS, length), lambda i: (i, 0, 0)),
            pl.BlockSpec((length, width), rows),
            pl.BlockSpec((length, width), rows),
            pl.BlockSpec((length, 2), rows),
            *returned_specs(ret, 0),
            whole((width, LANES)),
            pl.BlockSpec(memory_space=pltpu.SMEM),
        ],
        out_specs=[
            pl.BlockSpec((length, width), rows),
            whole((width // 2, 4 * width + LANES)),
            whole((width // 4, 4 * width + LANES)),
            whole((width // 4, 4 * width + LANES)),
        ],
        out_shape=[
            jax.ShapeDtypeStruct((total, width), F32),
            jax.ShapeDtypeStruct((width // 2, 4 * width + LANES), BF16),
            jax.ShapeDtypeStruct((width // 4, 4 * width + LANES), BF16),
            jax.ShapeDtypeStruct((width // 4, 4 * width + LANES), BF16),
        ],
        scratch_shapes=[
            pltpu.VMEM((length, 3 * width), BF16),
            pltpu.VMEM((8, width), F32),
            pltpu.VMEM((width, 3 * width), F32),
            pltpu.VMEM((width, width), F32),
            pltpu.VMEM((LANES, width), F32),
            pltpu.VMEM((stack_rows(length, width), LANES), BF16),
            pltpu.VMEM((stack_rows(length, width), LANES), BF16),
            pltpu.VMEM((width, length), F32),
        ],
        compiler_params=params(1),
        name="attention_backward",
        cost_estimate=cost(50),
    )(
        x, mask.reshape(images, 1, length), dense, dense, dense, triple, context, logs, residual,
        up, slot, *ret, drouter, parity,
    )


def combine_kernel(slot, residual, ret_a, ret_b, out):
    out[...] = (residual[...] + gather_slots(slot, (ret_a, ret_b))).astype(BF16)


def combine(slot, residual, ret, block):
    total, width = residual.shape
    rows = lambda i: (i, 0)
    return pl.pallas_call(
        combine_kernel,
        grid=(total // block,),
        in_specs=[
            pl.BlockSpec((block, 2), rows),
            pl.BlockSpec((block, width), rows),
            *returned_specs(ret, 1),
        ],
        out_specs=pl.BlockSpec((block, width), rows),
        out_shape=jax.ShapeDtypeStruct((total, width), BF16),
        compiler_params=params(1),
        name="combine",
        cost_estimate=cost(10),
    )(slot, residual, *ret)


def unpack_kernel(experts, total, wqkv, wout, router, *gains):
    width = wout.shape[1]
    wqkv[...] = total[:, : 3 * width].astype(F32)
    wout[...] = total[:, 3 * width : 4 * width].astype(F32)
    turned = jnp.transpose(total[:, 4 * width :].astype(F32))
    router[...] = turned[0:experts, :]
    for k, gain in enumerate(gains):
        gain[...] = turned[experts + k : experts + k + 1, :]


def unpack(total, experts):
    share = total.shape[0]
    width = (total.shape[1] - LANES) // 4
    shapes = [(share, 3 * width), (share, width), (experts, share)] + [(1, share)] * 4
    return pl.pallas_call(
        partial(unpack_kernel, experts),
        out_shape=[jax.ShapeDtypeStruct(shape, F32) for shape in shapes],
        compiler_params=params(),
        name="unpack",
        cost_estimate=cost(2),
    )(total)


class PlainPlan:
    def __init__(self, seq, wt):
        self.seq, self.wt = seq, wt

    def own_id(self):
        return lax.axis_index("seq")

    def exchange(self, a):
        return lax.all_to_all(a, "seq", split_axis=0, concat_axis=0, tiled=True)

    def begin_dense(self, packed):
        return packed

    def gather_dense(self, packed, begun):
        return lax.all_gather(begun, "wt", axis=0, tiled=True)

    def begin_fetch(self, packed):
        return (packed,)

    def fetch(self, packed, begun):
        return lax.all_gather(begun[0], "wt", axis=0)

    def spread_out_bias(self, quarters):
        return quarters

    def begin_reduce(self, mine, mate):
        return (jnp.concatenate([mine, mate]).reshape(-1, mine.shape[-1]),)

    def reduce_expert(self, parts):
        (parts,) = parts
        return lax.psum_scatter(parts, "wt", scatter_dimension=0, tiled=True)

    def finish_expert(self, parts, received):
        return received.astype(F32)

    def parity(self):
        return jnp.zeros((1, 1), jnp.int32)

    def begin_dense_sum(self, keep, give_a, give_b):
        half = keep.shape[0] // 2
        grads = jnp.concatenate([keep[:half], give_a, keep[half:], give_b])
        return lax.psum_scatter(grads, "wt", scatter_dimension=0, tiled=True)

    def reduce_dense(self, part):
        return lax.psum(part, "seq")


class CubePlan:
    AXES = ("seq", "wt")

    def __init__(self, seq, wt):
        self.seq, self.wt = seq, wt
        self.levels = seq // 2
        places = [
            (z, y, x, c)
            for z in range(self.levels)
            for y in range(2)
            for x in range(2)
            for c in range(2)
        ]
        flat = self.flat
        self.cross = [(flat(*p), flat(p[0], p[1], 1 - p[2], p[3])) for p in places]
        self.core = [(flat(*p), flat(p[0], p[1], p[2], 1 - p[3])) for p in places]
        near = lambda p: p[2] == p[0] % 2
        away = lambda p: (p[0] ^ 2, p[1], 1 - p[0] % 2, p[3])
        home = lambda p: (p[0], p[1], p[0] % 2, p[3])
        self.first = [(flat(*p), flat(*(away(p) if near(p) else home(p)))) for p in places]
        self.second = [(flat(*p), flat(*away(p))) for p in places if not near(p)]
        self.groups = [
            [self.host(half, e, c) for e in range(seq)] for half in range(2) for c in range(2)
        ]

    def flat(self, z, y, x, c):
        return (z * 2 + y) * self.wt + x * 2 + c

    def host(self, half, expert, c):
        z, y = expert // 2, expert % 2
        if z // 2 == half:
            return self.flat(z, y, z % 2, c)
        return self.flat(z ^ 2, y, 1 - z % 2, c)

    def send(self, a, pairs):
        return lax.ppermute(a, self.AXES, pairs)

    def x_zero(self):
        return lax.axis_index("wt") < 2

    def odd_level(self):
        return lax.axis_index("seq") // 2 % 2 == 1

    def near(self):
        return self.x_zero() != self.odd_level()

    def core_zero(self):
        return lax.axis_index("wt") % 2 == 0

    def own_id(self):
        rank = lax.axis_index("seq")
        return jnp.where(self.near(), rank, rank ^ 4)

    def exchange(self, a):
        return lax.all_to_all(
            a, self.AXES, split_axis=0, concat_axis=0, axis_index_groups=self.groups, tiled=True
        )

    def begin_dense(self, packed):
        return self.send(packed, self.cross)

    def gather_dense(self, packed, far):
        mate = self.send(packed, self.core)
        far_mate = self.send(far, self.core)
        flip = self.x_zero()
        low, high = jnp.where(flip, packed, far), jnp.where(flip, far, packed)
        low_mate, high_mate = jnp.where(flip, mate, far_mate), jnp.where(flip, far_mate, mate)
        first = self.core_zero()
        return jnp.concatenate(
            [
                jnp.where(first, low, low_mate),
                jnp.where(first, low_mate, low),
                jnp.where(first, high, high_mate),
                jnp.where(first, high_mate, high),
            ],
            axis=0,
        )

    def begin_fetch(self, packed):
        return self.send(packed, self.first), self.send(packed, self.second)

    def fetch(self, packed, begun):
        got, got_b = begun
        flip = self.near()
        low = jnp.where(flip, packed, got)
        high = jnp.where(flip, got, got_b)
        return jnp.stack([low, high, self.send(low, self.core), self.send(high, self.core)])

    def spread_out_bias(self, quarters):
        mine, odd = self.core_zero(), self.odd_level()
        order = []
        for x in range(2):
            for c in range(2):
                same = mine == (c == 0)
                level = odd == (x == 1)
                order.append(
                    jnp.where(
                        same,
                        jnp.where(level, quarters[0], quarters[1]),
                        jnp.where(level, quarters[2], quarters[3]),
                    )
                )
        return jnp.stack(order)

    def begin_reduce(self, mine, mate):
        got = self.send(mate, self.core)
        low = (mine[0].astype(F32) + got[0].astype(F32)).astype(BF16)
        high = (mine[1].astype(F32) + got[1].astype(F32)).astype(BF16)
        return low, high, jnp.where(self.near(), high, low)

    def reduce_expert(self, parts):
        low, high, give = parts
        return self.send(give, self.first_back()), self.send(high, self.second)

    def finish_expert(self, parts, received):
        far, far_b = received
        return jnp.where(self.near(), parts[0], far_b).astype(F32) + far.astype(F32)

    def first_back(self):
        return [(b, a) for a, b in self.first]

    def parity(self):
        return (lax.axis_index("wt") % 2).reshape(1, 1)

    def begin_dense_sum(self, keep, *give):
        share = keep.shape[0] // 2
        low, high = (
            keep[k * share : (k + 1) * share].astype(F32) + self.send(v, self.core).astype(F32)
            for k, v in enumerate(give)
        )
        flip = self.x_zero()
        out = self.send(jnp.where(flip, high, low).astype(BF16), self.cross)
        mine = jnp.where(flip, low, high) + out.astype(F32)
        return mine.astype(BF16)

    def reduce_dense(self, mine):
        share, width = mine.shape
        pieces = mine.reshape(self.seq, share // self.seq, width)
        swap = lambda v: lax.all_to_all(v, "seq", split_axis=0, concat_axis=0, tiled=True)
        total = jnp.sum(swap(pieces).astype(F32), axis=0, keepdims=True).astype(BF16)
        spread = swap(jnp.broadcast_to(total, pieces.shape))
        return spread.reshape(share, width)


def plan_of(seq, wt):
    return CubePlan(seq, wt) if (seq, wt) == (8, 4) else PlainPlan(seq, wt)


def local(
    inputs,
    key_mask,
    routes,
    priority,
    capacity,
    attention_gain,
    attention_shift,
    query_key_value,
    attention_out,
    mixture_gain,
    mixture_shift,
    router_weight,
    expert_in,
    expert_in_bias,
    expert_out,
    expert_out_bias,
    cotangent,
):
    total, width = inputs.shape
    experts = capacity.shape[0]
    cap = 8 * max(1, total // (4 * experts))
    share = query_key_value.shape[0]
    hidden_share = expert_in.shape[1]
    plan = plan_of(lax.axis_size("seq"), lax.axis_size("wt"))

    tie = lax.optimization_barrier
    front = (cap // 2 + EXTRA - 1) // EXTRA * EXTRA
    parts = (front, cap - front)
    packed, *shards = pack(
        query_key_value, attention_out, router_weight.T,
        (attention_gain, attention_shift, mixture_gain, mixture_shift),
        expert_in[0], expert_out[0], expert_in_bias, expert_out_bias,
    )
    fetched = [plan.begin_fetch(shard) for shard in shards]
    far = plan.begin_dense(packed)
    own = (jnp.arange(LANES) == plan.own_id()).astype(F32)[None, :]
    route_rows = routes.T
    slot, slot_rows = make_slots(route_rows, priority, capacity, parts)
    slot_rows, far, fetched[0] = tie((slot_rows, far, fetched[0]))
    pieces = ((0, front), (experts * front, cap - front))
    send = partial(dispatch, slot_rows, route_rows)
    ups_a = send((cotangent,), experts, pieces[0], True)
    dense = plan.gather_dense(packed, far)
    dense, ups_a = tie((dense, ups_a))
    ups_a = plan.exchange(ups_a)

    triple, context, logs, residual, normed = attention_forward(inputs, key_mask, dense, experts)
    rows_a = send((normed,), experts, pieces[0], False)
    mixed_b = send((normed, cotangent), experts, pieces[1], True)
    rows_a, ups_a, fetched[1] = tie((rows_a, ups_a, fetched[1]))
    rows_a = plan.exchange(rows_a)
    weights = jnp.concatenate(
        [plan.fetch(*pair) for pair in zip(shards, fetched)], axis=1
    )
    b_out = plan.spread_out_bias(
        weights[:, 2 * hidden_share + 1, :share].astype(F32)
    ).reshape(1, width)
    rows_a, mixed_b, weights, b_out = tie((rows_a, mixed_b, weights, b_out))
    mixed_b = plan.exchange(mixed_b)
    ret_a, *sums = run_experts((rows_a, ups_a), parts[0], own, dense, weights, b_out, ())
    ret_a, mixed_b = tie((ret_a, mixed_b))
    ret_a = plan.exchange(ret_a)
    back_b, sent_b, *sums = run_experts(
        (mixed_b,), parts[1], own, dense, weights, b_out, tuple(sums)
    )
    back_b, ret_a = tie((back_b, ret_a))
    back_b = plan.exchange(back_b)
    halves = plan.begin_reduce(*sums[:2])
    back_b, sent_b, halves = tie((back_b, sent_b, halves))
    sent_b = plan.exchange(sent_b)
    received = plan.reduce_expert(halves)
    ret_a = ret_a.reshape(experts, 2, front, width)
    input_grad, *grads = attention_backward(
        inputs, key_mask, dense, triple, context, logs, residual, cotangent, slot,
        (ret_a, back_b), sums[2], plan.parity(), experts,
    )
    grads, received = tie((grads, received))
    mine = plan.begin_dense_sum(*grads)
    mine, sent_b = tie((mine, sent_b))
    shard = plan.finish_expert(halves, received)
    done = plan.reduce_dense(mine)
    block_output = combine(slot, residual, (ret_a, sent_b), 200)
    dqkv, dwout, drouter, *dgains = unpack(done, experts)
    dgains = [g.reshape(share) for g in dgains]
    rank = lax.axis_index("wt")
    return (
        block_output,
        input_grad,
        dgains[0],
        dgains[1],
        dqkv,
        dwout,
        dgains[2],
        dgains[3],
        drouter.T,
        shard[None, :hidden_share],
        shard[2 * hidden_share, :hidden_share][None],
        shard[None, hidden_share : 2 * hidden_share],
        lax.dynamic_slice(shard[2 * hidden_share + 1], (rank * share,), (share,))[None],
    )


def solution(mesh):
    both = P(("seq", "wt"), None)
    placed = (
        both,
        both,
        both,
        both,
        P(),
        P("wt"),
        P("wt"),
        P("wt", None),
        P("wt", None),
        P("wt"),
        P("wt"),
        P("wt", None),
        P("seq", "wt", None),
        P("seq", "wt"),
        P("seq", "wt", None),
        P("seq", "wt"),
        both,
    )
    return jax.shard_map(
        local,
        mesh=mesh,
        in_specs=placed,
        out_specs=(
            both,
            both,
            P("wt"),
            P("wt"),
            P("wt", None),
            P("wt", None),
            P("wt"),
            P("wt"),
            P("wt", None),
            P("seq", "wt", None),
            P("seq", "wt"),
            P("seq", "wt", None),
            P("seq", "wt"),
        ),
        check_vma=False,
    )
```

```python
from functools import partial

import jax
import jax.numpy as jnp
from jax import lax
from jax.experimental import pallas as pl
from jax.experimental.pallas import tpu as pltpu
from jax.sharding import PartitionSpec as P

HEADS = 8
NEGATIVE = -1e30
EPSILON = 1e-06
LANES = 128
BIG_STEPS = 2
VMEM_BYTES = 60 * 1024 * 1024
F32 = jnp.float32
BF16 = jnp.bfloat16
ROOT = 0.7978845608028654
CUBIC = 0.044715

NT = (((1,), (1,)), ((), ()))
TN = (((0,), (0,)), ((), ()))


def mm(a, b):
    return jnp.dot(a, b, preferred_element_type=F32)


def mm_nt(a, b):
    return lax.dot_general(a, b, NT, preferred_element_type=F32)


def mm_tn(a, b):
    return lax.dot_general(a, b, TN, preferred_element_type=F32)


def params(steps=0):
    return pltpu.CompilerParams(
        dimension_semantics=("arbitrary",) * steps if steps else None,
        vmem_limit_bytes=VMEM_BYTES,
    )


def cost(micros):
    return pl.CostEstimate(
        flops=int(micros * 1.0e7), bytes_accessed=int(micros * 1.0e4), transcendentals=0
    )


def gain_rows(small, experts):
    turned = jnp.transpose(small[...].astype(F32))
    return turned[experts : experts + 4, :]


def whole(shape):
    zeros = (0,) * len(shape)
    return pl.BlockSpec(shape, lambda *_: zeros, pipeline_mode=pl.Buffered(1))


def gather_slots(slot, parts):
    found = None
    start = 0
    for piece in parts:
        rows = piece[...].reshape(-1, piece.shape[-1])
        lanes = lane_iota(1, rows.shape[0]) + start
        start += rows.shape[0]
        pick = jnp.where((lanes == slot[:, 0:1]) | (lanes == slot[:, 1:2]), 1.0, 0.0)
        piece = jnp.dot(pick.astype(BF16), rows, preferred_element_type=F32)
        found = piece if found is None else found + piece
    return found


def returned_specs(ret, which):
    both, alone = ret
    experts, _, size, width = both.shape
    spot = lambda *_: (0, which, 0, 0)
    return [
        pl.BlockSpec((experts, None, size, width), spot, pipeline_mode=pl.Buffered(1)),
        whole(alone.shape),
    ]


def lane_iota(rows, width):
    return lax.broadcasted_iota(jnp.int32, (rows, width), 1)


def norm_stats(values):
    row_mean = jnp.mean(values, axis=-1, keepdims=True)
    offsets = values - row_mean
    spread = jnp.mean(offsets * offsets, axis=-1, keepdims=True)
    scale = lax.rsqrt(spread + EPSILON)
    return offsets * scale, scale


def norm_back(grad, unit, scale, gain):
    weighted = grad * gain
    first = jnp.mean(weighted, axis=-1, keepdims=True)
    second = jnp.mean(weighted * unit, axis=-1, keepdims=True)
    return scale * (weighted - first - unit * second)


EXTRA = 16


def pack_kernel(wqkv, wout, router, ga, sa, gm, sm, w_in, w_out, b_in, b_out, dense, *refs):
    *pieces, tail = refs
    width = wout.shape[1]
    experts = router.shape[0]
    share = wout.shape[0]
    hidden = w_in.shape[0]
    dense[:, : 3 * width] = wqkv[...]
    dense[:, 3 * width : 4 * width] = wout[...]
    tail[...] = jnp.zeros_like(tail)
    tail[0:experts, 0:share] = router[...].astype(F32)
    for k, row in enumerate((ga, sa, gm, sm)):
        tail[experts + k : experts + k + 1, 0:share] = row[...].astype(F32)
    columns = jnp.transpose(tail[0:LANES, 0:LANES])[:share, :]
    dense[:, 4 * width :] = columns.astype(BF16)
    sources = ((w_in, 0), (w_out, hidden))
    start = 0
    for piece in pieces:
        stop = start + piece.shape[0]
        for source, base in sources:
            low, high = max(start, base), min(stop, base + hidden)
            if low < high:
                piece[low - start : high - start, :] = source[low - base : high - base, :]
        start = stop
    tail[0:EXTRA, :] = jnp.zeros((EXTRA, width), F32)
    tail[0:1, 0:hidden] = b_in[...].astype(F32)
    tail[1:2, 0:share] = b_out[...].astype(F32)
    pieces[-1][pieces[-1].shape[0] - EXTRA :, :] = tail[0:EXTRA, :].astype(BF16)


def pack(wqkv, wout, router, gains, w_in, w_out, b_in, b_out):
    share, width = wout.shape
    hidden = w_in.shape[0]
    double = 2 * hidden + EXTRA
    cuts = [0] + [double * part // 100 // EXTRA * EXTRA for part in (47,)] + [double]
    sizes = [high - low for low, high in zip(cuts, cuts[1:])]
    return pl.pallas_call(
        pack_kernel,
        out_shape=[
            jax.ShapeDtypeStruct((share, 4 * width + LANES), BF16),
            *[jax.ShapeDtypeStruct((n, width), BF16) for n in sizes],
        ],
        scratch_shapes=[pltpu.VMEM((LANES, width), F32)],
        compiler_params=params(),
        name="pack",
        cost_estimate=cost(3),
    )(wqkv, wout, router, *[g[None, :] for g in gains], w_in, w_out, b_in, b_out)


def slots_kernel(parts, block, prow, routes, capacity, out, out_rows, poscol, hot, limits, wide):
    total = routes.shape[1]
    experts = capacity.shape[1]
    steps = total // block
    half = LANES // 2
    sub = lax.broadcasted_iota(jnp.int32, (LANES, 1), 0)
    hot_t = jnp.where((routes[0:1, :] == sub) | (routes[1:2, :] + half == sub), 1.0, 0.0)
    hot[...] = jnp.transpose(hot_t).astype(BF16)
    limits[...] = jnp.zeros_like(limits)
    limits[:, 0:experts] = capacity[...].astype(F32)
    limits[:, half : half + experts] = capacity[...].astype(F32)
    lane = lane_iota(1, LANES)
    index = lax.broadcasted_iota(jnp.int32, (total, LANES), 0)
    digits = jnp.where(
        lane_iota(total, LANES) == 0, index // 8, jnp.where(lane_iota(total, LANES) == 1, index % 8, 0)
    ).astype(F32).astype(BF16)

    def find(i, carry):
        at = pl.ds(pl.multiple_of(i * block, block), block)
        token = lax.broadcasted_iota(jnp.int32, (block, 1), 0) + i * block
        hit = jnp.where(prow[...] == token, 1.0, 0.0).astype(BF16)
        poscol[at, :] = mm(hit, digits)
        return carry

    lax.fori_loop(0, steps, find, 0)
    turned = jnp.transpose(poscol[...])
    posrow = turned[0:1, :] * 8.0 + turned[1:2, :]
    low_lanes = lane < half
    seen = jnp.sum(hot[...].astype(F32), axis=0, keepdims=True)
    seen_b = jnp.where(low_lanes, 0.0, pltpu.roll(jnp.broadcast_to(seen, (8, LANES)), half, 1)[0:1, :])
    expert = jnp.where(low_lanes, lane, lane - half)
    front, rest = parts
    base = (expert * front + 1).astype(F32)
    base_b = (experts * front + expert * rest - front + 1).astype(F32)

    def step(i, carry):
        at = pl.ds(pl.multiple_of(i * block, block), block)
        mine = poscol[at, 0:1] * 8.0 + poscol[at, 1:2]
        earlier = jnp.where(posrow < mine, 1.0, 0.0).astype(BF16)
        own = hot[at, :].astype(F32)
        place = mm(earlier, hot[...]) + seen_b
        number = place + jnp.where(place < front, base, base_b)
        value = jnp.where(place < limits[...], number, 0.0) * own
        slot_a = jnp.sum(jnp.where(low_lanes, value, 0.0), axis=1, keepdims=True) - 1.0
        slot_b = jnp.sum(jnp.where(low_lanes, 0.0, value), axis=1, keepdims=True) - 1.0
        wide[at, :] = jnp.where(lane == 0, slot_a, slot_b)
        out[at, :] = jnp.where(lane_iota(1, 2) == 0, slot_a, slot_b).astype(jnp.int32)
        return carry

    lax.fori_loop(0, steps, step, 0)
    out_rows[...] = jnp.transpose(wide[...])[0:2, :].astype(jnp.int32)


def make_slots(route_rows, priority, capacity, parts):
    total = route_rows.shape[1]
    return pl.pallas_call(
        partial(slots_kernel, parts, 400),
        out_shape=[
            jax.ShapeDtypeStruct((total, 2), jnp.int32),
            jax.ShapeDtypeStruct((2, total), jnp.int32),
        ],
        scratch_shapes=[
            pltpu.VMEM((total, LANES), F32),
            pltpu.VMEM((total, LANES), BF16),
            pltpu.VMEM((1, LANES), F32),
            pltpu.VMEM((total, LANES), F32),
        ],
        compiler_params=params(),
        name="slots",
        cost_estimate=cost(8),
    )(priority, route_rows, capacity[None, :])


def dispatch_kernel(start, size, with_other, slot_rows, route_rows, *refs):
    *sources, out = refs
    group = out.shape[0]
    tall = group * size
    width = out.shape[2]
    place = lax.broadcasted_iota(jnp.int32, (tall, 1), 0) + (start + pl.program_id(0) * tall)
    hit_a = slot_rows[0:1, :] == place
    hit_b = slot_rows[1:2, :] == place
    pick = jnp.where(hit_a | hit_b, 1.0, 0.0).astype(BF16)
    for k, source in enumerate(sources):
        found = mm(pick, source[...]).astype(BF16)
        out[:, k * size : (k + 1) * size, :] = found.reshape(group, size, width)
    if with_other:
        named = route_rows[...].astype(F32) + 1.0
        found = jnp.where(hit_a, named[1:2, :], jnp.where(hit_b, named[0:1, :], 0.0))
        column = jnp.sum(found, axis=1, keepdims=True) - 1.0
        last = len(sources) * size
        for g in range(group):
            turned = jnp.transpose(
                jnp.broadcast_to(column[g * size : (g + 1) * size, :], (size, LANES))
            )
            out[g, last : last + EXTRA, 0:size] = turned[0:EXTRA, :].astype(BF16)


def dispatch(slot_rows, route_rows, sources, experts, piece, with_other):
    total, width = sources[0].shape
    start, size = piece
    tall = size * len(sources) + (EXTRA if with_other else 0)
    group = 1 if with_other else 2
    return pl.pallas_call(
        partial(dispatch_kernel, start, size, with_other),
        grid=(experts // group,),
        in_specs=[
            whole((2, total)),
            whole((2, total)),
            *[whole((total, width)) for _ in sources],
        ],
        out_specs=pl.BlockSpec((group, tall, width), lambda e: (e, 0, 0)),
        out_shape=jax.ShapeDtypeStruct((experts, tall, width), BF16),
        compiler_params=params(1),
        name="dispatch",
        cost_estimate=cost(10),
    )(slot_rows, route_rows, *sources)


def stack_rows(length, width):
    return LANES * HEADS // width * ((length + 15) // 16 * 16)


def attention_kernel(
    experts, x, mask, small, wqkv, wout, triple, context, logs, residual, normed, gains
):
    @pl.when(pl.program_id(0) == 0)
    def _():
        gains[0:4, :] = gain_rows(small, experts)

    width = x.shape[1]
    length = x.shape[0]
    x_wide = x[...].astype(F32)
    unit, _ = norm_stats(x_wide)
    low = (unit * gains[0:1, :] + gains[1:2, :]).astype(BF16)
    mixed = mm(low, wqkv[...]).astype(BF16)
    triple[...] = mixed
    bias = jnp.where(mask[0] > 0, 0.0, NEGATIVE)
    lane = lane_iota(1, LANES)
    head_width = width // HEADS
    scale = head_width ** (-0.5)
    per = LANES // head_width
    gathered = jnp.zeros((length, LANES), F32)
    lanes_all = lane_iota(length, LANES)
    for group in range(HEADS // per):
        begin = group * LANES
        queries = mixed[:, begin : begin + LANES]
        keys = mixed[:, width + begin : width + begin + LANES]
        values = mixed[:, 2 * width + begin : 2 * width + begin + LANES]
        merged = jnp.zeros((length, LANES), F32)
        for inner in range(per):
            inside = (lane >= inner * head_width) & (lane < (inner + 1) * head_width)
            chosen = queries * jnp.where(inside, scale, 0.0).astype(BF16)
            scores = mm_nt(chosen, keys) + bias
            peak = jnp.max(scores, axis=-1, keepdims=True)
            raised = jnp.exp(scores - peak)
            sums = jnp.sum(raised, axis=-1, keepdims=True)
            found = mm(raised.astype(BF16), values) * (1.0 / sums)
            merged = jnp.where(inside, found, merged)
            gathered = jnp.where(
                lanes_all == group * per + inner, peak + jnp.log(sums), gathered
            )
        context[:, begin : begin + LANES] = merged.astype(BF16)
    logs[0] = jnp.transpose(gathered)[:HEADS, :]
    after = x_wide + mm(context[...], wout[...])
    residual[...] = after
    unit_b, _ = norm_stats(after)
    normed[...] = (unit_b * gains[2:3, :] + gains[3:4, :]).astype(BF16)


def small_spec(width):
    last = 4 * width // LANES
    return pl.BlockSpec((width, LANES), lambda i: (0, last), pipeline_mode=pl.Buffered(1))


def attention_forward(x, mask, dense, experts):
    total, width = x.shape
    images, length = mask.shape
    rows = lambda i: (i, 0)
    return pl.pallas_call(
        partial(attention_kernel, experts),
        grid=(images,),
        in_specs=[
            pl.BlockSpec((length, width), rows),
            pl.BlockSpec((1, 1, length), lambda i: (i, 0, 0)),
            small_spec(width),
            pl.BlockSpec((width, 3 * width), lambda i: (0, 0), pipeline_mode=pl.Buffered(1)),
            pl.BlockSpec((width, width), lambda i: (0, 3), pipeline_mode=pl.Buffered(1)),
        ],
        out_specs=[
            pl.BlockSpec((length, 3 * width), rows),
            pl.BlockSpec((length, width), rows),
            pl.BlockSpec((1, HEADS, length), lambda i: (i, 0, 0)),
            pl.BlockSpec((length, width), rows),
            pl.BlockSpec((length, width), rows),
        ],
        out_shape=[
            jax.ShapeDtypeStruct((total, 3 * width), BF16),
            jax.ShapeDtypeStruct((total, width), BF16),
            jax.ShapeDtypeStruct((images, HEADS, length), F32),
            jax.ShapeDtypeStruct((total, width), F32),
            jax.ShapeDtypeStruct((total, width), BF16),
        ],
        scratch_shapes=[pltpu.VMEM((8, width), F32)],
        compiler_params=params(1),
        name="attention_forward",
        cost_estimate=cost(17),
    )(x, mask.reshape(images, 1, length), dense, dense, dense)


def experts_kernel(block, more, *refs):
    if more:
        mixed, own, router, w_in, w_out, b_in, b_out, *rest = refs
        old_mine, old_mate, old_router, back, sent, dw_mine, dw_mate, drouter, *rest = rest
        *rest, rows = rest
        ups, shift = mixed, block

        @pl.when(pl.program_id(0) == 0)
        def _():
            for i in range(mixed.shape[0]):
                rows[i * block : (i + 1) * block, :] = mixed[i, 0:block, :]

        outs = (back, sent, 0)
        old = (old_mine, old_mate, old_router)
    else:
        rows, ups, own, router, w_in, w_out, b_in, b_out, *rest = refs
        ret, dw_mine, dw_mate, drouter, *rest = rest
        outs = (ret, ret, block)
        shift, old = 0, None
    experts_body(
        block, rows, ups, shift, own, router, w_in, w_out, b_in, b_out, old,
        outs, dw_mine, dw_mate, drouter, *rest,
    )


def experts_body(
    block, rows, ups, shift, own, router, w_in, w_out, b_in, b_out, old,
    outs, dw_mine, dw_mate, drouter,
    gate, weighted, made, pushed, hid, pre_g, other, db,
):
    f = pl.program_id(0)
    last = pl.num_programs(0) - 1
    total, width = rows.shape
    steps = total // block
    lane = lane_iota(1, LANES)

    @pl.when(f == 0)
    def _():
        own_hot = own[...] > 0.0

        def step(i, acc):
            at = pl.ds(pl.multiple_of(i * block, block), block)
            logits = mm(rows[at, :], router[...])
            mine = jnp.sum(jnp.where(own_hot, logits, 0.0), axis=1, keepdims=True)
            named = ups[i, shift + block : shift + block + EXTRA, 0:block].astype(F32)
            rival = jnp.transpose(named)[:, 0:1].astype(jnp.int32)
            other[at, :] = rival
            theirs = jnp.sum(jnp.where(lane == rival, logits, 0.0), axis=1, keepdims=True)
            share = 1.0 / (1.0 + jnp.exp(theirs - mine))
            gate[at, 0:1] = share
            gate[at, 1:2] = 1.0 / (1.0 + jnp.exp(mine - theirs))
            scaled = (share * ups[i, shift : shift + block, :].astype(F32)).astype(BF16)
            weighted[at, :] = scaled
            return acc + jnp.sum(scaled.astype(F32), axis=0, keepdims=True)

        db[...] = jnp.zeros_like(db)
        db[1:2, :] = lax.fori_loop(0, steps, step, jnp.zeros((1, width), F32), unroll=4)

    chunk = w_in.shape[1]
    hidden_share = (dw_mine.shape[1] - EXTRA) // 2
    per = hidden_share // chunk
    place = f % per
    biases = b_in[0, 0:1, :].astype(F32)
    bias = biases[:, 0:chunk]
    for k in range(1, per):
        bias = jnp.where(place == k, biases[:, k * chunk : (k + 1) * chunk], bias)

    big = total // BIG_STEPS

    def body(i, acc):
        at = pl.ds(pl.multiple_of(i * big, big), big)
        here = rows[at, :]
        u = mm_nt(here, w_in[0]) + bias
        inner = ROOT + (ROOT * CUBIC) * (u * u)
        share = 0.5 + 0.5 * jnp.tanh(u * inner)
        raised = u * share
        hidden = raised.astype(BF16)
        slope = share + raised * (1.0 - share) * (6.0 * inner - 4.0 * ROOT)
        hid[at, :] = hidden
        grad = mm_nt(weighted[at, :], w_out[0]) * slope
        low = grad.astype(BF16)
        pre_g[at, :] = low
        part = mm(hidden, w_out[0])
        part_b = mm(low, w_in[0])

        @pl.when(f == 0)
        def _():
            made[at, :] = part
            pushed[at, :] = part_b

        @pl.when(f > 0)
        def _():
            made[at, :] += part
            pushed[at, :] += part_b

        return acc + jnp.sum(grad, axis=0, keepdims=True)

    db_here = lax.fori_loop(0, BIG_STEPS, body, jnp.zeros((1, chunk), F32))
    for k in range(per):

        @pl.when(place == k)
        def _():
            db[0:1, k * chunk : (k + 1) * chunk] = db_here

    dw_out_here = mm_tn(hid[...], weighted[...])
    dw_in_here = mm_tn(pre_g[...], rows[...])

    def put(target, prior):
        spots = (
            (pl.ds(pl.multiple_of(place * chunk, chunk), chunk), dw_in_here),
            (pl.ds(pl.multiple_of(hidden_share + place * chunk, chunk), chunk), dw_out_here),
            (pl.ds(2 * hidden_share, EXTRA), db[...]),
        )
        for spot, value in spots:
            if prior is not None:
                value = value + prior[0, spot, :].astype(F32)
            target[0, spot, :] = value.astype(BF16)

    quarters = (last + 1) // per

    @pl.when(f // per < quarters // 2)
    def _():
        put(dw_mine, old and old[0])

    @pl.when(f // per >= quarters // 2)
    def _():
        put(dw_mate, old and old[1])

    @pl.when(f == last)
    def _():
        own_row = own[...]
        back, sent, after = outs

        def step(i, carry):
            at = pl.ds(pl.multiple_of(i * block, block), block)
            produced = (made[at, :] + b_out[...]).astype(BF16).astype(F32)
            share = gate[at, 0:1]
            sent[i, after : after + block, :] = (share * produced).astype(BF16)
            inner = jnp.sum(produced * ups[i, shift : shift + block, :].astype(F32), axis=1, keepdims=True)
            pull = share * gate[at, 1:2] * inner
            rival = other[at, :]
            spread = (pull * (own_row - jnp.where(lane == rival, 1.0, 0.0))).astype(BF16)
            back[i, 0:block, :] = (pushed[at, :] + mm_nt(spread, router[...])).astype(BF16)
            hid[at, 0:LANES] = spread
            return carry

        lax.fori_loop(0, steps, step, 0, unroll=4)
        drouter[...] = mm_tn(rows[...], hid[:, 0:LANES]) + (0.0 if old is None else old[2][...])


def run_experts(given, block, own, dense, weights, b_out, old):
    experts, _, width = given[0].shape
    total = experts * block
    quarters, double, _ = weights.shape
    share = (double - EXTRA) // 2
    chunk = min(share, 512)
    per = share // chunk
    half = quarters // 2
    at = lambda f: (f // per, f % per, 0)
    out_at = lambda f: (f // per, per + f % per, 0)
    bias_at = lambda f: (f // per, 2 * share // EXTRA, 0)
    mine_at = lambda f: (jnp.minimum(f // per, half - 1), 0, 0)
    mate_at = lambda f: (jnp.maximum(f // per - half, 0), 0, 0)
    steps = quarters * per
    dw_shape = jax.ShapeDtypeStruct((half, double, width), BF16)
    sums = [
        pl.BlockSpec((1, double, width), mine_at),
        pl.BlockSpec((1, double, width), mate_at),
        whole((width, LANES)),
    ]
    if old:
        given_specs = [whole(given[0].shape)]
        ret_shapes = [(experts, block, width)] * 2
        more_scratch = [pltpu.VMEM((total, width), BF16)]
    else:
        given = (given[0].reshape(total, width), given[1])
        given_specs = [whole(given[0].shape), whole(given[1].shape)]
        ret_shapes = [(experts, 2 * block, width)]
        more_scratch = []
    return pl.pallas_call(
        partial(experts_kernel, block, bool(old)),
        grid=(steps,),
        in_specs=given_specs
        + [
            whole((1, LANES)),
            small_spec(width),
            pl.BlockSpec((1, chunk, width), at),
            pl.BlockSpec((1, chunk, width), out_at),
            pl.BlockSpec((1, EXTRA, width), bias_at),
            whole((1, width)),
        ]
        + (sums if old else []),
        out_specs=[whole(r) for r in ret_shapes] + sums,
        out_shape=[jax.ShapeDtypeStruct(r, BF16) for r in ret_shapes]
        + [dw_shape, dw_shape, jax.ShapeDtypeStruct((width, LANES), F32)],
        scratch_shapes=[
            pltpu.VMEM((total, 2), F32),
            pltpu.VMEM((total, width), BF16),
            pltpu.VMEM((total, width), F32),
            pltpu.VMEM((total, width), F32),
            pltpu.VMEM((total, chunk), BF16),
            pltpu.VMEM((total, chunk), BF16),
            pltpu.VMEM((total, 1), jnp.int32),
            pltpu.VMEM((EXTRA, width), F32),
        ]
        + more_scratch,
        compiler_params=params(1),
        name="experts",
        cost_estimate=cost(50),
    )(*given, own, dense, weights, weights, weights, b_out, *old)


def backward_kernel(
    experts, x, mask, small, wqkv, wout, triple, context, logs, residual, up, slot, ret_a, ret_b, drouter, parity,
    input_grad, keep, give_a, give_b,
    tg, gains, dqkv, dwout, dgains, stack_k, stack_v, dq_t,
):
    step = pl.program_id(0)
    length, width = x.shape

    @pl.when(step == 0)
    def _():
        dqkv[...] = jnp.zeros_like(dqkv)
        dwout[...] = jnp.zeros_like(dwout)
        dgains[...] = jnp.zeros_like(dgains)
        gains[0:4, :] = gain_rows(small, experts)
        stack_k[...] = jnp.zeros_like(stack_k)
        stack_v[...] = jnp.zeros_like(stack_v)

    second_grad = gather_slots(slot, (ret_a, ret_b))
    unit_b, scale_b = norm_stats(residual[...])
    dgains[experts + 2 : experts + 3, :] += jnp.sum(second_grad * unit_b, axis=0, keepdims=True)
    dgains[experts + 3 : experts + 4, :] += jnp.sum(second_grad, axis=0, keepdims=True)
    residual_grad = up[...].astype(F32) + norm_back(second_grad, unit_b, scale_b, gains[2:3, :])
    residual_low = residual_grad.astype(BF16)
    dwout[...] += mm_tn(context[...], residual_low)
    context_grad = mm_nt(residual_low, wout[...]).astype(BF16)

    lane = lane_iota(1, LANES)
    head_width = width // HEADS
    scale = head_width ** (-0.5)
    per = LANES // head_width
    tall = stack_k.shape[0] // per
    hide_row = jnp.where(mask[0] > 0, 0.0, NEGATIVE)
    hide = jnp.transpose(jnp.broadcast_to(hide_row, (LANES, length)))[:, 0:1]
    hide = jnp.concatenate([hide, jnp.full((tall - length, 1), NEGATIVE, F32)], axis=0)
    for group in range(HEADS // per):
        begin = group * LANES
        queries = triple[:, begin : begin + LANES] * jnp.asarray(scale, BF16)
        keys = triple[:, width + begin : width + begin + LANES]
        values = triple[:, 2 * width + begin : 2 * width + begin + LANES]
        pulled = context_grad[:, begin : begin + LANES]
        for inner in range(per):
            inside = (lane >= inner * head_width) & (lane < (inner + 1) * head_width)
            only = jnp.where(inside, 1.0, 0.0).astype(BF16)
            stack_k[inner * tall : inner * tall + length, :] = keys * only
            stack_v[inner * tall : inner * tall + length, :] = values * only
        scores = mm_nt(stack_k[...], queries)
        prob_grad = mm_nt(stack_v[...], pulled)
        probs, score_grad = [], []
        for inner in range(per):
            rows = slice(inner * tall, (inner + 1) * tall)
            head = group * per + inner
            prob = jnp.exp(scores[rows, :] + (hide - logs[0, head : head + 1, :]))
            pull = prob_grad[rows, :]
            inner_sum = jnp.sum(prob * pull, axis=0, keepdims=True)
            probs.append(prob.astype(BF16))
            score_grad.append((prob * (pull - inner_sum)).astype(BF16))
        probs = jnp.concatenate(probs, axis=0)
        score_grad = jnp.concatenate(score_grad, axis=0)
        dk_all = mm(score_grad, queries)
        dv_all = mm(probs, pulled)
        dq_t[begin : begin + LANES, :] = mm(jnp.transpose(stack_k[...]), score_grad) * scale
        dk, dv = dk_all[0:length, :], dv_all[0:length, :]
        for inner in range(1, per):
            rows = slice(inner * tall, inner * tall + length)
            dk = jnp.where(lane >= inner * head_width, dk_all[rows, :], dk)
            dv = jnp.where(lane >= inner * head_width, dv_all[rows, :], dv)
        tg[:, width + begin : width + begin + LANES] = dk.astype(BF16)
        tg[:, 2 * width + begin : 2 * width + begin + LANES] = dv.astype(BF16)
    tg[:, 0:width] = jnp.transpose(dq_t[...]).astype(BF16)
    unit, scale_a = norm_stats(x[...].astype(F32))
    low = (unit * gains[0:1, :] + gains[1:2, :]).astype(BF16)
    dqkv[...] += mm_tn(low, tg[...])
    first_grad = mm_nt(tg[...], wqkv[...])
    dgains[experts + 0 : experts + 1, :] += jnp.sum(first_grad * unit, axis=0, keepdims=True)
    dgains[experts + 1 : experts + 2, :] += jnp.sum(first_grad, axis=0, keepdims=True)
    input_grad[...] = residual_grad + norm_back(first_grad, unit, scale_a, gains[0:1, :])

    @pl.when(step == pl.num_programs(0) - 1)
    def _():
        tail = drouter[...] + jnp.transpose(dgains[...])
        share = width // 4
        odd = parity[0, 0]
        for part in range(4):
            rows = slice(part * share, (part + 1) * share)
            spot = slice(part // 2 * share, (part // 2 + 1) * share)

            def put(target, spot):
                target[spot, : 3 * width] = dqkv[rows, :].astype(BF16)
                target[spot, 3 * width : 4 * width] = dwout[rows, :].astype(BF16)
                target[spot, 4 * width :] = tail[rows, :].astype(BF16)

            @pl.when(odd == part % 2)
            def _():
                put(keep, spot)

            @pl.when(odd != part % 2)
            def _():
                put(give_b if part // 2 else give_a, slice(0, share))


def attention_backward(
    x, mask, dense, triple, context, logs, residual, up, slot, ret, drouter, parity,
    experts,
):
    total, width = x.shape
    images, length = mask.shape
    rows = lambda i: (i, 0)
    return pl.pallas_call(
        partial(backward_kernel, experts),
        grid=(images,),
        in_specs=[
            pl.BlockSpec((length, width), rows),
            pl.BlockSpec((1, 1, length), lambda i: (i, 0, 0)),
            small_spec(width),
            pl.BlockSpec((width, 3 * width), lambda i: (0, 0), pipeline_mode=pl.Buffered(1)),
            pl.BlockSpec((width, width), lambda i: (0, 3), pipeline_mode=pl.Buffered(1)),
            pl.BlockSpec((length, 3 * width), rows),
            pl.BlockSpec((length, width), rows),
            pl.BlockSpec((1, HEADS, length), lambda i: (i, 0, 0)),
            pl.BlockSpec((length, width), rows),
            pl.BlockSpec((length, width), rows),
            pl.BlockSpec((length, 2), rows),
            *returned_specs(ret, 0),
            whole((width, LANES)),
            pl.BlockSpec(memory_space=pltpu.SMEM),
        ],
        out_specs=[
            pl.BlockSpec((length, width), rows),
            whole((width // 2, 4 * width + LANES)),
            whole((width // 4, 4 * width + LANES)),
            whole((width // 4, 4 * width + LANES)),
        ],
        out_shape=[
            jax.ShapeDtypeStruct((total, width), F32),
            jax.ShapeDtypeStruct((width // 2, 4 * width + LANES), BF16),
            jax.ShapeDtypeStruct((width // 4, 4 * width + LANES), BF16),
            jax.ShapeDtypeStruct((width // 4, 4 * width + LANES), BF16),
        ],
        scratch_shapes=[
            pltpu.VMEM((length, 3 * width), BF16),
            pltpu.VMEM((8, width), F32),
            pltpu.VMEM((width, 3 * width), F32),
            pltpu.VMEM((width, width), F32),
            pltpu.VMEM((LANES, width), F32),
            pltpu.VMEM((stack_rows(length, width), LANES), BF16),
            pltpu.VMEM((stack_rows(length, width), LANES), BF16),
            pltpu.VMEM((width, length), F32),
        ],
        compiler_params=params(1),
        name="attention_backward",
        cost_estimate=cost(50),
    )(
        x, mask.reshape(images, 1, length), dense, dense, dense, triple, context, logs, residual,
        up, slot, *ret, drouter, parity,
    )


def combine_kernel(slot, residual, ret_a, ret_b, out):
    out[...] = (residual[...] + gather_slots(slot, (ret_a, ret_b))).astype(BF16)


def combine(slot, residual, ret, block):
    total, width = residual.shape
    rows = lambda i: (i, 0)
    return pl.pallas_call(
        combine_kernel,
        grid=(total // block,),
        in_specs=[
            pl.BlockSpec((block, 2), rows),
            pl.BlockSpec((block, width), rows),
            *returned_specs(ret, 1),
        ],
        out_specs=pl.BlockSpec((block, width), rows),
        out_shape=jax.ShapeDtypeStruct((total, width), BF16),
        compiler_params=params(1),
        name="combine",
        cost_estimate=cost(10),
    )(slot, residual, *ret)


def unpack_kernel(experts, total, wqkv, wout, router, *gains):
    width = wout.shape[1]
    wqkv[...] = total[:, : 3 * width].astype(F32)
    wout[...] = total[:, 3 * width : 4 * width].astype(F32)
    turned = jnp.transpose(total[:, 4 * width :].astype(F32))
    router[...] = turned[0:experts, :]
    for k, gain in enumerate(gains):
        gain[...] = turned[experts + k : experts + k + 1, :]


def unpack(total, experts):
    share = total.shape[0]
    width = (total.shape[1] - LANES) // 4
    shapes = [(share, 3 * width), (share, width), (experts, share)] + [(1, share)] * 4
    return pl.pallas_call(
        partial(unpack_kernel, experts),
        out_shape=[jax.ShapeDtypeStruct(shape, F32) for shape in shapes],
        compiler_params=params(),
        name="unpack",
        cost_estimate=cost(2),
    )(total)


class PlainPlan:
    def __init__(self, seq, wt):
        self.seq, self.wt = seq, wt

    def own_id(self):
        return lax.axis_index("seq")

    def exchange(self, a):
        return lax.all_to_all(a, "seq", split_axis=0, concat_axis=0, tiled=True)

    def begin_dense(self, packed):
        return packed

    def gather_dense(self, packed, begun):
        return lax.all_gather(begun, "wt", axis=0, tiled=True)

    def begin_fetch(self, packed):
        return (packed,)

    def fetch(self, packed, begun):
        return lax.all_gather(begun[0], "wt", axis=0)

    def spread_out_bias(self, quarters):
        return quarters

    def begin_reduce(self, mine, mate):
        return (jnp.concatenate([mine, mate]).reshape(-1, mine.shape[-1]),)

    def reduce_expert(self, parts):
        (parts,) = parts
        return lax.psum_scatter(parts, "wt", scatter_dimension=0, tiled=True)

    def finish_expert(self, parts, received):
        return received.astype(F32)

    def parity(self):
        return jnp.zeros((1, 1), jnp.int32)

    def begin_dense_sum(self, keep, give_a, give_b):
        half = keep.shape[0] // 2
        grads = jnp.concatenate([keep[:half], give_a, keep[half:], give_b])
        return lax.psum_scatter(grads, "wt", scatter_dimension=0, tiled=True)

    def reduce_dense(self, part):
        return lax.psum(part, "seq")


class CubePlan:
    AXES = ("seq", "wt")

    def __init__(self, seq, wt):
        self.seq, self.wt = seq, wt
        self.levels = seq // 2
        places = [
            (z, y, x, c)
            for z in range(self.levels)
            for y in range(2)
            for x in range(2)
            for c in range(2)
        ]
        flat = self.flat
        self.cross = [(flat(*p), flat(p[0], p[1], 1 - p[2], p[3])) for p in places]
        self.core = [(flat(*p), flat(p[0], p[1], p[2], 1 - p[3])) for p in places]
        near = lambda p: p[2] == p[0] % 2
        away = lambda p: (p[0] ^ 2, p[1], 1 - p[0] % 2, p[3])
        home = lambda p: (p[0], p[1], p[0] % 2, p[3])
        self.first = [(flat(*p), flat(*(away(p) if near(p) else home(p)))) for p in places]
        self.second = [(flat(*p), flat(*away(p))) for p in places if not near(p)]
        self.groups = [
            [self.host(half, e, c) for e in range(seq)] for half in range(2) for c in range(2)
        ]

    def flat(self, z, y, x, c):
        return (z * 2 + y) * self.wt + x * 2 + c

    def host(self, half, expert, c):
        z, y = expert // 2, expert % 2
        if z // 2 == half:
            return self.flat(z, y, z % 2, c)
        return self.flat(z ^ 2, y, 1 - z % 2, c)

    def send(self, a, pairs):
        return lax.ppermute(a, self.AXES, pairs)

    def x_zero(self):
        return lax.axis_index("wt") < 2

    def odd_level(self):
        return lax.axis_index("seq") // 2 % 2 == 1

    def near(self):
        return self.x_zero() != self.odd_level()

    def core_zero(self):
        return lax.axis_index("wt") % 2 == 0

    def own_id(self):
        rank = lax.axis_index("seq")
        return jnp.where(self.near(), rank, rank ^ 4)

    def exchange(self, a):
        return lax.all_to_all(
            a, self.AXES, split_axis=0, concat_axis=0, axis_index_groups=self.groups, tiled=True
        )

    def begin_dense(self, packed):
        return self.send(packed, self.cross)

    def gather_dense(self, packed, far):
        mate = self.send(packed, self.core)
        far_mate = self.send(far, self.core)
        flip = self.x_zero()
        low, high = jnp.where(flip, packed, far), jnp.where(flip, far, packed)
        low_mate, high_mate = jnp.where(flip, mate, far_mate), jnp.where(flip, far_mate, mate)
        first = self.core_zero()
        return jnp.concatenate(
            [
                jnp.where(first, low, low_mate),
                jnp.where(first, low_mate, low),
                jnp.where(first, high, high_mate),
                jnp.where(first, high_mate, high),
            ],
            axis=0,
        )

    def begin_fetch(self, packed):
        return self.send(packed, self.first), self.send(packed, self.second)

    def fetch(self, packed, begun):
        got, got_b = begun
        flip = self.near()
        low = jnp.where(flip, packed, got)
        high = jnp.where(flip, got, got_b)
        return jnp.stack([low, high, self.send(low, self.core), self.send(high, self.core)])

    def spread_out_bias(self, quarters):
        mine, odd = self.core_zero(), self.odd_level()
        order = []
        for x in range(2):
            for c in range(2):
                same = mine == (c == 0)
                level = odd == (x == 1)
                order.append(
                    jnp.where(
                        same,
                        jnp.where(level, quarters[0], quarters[1]),
                        jnp.where(level, quarters[2], quarters[3]),
                    )
                )
        return jnp.stack(order)

    def begin_reduce(self, mine, mate):
        got = self.send(mate, self.core)
        low = (mine[0].astype(F32) + got[0].astype(F32)).astype(BF16)
        high = (mine[1].astype(F32) + got[1].astype(F32)).astype(BF16)
        return low, high, jnp.where(self.near(), high, low)

    def reduce_expert(self, parts):
        low, high, give = parts
        return self.send(give, self.first_back()), self.send(high, self.second)

    def finish_expert(self, parts, received):
        far, far_b = received
        return jnp.where(self.near(), parts[0], far_b).astype(F32) + far.astype(F32)

    def first_back(self):
        return [(b, a) for a, b in self.first]

    def parity(self):
        return (lax.axis_index("wt") % 2).reshape(1, 1)

    def begin_dense_sum(self, keep, *give):
        share = keep.shape[0] // 2
        low, high = (
            keep[k * share : (k + 1) * share].astype(F32) + self.send(v, self.core).astype(F32)
            for k, v in enumerate(give)
        )
        flip = self.x_zero()
        out = self.send(jnp.where(flip, high, low).astype(BF16), self.cross)
        mine = jnp.where(flip, low, high) + out.astype(F32)
        return mine.astype(BF16)

    def reduce_dense(self, mine):
        share, width = mine.shape
        pieces = mine.reshape(self.seq, share // self.seq, width)
        swap = lambda v: lax.all_to_all(v, "seq", split_axis=0, concat_axis=0, tiled=True)
        total = jnp.sum(swap(pieces).astype(F32), axis=0, keepdims=True).astype(BF16)
        spread = swap(jnp.broadcast_to(total, pieces.shape))
        return spread.reshape(share, width)


def plan_of(seq, wt):
    return CubePlan(seq, wt) if (seq, wt) == (8, 4) else PlainPlan(seq, wt)


def local(
    inputs,
    key_mask,
    routes,
    priority,
    capacity,
    attention_gain,
    attention_shift,
    query_key_value,
    attention_out,
    mixture_gain,
    mixture_shift,
    router_weight,
    expert_in,
    expert_in_bias,
    expert_out,
    expert_out_bias,
    cotangent,
):
    total, width = inputs.shape
    experts = capacity.shape[0]
    cap = 8 * max(1, total // (4 * experts))
    share = query_key_value.shape[0]
    hidden_share = expert_in.shape[1]
    plan = plan_of(lax.axis_size("seq"), lax.axis_size("wt"))

    tie = lax.optimization_barrier
    front = (cap // 2 + EXTRA - 1) // EXTRA * EXTRA
    parts = (front, cap - front)
    packed, *shards = pack(
        query_key_value, attention_out, router_weight.T,
        (attention_gain, attention_shift, mixture_gain, mixture_shift),
        expert_in[0], expert_out[0], expert_in_bias, expert_out_bias,
    )
    fetched = [plan.begin_fetch(shard) for shard in shards]
    far = plan.begin_dense(packed)
    own = (jnp.arange(LANES) == plan.own_id()).astype(F32)[None, :]
    route_rows = routes.T
    slot, slot_rows = make_slots(route_rows, priority, capacity, parts)
    slot_rows, far, fetched[0] = tie((slot_rows, far, fetched[0]))
    pieces = ((0, front), (experts * front, cap - front))
    send = partial(dispatch, slot_rows, route_rows)
    ups_a = send((cotangent,), experts, pieces[0], True)
    dense = plan.gather_dense(packed, far)
    dense, ups_a = tie((dense, ups_a))
    ups_a = plan.exchange(ups_a)

    triple, context, logs, residual, normed = attention_forward(inputs, key_mask, dense, experts)
    rows_a = send((normed,), experts, pieces[0], False)
    mixed_b = send((normed, cotangent), experts, pieces[1], True)
    rows_a, ups_a, fetched[1] = tie((rows_a, ups_a, fetched[1]))
    rows_a = plan.exchange(rows_a)
    weights = jnp.concatenate(
        [plan.fetch(*pair) for pair in zip(shards, fetched)], axis=1
    )
    b_out = plan.spread_out_bias(
        weights[:, 2 * hidden_share + 1, :share].astype(F32)
    ).reshape(1, width)
    rows_a, mixed_b, weights, b_out = tie((rows_a, mixed_b, weights, b_out))
    mixed_b = plan.exchange(mixed_b)
    ret_a, *sums = run_experts((rows_a, ups_a), parts[0], own, dense, weights, b_out, ())
    ret_a, mixed_b = tie((ret_a, mixed_b))
    ret_a = plan.exchange(ret_a)
    back_b, sent_b, *sums = run_experts(
        (mixed_b,), parts[1], own, dense, weights, b_out, tuple(sums)
    )
    back_b, ret_a = tie((back_b, ret_a))
    back_b = plan.exchange(back_b)
    halves = plan.begin_reduce(*sums[:2])
    back_b, sent_b, halves = tie((back_b, sent_b, halves))
    sent_b = plan.exchange(sent_b)
    received = plan.reduce_expert(halves)
    ret_a = ret_a.reshape(experts, 2, front, width)
    input_grad, *grads = attention_backward(
        inputs, key_mask, dense, triple, context, logs, residual, cotangent, slot,
        (ret_a, back_b), sums[2], plan.parity(), experts,
    )
    grads, received = tie((grads, received))
    mine = plan.begin_dense_sum(*grads)
    mine, sent_b = tie((mine, sent_b))
    shard = plan.finish_expert(halves, received)
    done = plan.reduce_dense(mine)
    block_output = combine(slot, residual, (ret_a, sent_b), 200)
    dqkv, dwout, drouter, *dgains = unpack(done, experts)
    dgains = [g.reshape(share) for g in dgains]
    rank = lax.axis_index("wt")
    return (
        block_output,
        input_grad,
        dgains[0],
        dgains[1],
        dqkv,
        dwout,
        dgains[2],
        dgains[3],
        drouter.T,
        shard[None, :hidden_share],
        shard[2 * hidden_share, :hidden_share][None],
        shard[None, hidden_share : 2 * hidden_share],
        lax.dynamic_slice(shard[2 * hidden_share + 1], (rank * share,), (share,))[None],
    )


def solution(mesh):
    both = P(("seq", "wt"), None)
    placed = (
        both,
        both,
        both,
        both,
        P(),
        P("wt"),
        P("wt"),
        P("wt", None),
        P("wt", None),
        P("wt"),
        P("wt"),
        P("wt", None),
        P("seq", "wt", None),
        P("seq", "wt"),
        P("seq", "wt", None),
        P("seq", "wt"),
        both,
    )
    return jax.shard_map(
        local,
        mesh=mesh,
        in_specs=placed,
        out_specs=(
            both,
            both,
            P("wt"),
            P("wt"),
            P("wt", None),
            P("wt", None),
            P("wt"),
            P("wt"),
            P("wt", None),
            P("seq", "wt", None),
            P("seq", "wt"),
            P("seq", "wt", None),
            P("seq", "wt"),
        ),
        check_vma=False,
    )
```
